256 devices in a mesh: grp: 2 (over z_lo), gx: 64 (over x, z_hi, y), gz: 2 (over core).
Axes of the slice: x: 4, y: 4, z: 8 (z_hi: 4, z_lo: 2; z = z_hi * 2 + z_lo), core: 2. Of those that a mesh axis runs over, the one named last changes fastest.
Arguments:
- fields: float32 [4, 2, 4, 4096, 1024], P(None, 'grp', None, 'gx', 'gz'), may hold values from -4 to 4
- buoyancy: float32 [2, 4, 4096, 1024], P('grp', None, 'gx', 'gz'), may hold values from 0.3 to 0.9
- stiffness: float32 [2, 4, 4096, 1024], P('grp', None, 'gx', 'gz'), may hold values from 0.2 to 0.7
- stress_zero: float32 [4096, 1024], P('gx', 'gz'), may hold values from -5 to 5
- direct_effect: float32 [4096, 1024], P('gx', 'gz'), may hold values from 1 to 8
- log_state: float32 [4096, 1024], P('gx', 'gz'), may hold values from -2 to 2
- kernel: float32 [16, 1024, 4096], P(None, ('grp', 'gx', 'gz')), may hold values from -2 to 2
- history: float32 [16, 1024, 2, 4096], P(None, ('grp', 'gx', 'gz')), may hold values from -5 to 5
- truncation: int32 [1024, 4096], P(('grp', 'gx', 'gz')), may hold values from 1 to 16
Outputs:
- fields_next: float32 [4, 2, 4, 4096, 1024], P(None, 'grp', None, 'gx', 'gz')
- state_next: float32 [4096, 1024], P('gx', 'gz')
- spectra_new: float32 [4, 1024, 2, 4096], P(None, ('grp', 'gx', 'gz'))
The draws below stay inside these ranges and needn't reach their ends.
All inputs are finite; a program needn't handle non-finite values.
Results may differ from the reference program's by a relative error of at most 0.0003.
Values sent between devices are 32-bit elements; how exact they have to be, the bound alone decides.
A program may use at most 128 MiB of HBM per device.

```python
import math
import jax
import jax.numpy as jnp
from jax import lax

PL = 4
HIST = 16
NSTEP = 4
NEWTON = 4
STRIKE = 4096
DEPTH = 1024


def touch_ends(result, rng, smallest, top_value):
    dims = result.shape
    spot = [jax.random.randint(jax.random.fold_in(rng, axis), (), 0, dims[axis]) for axis in range(len(dims))]
    result = result.at[tuple(spot)].set(smallest)
    longest = dims.index(max(dims))
    spot[longest] = (spot[longest] + 1) % dims[longest]
    return result.at[tuple(spot)].set(top_value)


def steps_of(own_key, dims, pieces, low, largest):
    def one(axis_at, parts):
        draws = jax.random.uniform(jax.random.fold_in(jax.random.fold_in(own_key, 6), axis_at), (parts,), jnp.float32, low / len(pieces), largest / len(pieces))
        return jnp.repeat(jnp.exp(draws), dims[axis_at] // parts).reshape((-1,) + (1,) * (len(dims) - axis_at - 1))

    loudness = one(*pieces[0])
    for cut in pieces[1:]:
        loudness = loudness * one(*cut)
    return loudness


def gaussian(key, extent, width, limit, shards=(), held_as=jnp.bfloat16):
    loudness = steps_of(key, extent, shards, -0.22, 0.18) if shards else 1.0
    array = jax.random.normal(key, extent, jnp.float32) * width * loudness
    return jnp.minimum(jnp.maximum(array, -limit), limit).astype(held_as)


def setup_inputs(seed: int = 0) -> dict:
    key_list = jax.random.split(jax.random.key(seed), 10)
    fields = gaussian(key_list[0], (4, 2, PL, STRIKE, DEPTH), 0.5, 4.0, ((1, 2), (3, 64), (4, 2)), jnp.float32)
    buoyancy = jnp.clip(jnp.exp(math.log(0.9) - 1.0986122 * jax.random.uniform(key_list[1], (2, PL, STRIKE, DEPTH), jnp.float32) ** steps_of(key_list[1], (2, PL, STRIKE, DEPTH), ((0, 2), (2, 64), (3, 2)), -0.2, 0.2)), 0.3, 0.9)
    stiffness = jnp.clip(jnp.exp(math.log(0.7) - 1.2527629 * jax.random.uniform(key_list[2], (2, PL, STRIKE, DEPTH), jnp.float32) ** steps_of(key_list[2], (2, PL, STRIKE, DEPTH), ((0, 2), (2, 64), (3, 2)), -0.2, 0.2)), 0.2, 0.7)
    stress_zero = gaussian(key_list[3], (STRIKE, DEPTH), 1.0, 5.0, ((0, 64), (1, 2)), jnp.float32)
    direct_effect = jnp.clip(jnp.exp(math.log(8.0) - 2.0794415 * jax.random.uniform(key_list[4], (STRIKE, DEPTH), jnp.float32) ** steps_of(key_list[4], (STRIKE, DEPTH), ((0, 64), (1, 2)), -0.2, 0.2)), 1.0, 8.0)
    log_state = jnp.clip(jax.random.uniform(key_list[5], (STRIKE, DEPTH), jnp.float32, -2.0, 2.0) * steps_of(key_list[5], (STRIKE, DEPTH), ((0, 64), (1, 2)), -0.4, 0.0), -2.0, 2.0)
    kernel = gaussian(key_list[6], (HIST, DEPTH, STRIKE), 0.3, 2.0, ((1, 256),), jnp.float32)
    history = gaussian(key_list[7], (HIST, DEPTH, 2, STRIKE), 0.7, 5.0, ((1, 256),), jnp.float32)
    truncation = touch_ends(jax.random.randint(key_list[8], (DEPTH, STRIKE), 1, HIST + 1), jax.random.fold_in(key_list[8], 1), 1, HIST).astype(jnp.int32)
    return {"fields": fields, "buoyancy": buoyancy, "stiffness": stiffness, "stress_zero": stress_zero, "direct_effect": direct_effect, "log_state": log_state, "kernel": kernel, "history": history, "truncation": truncation}


FACE_NEAR = 9.0 / 8.0
FACE_FAR = 1.0 / 24.0
DAMPING = 1.0

def stencil(values, axis_index, pad_before, pad_after):
    widths = [(0, 0)] * values.ndim
    widths[axis_index] = (pad_before, pad_after)
    padded = jnp.pad(values, widths)
    length = values.shape[axis_index]

    def window(offset):
        return lax.slice_in_dim(padded, offset, offset + length, axis=axis_index)
    return FACE_NEAR * (window(2) - window(1)) - FACE_FAR * (window(3) - window(0))

def inverse_sinh(scaled):
    magnitude = jnp.abs(scaled)
    positive = jnp.log(magnitude + jnp.sqrt(1.0 + magnitude * magnitude))
    return jnp.where(scaled < 0.0, -positive, positive)

def friction(loading, direct_effect, log_state, initial):
    factor = jnp.exp(log_state)
    slip_rate = initial
    for repeat in range(NEWTON):
        scaled = slip_rate * factor
        misfit = direct_effect * inverse_sinh(scaled) + DAMPING * slip_rate - loading
        slope_total = direct_effect * factor / jnp.sqrt(1.0 + scaled * scaled) + DAMPING
        slip_rate = slip_rate - misfit / slope_total
    return slip_rate

def reference(fields, buoyancy, stiffness, stress_zero, direct_effect, log_state, kernel, history, truncation):
    velocity = fields[0]
    normal_stress = fields[1]
    strike_stress = fields[2]
    depth_stress = fields[3]
    root_total = math.sqrt(STRIKE * DEPTH)
    lag_number = jnp.arange(HIST, dtype=jnp.int32)[:, None, None]
    weights = jnp.where(lag_number < truncation[None], kernel, jnp.zeros_like(kernel))
    lagged = history
    spectra = []
    for step_number in range(NSTEP):
        summed = weights[0][:, None, :] * lagged[0]
        for lag_turn in range(1, HIST):
            summed = summed + weights[lag_turn][:, None, :] * lagged[lag_turn]
        mode_values = lax.complex(summed[:, 0, :], summed[:, 1, :])
        relief = jnp.real(jnp.fft.ifft2(mode_values.T)) * root_total
        velocity_minus = velocity[0, 0]
        velocity_plus = velocity[1, 0]
        normal_stress = normal_stress + stiffness * stencil(velocity, 1, 2, 1)
        strike_stress = strike_stress + stiffness * stencil(velocity, 2, 1, 2)
        depth_stress = depth_stress + stiffness * stencil(velocity, 3, 1, 2)
        slip_guess = velocity_plus - velocity_minus
        loading = stress_zero + relief + DAMPING * slip_guess
        slip_rate = friction(loading, direct_effect, log_state, slip_guess)
        traction = loading - DAMPING * slip_rate
        log_state = 0.75 * log_state - 0.2 * jnp.log(1.0 + slip_rate * slip_rate) + 0.1
        normal_stress = normal_stress.at[:, 0].set(jnp.stack([-traction, traction]))
        velocity = velocity + buoyancy * (stencil(normal_stress, 1, 1, 2) + stencil(strike_stress, 2, 2, 1) + stencil(depth_stress, 3, 2, 1))
        transform = jnp.fft.fft2(slip_rate) / root_total
        fresh_modes = jnp.stack([jnp.real(transform).T, jnp.imag(transform).T], axis=1)
        spectra.append(fresh_modes)
        lagged = jnp.concatenate([fresh_modes[None], lagged[:-1]], axis=0)
    return (jnp.stack([velocity, normal_stress, strike_stress, depth_stress]), log_state, jnp.stack(spectra))
```

```python
import functools
import math

import jax
import jax.numpy as jnp
import numpy as np
from jax import lax
from jax.experimental import pallas as pl
from jax.experimental.pallas import tpu as pltpu
from jax.sharding import PartitionSpec as P

NSTEP = 4
NEWTON = 4
C1 = 9.0 / 8.0
C2 = 1.0 / 24.0
MESH = pl.DeviceIdType.MESH
BF = jnp.bfloat16
F32 = jnp.float32


def split_table(table):
    hi = np.asarray(table, np.float32).astype(jnp.bfloat16)
    lo = (table - hi.astype(np.float64)).astype(jnp.bfloat16)
    return np.stack([hi, lo])


def cis(turns):
    return np.cos(2 * np.pi * turns), np.sin(2 * np.pi * turns)


def make_tables(nx, rows, modes, scale):
    A = 2 * nx
    B = rows // 2
    R = modes
    depth = 4 * nx * R
    strike = nx * rows
    eye_r = np.eye(R)
    eye_p = np.eye(2)
    m, b, k, a = np.arange(B), np.arange(B), np.arange(A), np.arange(A)
    c, s = cis(np.outer(m, b) / B)
    inv = np.array([[c, -s], [s, c]])
    fwd = np.array([[c, s], [-s, c]])
    L1 = np.einsum("xybm,rs->xrbysm", inv, eye_r).reshape(2 * R * B, 2 * R * B)
    L3 = np.einsum("xymb,rs->xrmysb", fwd, eye_r).reshape(2 * R * B, 2 * R * B) * scale
    c, s = cis(np.outer(b, k) / strike)
    twiddle = np.stack([np.tile(c, (R, 1)), np.tile(s, (R, 1))])
    c, s = cis(np.outer(a, k) / A)
    inv = np.array([[c, -s], [s, c]]).reshape(2, 2, nx, 2, A)
    T2 = np.einsum("xyjpk->jxpyk", inv).reshape(4 * nx, 2 * A)
    fwd = np.array([[c, s], [-s, c]]).reshape(2, 2, nx, 2, A)
    TV = np.einsum("xyjpk->jpyxk", fwd).reshape(4 * nx, 2 * A)
    i, z = np.arange(nx), np.arange(A)
    c, s = cis(np.outer(i, z) / A)
    sign = np.where(np.arange(2)[:, None] * z[None, :] % 2 == 1, -1.0, 1.0)
    inv = np.array([[c, -s], [s, c]])
    TI = np.einsum("xyiz,gz,pn->giypnxz", inv, sign, eye_p).reshape(8 * nx, 4 * A)
    fwd = np.array([[c, s], [-s, c]])
    TF = np.einsum("xyiz,pn->ipxnyz", fwd, eye_p).reshape(4 * nx, 4 * A)
    zz = np.arange(depth).reshape(2 * R, 1, A)
    r = np.arange(R)[None, :, None]
    wi, wf = [], []
    for q in range(2):
        c, s = cis((R * q + r) * zz / depth)
        wi.append(np.stack([c, -s], axis=2).reshape(2 * R, 2 * R, A) * scale)
    for g in range(2):
        for q in range(2):
            c, s = cis((R * q + r) * zz / depth)
            wf.append(np.stack([c, -s], axis=2).reshape(2 * R, 2 * R, A) * sign[g])
    mats = [split_table(x) for x in (L1, T2, TI, TF, TV, L3)]
    return mats, [np.asarray(x, np.float32) for x in (twiddle, np.stack(wi), np.stack(wf))]


def split(x):
    hi = x.astype(BF)
    return hi, (x - hi.astype(F32)).astype(BF)


def dot(x, y, dims):
    return lax.dot_general(x, y, (dims, ((), ())), preferred_element_type=F32)


def table_left(tab, x, dims):
    hi, lo = split(x)
    return dot(tab[0], hi, dims) + (dot(tab[0], lo, dims) + dot(tab[1], hi, dims))


def table_right(x, tab, dims):
    hi, lo = split(x)
    return dot(hi, tab[0], dims) + (dot(lo, tab[0], dims) + dot(hi, tab[1], dims))


def roll(x, shift, axis):
    return pltpu.roll(x, shift % x.shape[axis], axis)


def kernel_body(
    nx, both, fields, buoy, stiff, szero, direct, logs, start, wts, L1, T2, TI, TF, TV, L3, TW, WI, WF,
    out_f, out_l, out_s,
    VP, SP, DP, ACC, GS, RI, OS, PS, RL, PR, SL, US, SF, RF, TR, SG, HV, DV, NP, HS, DS,
    isend, irecv, fsend, frecv, psend, precv, lsend, lrecv, vsend, vrecv, ssend, srecv, gsend, grecv,
):
    g, j, q = lax.axis_index("grp"), lax.axis_index("gx"), lax.axis_index("gz")
    A = 2 * nx
    RB = TW.shape[1]
    RW, CW = szero.shape
    B = RW // 2
    R = RB // B
    LW = DV.shape[3]
    HC = CW // A
    side = (2 * g - 1).astype(F32)
    rows_in = pl.ds(8, RW)
    cols_in = pl.ds(LW, CW)

    def target(step):
        if nx == 64:
            dx, dz, dy = step // 4 % 4, step // 16, step % 4
            x = lax.rem(j // 16 + (6 - dx), 4)
            z = lax.rem(j // 4 % 4 + (6 - dz), 4)
            y = lax.rem(j % 4 + (6 - dy), 4)
            return x * 16 + z * 4 + y
        return lax.rem(j + step, nx)

    own_step = 2 * 16 + 2 * 4 + 2 if nx == 64 else 0

    barrier = pltpu.get_barrier_semaphore()

    def greet(step, carry):
        peer = target(step)

        @pl.when(step != own_step)
        def _():
            pl.semaphore_signal(barrier, inc=1, device_id=(g, peer, q), device_id_type=MESH)
            if both:
                pl.semaphore_signal(barrier, inc=1, device_id=(1 - g, peer, q), device_id_type=MESH)

        return carry

    lax.fori_loop(0, nx, greet, 0)
    pl.semaphore_signal(barrier, inc=1, device_id=(1 - g, j, q), device_id_type=MESH)
    pl.semaphore_signal(barrier, inc=1, device_id=(g, j, 1 - q), device_id_type=MESH)

    VP[...] = jnp.zeros_like(VP)
    SP[...] = jnp.zeros_like(SP)
    DP[...] = jnp.zeros_like(DP)
    VP[:, rows_in, cols_in] = fields[0]
    out_f[1] = fields[1]
    SP[:, rows_in, :] = fields[2]
    DP[:, :, cols_in] = fields[3]
    out_l[...] = logs[...]
    ACC[pl.ds(0, NSTEP)] = start[...]
    for t in range(NSTEP, ACC.shape[0]):
        ACC[t] = jnp.zeros_like(ACC[t])
    pl.semaphore_wait(barrier, (2 * (nx - 1) if both else nx - 1) + 2)

    def remote(src, dst, send, recv, device):
        return pltpu.make_async_remote_copy(
            src_ref=src, dst_ref=dst, send_sem=send, recv_sem=recv, device_id=device, device_id_type=MESH
        )

    def row_copies(src_of, land, t, send, recv):
        up = remote(src_of(pl.ds(RW, 8)), land.at[t, 0], send.at[0], recv.at[0, t], (g, lax.rem(j + 1, nx), q))
        down = remote(src_of(pl.ds(8, 8)), land.at[t, 1], send.at[1], recv.at[1, t], (g, lax.rem(j + nx - 1, nx), q))
        return up, down

    def v_copies(t):
        up, down = row_copies(lambda d: VP.at[:, d, cols_in], HV, t, vsend, vrecv)
        right = remote(VP.at[:, rows_in, pl.ds(CW, LW)], DV.at[t], vsend.at[2], vrecv.at[2, t], (g, j, 1 - q))
        left = remote(VP.at[:, rows_in, pl.ds(LW, LW)], DV.at[t], vsend.at[2], vrecv.at[2, t], (g, j, 1 - q))
        across = remote(VP.at[0, rows_in, cols_in], NP.at[t], gsend, grecv.at[t], (1 - g, j, q))
        return up, down, right, left, across

    def s_copies(t):
        up, down = row_copies(lambda d: SP.at[:, d, :], HS, t, ssend, srecv)
        right = remote(DP.at[:, :, pl.ds(CW, LW)], DS.at[t], ssend.at[2], srecv.at[2, t], (g, j, 1 - q))
        left = remote(DP.at[:, :, pl.ds(LW, LW)], DS.at[t], ssend.at[2], srecv.at[2, t], (g, j, 1 - q))
        return up, down, right, left

    def start_halo(up, down, right, left):
        @pl.when(j < nx - 1)
        def _():
            up.start()

        @pl.when(j > 0)
        def _():
            down.start()

        @pl.when(q == 0)
        def _():
            right.start()

        @pl.when(q == 1)
        def _():
            left.start()

    def sent_halo(up, down, right, left):
        @pl.when(j < nx - 1)
        def _():
            up.wait_send()

        @pl.when(j > 0)
        def _():
            down.wait_send()

        right.wait_send()

    def recv_halo(up, down, right, t, land, depth_land, put_rows, put_cols):
        @pl.when(j > 0)
        def _():
            up.wait_recv()
            put_rows(0, land[t, 0])

        @pl.when(j < nx - 1)
        def _():
            down.wait_recv()
            put_rows(8 + RW, land[t, 1])

        right.wait_recv()

        @pl.when(q == 0)
        def _():
            put_cols(LW + CW, depth_land[t])

        @pl.when(q == 1)
        def _():
            put_cols(0, depth_land[t])

    def v_rows(at, x):
        VP[:, pl.ds(at, 8), cols_in] = x

    def v_cols(at, x):
        VP[:, rows_in, pl.ds(at, LW)] = x

    def s_rows(at, x):
        SP[:, pl.ds(at, 8), :] = x

    def d_cols(at, x):
        DP[:, :, pl.ds(at, LW)] = x

    first = v_copies(0)
    start_halo(*first[:4])
    first[4].start()

    def step_body(t, carry):
        x = table_left(L1, ACC[t], ((1,), (0,)))
        xr, xi = x[:RB], x[RB:]
        wide = jnp.concatenate([xr * TW[0] - xi * TW[1], xr * TW[1] + xi * TW[0]], axis=1)
        GS[t] = table_left(T2, wide, ((1,), (1,)))
        mine = pl.ds((g * nx + j) * 4, 4)

        def send_modes(step, c):
            peer = target(step)
            block = GS.at[t, pl.ds(peer * 4, 4)]

            @pl.when(step != own_step)
            def _():
                remote(block, RI.at[t, mine], isend.at[t], irecv.at[t], (g, peer, q)).start()
                if both:
                    remote(block, RI.at[t, mine], isend.at[t], irecv.at[t], (1 - g, peer, q)).start()

            return c

        lax.fori_loop(0, nx, send_modes, 0)
        own = GS.at[t, pl.ds(j * 4, 4)]
        pltpu.make_async_copy(own, RI.at[t, mine], irecv.at[t]).start()
        if both:
            remote(own, RI.at[t, mine], isend.at[t], irecv.at[t], (1 - g, j, q)).start()

        up, down, right, left, across = v_copies(t)
        recv_halo(up, down, right, t, HV, DV, v_rows, v_cols)
        sent_halo(up, down, right, left)
        across.wait()
        near = VP[0, rows_in, cols_in]
        SG[...] = side * (near - NP[t])

        def stress_chunk(i, c):
            r0 = pl.multiple_of(i * 8, 8)
            chunk = pl.ds(r0, 8)
            inner = pl.ds(r0 + 8, 8)
            vs = []
            for p in range(4):
                tall = VP[p, pl.ds(r0, 24), cols_in]
                wide = VP[p, inner, :]
                v = tall[8:16]
                vs.append(v)
                st = stiff[p, chunk, :]
                up1, up2, dn1 = (roll(tall, s, 0)[8:16] for s in (-1, -2, 1))
                SP[p, inner, :] = SP[p, inner, :] + st * (C1 * (up1 - v) - C2 * (up2 - dn1))
                up1, up2, dn1 = (roll(wide, s, 1)[:, LW : LW + CW] for s in (-1, -2, 1))
                DP[p, chunk, cols_in] = DP[p, chunk, cols_in] + st * (C1 * (up1 - v) - C2 * (up2 - dn1))
            for p in range(1, 4):
                far = 0.0 - (vs[p - 2] if p >= 2 else 0.0)
                if p < 3:
                    far = vs[p + 1] + far
                out_f[1, p, chunk, :] = out_f[1, p, chunk, :] + stiff[p, chunk, :] * (
                    C1 * (vs[p] - vs[p - 1]) - C2 * far
                )
            return c

        lax.fori_loop(0, RW // 8, stress_chunk, 0)
        up, down, right, left = s_copies(t)
        start_halo(up, down, right, left)
        recv_halo(up, down, right, t, HS, DS, s_rows, d_cols)
        sent_halo(up, down, right, left)

        def velocity_chunk(i, c):
            r0 = pl.multiple_of(i * 8, 8)
            chunk = pl.ds(r0, 8)
            inner = pl.ds(r0 + 8, 8)
            n1, n2, n3 = (out_f[1, p, chunk, :] for p in (1, 2, 3))
            plane_terms = [C1 * n1 - C2 * n2, C1 * (n2 - n1) - C2 * n3, C1 * (n3 - n2) + C2 * n1, C2 * n2 - C1 * n3]
            for p in range(4):
                tall = SP[p, pl.ds(r0, 24), :]
                wide = DP[p, chunk, :]
                dn1, dn2, up1 = (roll(tall, s, 0)[8:16] for s in (1, 2, -1))
                total = plane_terms[p] + (C1 * (tall[8:16] - dn1) - C2 * (up1 - dn2))
                dn1, dn2, up1 = (roll(wide, s, 1)[:, LW : LW + CW] for s in (1, 2, -1))
                total = total + (C1 * (wide[:, LW : LW + CW] - dn1) - C2 * (up1 - dn2))
                VP[p, inner, cols_in] = VP[p, inner, cols_in] + buoy[p, chunk, :] * total
            return c

        lax.fori_loop(0, RW // 8, velocity_chunk, 0)

        if not both:
            pltpu.make_async_copy(
                RI.at[t, pl.ds(g * nx * 4, nx * 4)], RI.at[t, pl.ds(g * nx * 4, nx * 4)], irecv.at[t]
            ).wait()
            relay = remote(
                RI.at[t, pl.ds(g * nx * 4, nx * 4)], RI.at[t, pl.ds(g * nx * 4, nx * 4)], psend.at[1, t],
                precv.at[1, t], (1 - g, j, q),
            )
            relay.start()
            relay.wait()
        else:
            pltpu.make_async_copy(RI.at[t], RI.at[t], irecv.at[t]).wait()
        OS[...] = table_right(RI[t].T, TI, ((1,), (0,)))

        def depth_half(half, put):
            for hl in range(HC):
                tw = WI[q, half * HC + hl]
                for p in range(2):
                    total = None
                    for r in range(R):
                        for c in range(2):
                            k = 2 * r + c
                            term = tw[k : k + 1] * OS[r * B : (r + 1) * B, (2 * p + c) * A : (2 * p + c + 1) * A]
                            total = term if total is None else total + term
                    put[p * B : (p + 1) * B, hl * A : (hl + 1) * A] = total

        depth_half(1 - q, PS.at[t])
        part = remote(PS.at[t], PR.at[t], psend.at[0, t], precv.at[0, t], (g, j, 1 - q))
        part.start()
        depth_half(q, RL)
        part.wait()

        CH = 16 if RW % 16 == 0 else 8

        def friction_chunk(i, c):
            chunk = pl.ds(pl.multiple_of(i * CH, CH), CH)
            guess = SG[chunk, :]
            loading = szero[chunk, :] + (RL[chunk, :] + PR[t, chunk, :]) + guess
            a = direct[chunk, :]
            ls = out_l[chunk, :]
            factor = jnp.exp(ls)
            af = a * factor
            v = guess
            for _ in range(NEWTON):
                s = v * factor
                root = jnp.sqrt(1.0 + s * s)
                size = jnp.log(jnp.abs(s) + root)
                misfit = a * jnp.where(s < 0.0, -size, size) + v - loading
                v = v - misfit / (af / root + 1.0)
            SL[t, q, chunk, :] = v
            TR[chunk, :] = side * (loading - v)
            out_l[chunk, :] = 0.75 * ls - 0.2 * jnp.log(1.0 + v * v) + 0.1
            return c

        lax.fori_loop(0, RW // CH, friction_chunk, 0)
        slip = remote(SL.at[t, q], SL.at[t, q], lsend.at[t], lrecv.at[t], (g, j, 1 - q))
        slip.start()

        def depth_terms(half, p, acc):
            for hl in range(HC):
                tw = WF[2 * g + q, half * HC + hl]
                cells = SL[t, half, p * B : (p + 1) * B, hl * A : (hl + 1) * A]
                terms = [tw[k : k + 1] * cells for k in range(2 * R)]
                acc = terms if acc is None else [x + y for x, y in zip(acc, terms)]
            return acc

        def put_terms(p, acc, add):
            for r in range(R):
                for c in range(2):
                    at = (slice(r * B, (r + 1) * B), slice((2 * p + c) * A, (2 * p + c + 1) * A))
                    US[at] = US[at] + acc[2 * r + c] if add else acc[2 * r + c]

        for p in range(2):
            put_terms(p, depth_terms(q, p, None), False)
        pltpu.make_async_copy(SL.at[t, 1 - q], SL.at[t, 1 - q], lrecv.at[t]).wait()
        for p in range(2):
            put_terms(p, depth_terms(1 - q, p, None), True)
        SF[t] = table_left(TF, US[...], ((1,), (1,)))
        here = pl.ds(j * 4, 4)

        def send_slip(step, c):
            peer = target(step)

            @pl.when(step != own_step)
            def _():
                remote(SF.at[t, pl.ds(peer * 4, 4)], RF.at[t, here], fsend.at[t], frecv.at[t], (g, peer, q)).start()

            return c

        lax.fori_loop(0, nx, send_slip, 0)
        pltpu.make_async_copy(SF.at[t, here], RF.at[t, here], frecv.at[t]).start()

        pull = TR[...]
        out_f[1, 0] = pull
        VP[0, rows_in, cols_in] = VP[0, rows_in, cols_in] - buoy[0] * (C1 * pull)
        VP[1, rows_in, cols_in] = VP[1, rows_in, cols_in] + buoy[1] * (C2 * pull)

        @pl.when(t < NSTEP - 1)
        def _():
            later = v_copies(t + 1)
            start_halo(*later[:4])
            later[4].start()

        slip.wait_send()
        pltpu.make_async_copy(RF.at[t], RF.at[t], frecv.at[t]).wait()
        x = table_right(RF[t].T, TV, ((1,), (0,)))
        xr, xi = x[:, :A], x[:, A:]
        tall = jnp.concatenate([xr * TW[0] + xi * TW[1], xi * TW[0] - xr * TW[1]], axis=0)
        fresh = table_left(L3, tall, ((1,), (0,)))
        out_s[t] = fresh
        for d in range(NSTEP - 1):
            for c in range(2):
                at = pl.ds(c * RB, RB)
                ACC[t + 1 + d, at] = ACC[t + 1 + d, at] + wts[d] * fresh[c * RB : (c + 1) * RB]
        return carry

    lax.fori_loop(0, NSTEP, step_body, 0)

    out_f[0] = VP[:, rows_in, cols_in]
    out_f[2] = SP[:, rows_in, :]
    out_f[3] = DP[:, :, cols_in]
    for t in range(NSTEP):
        count = (2 * nx - 1 if both else nx - 1) * 4
        left = RI.at[t, pl.ds(0, count)]
        pltpu.make_async_copy(left, left, isend.at[t]).wait()
        left = RF.at[t, pl.ds(0, (nx - 1) * 4)]
        pltpu.make_async_copy(left, left, fsend.at[t]).wait()


def per_device(nx, both, fields, buoyancy, stiffness, stress_zero, direct_effect, log_state, kernel, history, truncation):
    planes, rows, cols = fields.shape[2:]
    hist, modes, _, strike = history.shape
    A = 2 * nx
    B = rows // 2
    RB = modes * B
    depth = 2 * cols
    scale = 1.0 / math.sqrt(strike * depth)
    mats, vecs = make_tables(nx, rows, modes, scale)
    lag_number = lax.broadcasted_iota(jnp.int32, kernel.shape, 0)
    weights = jnp.where(lag_number < truncation[None], kernel, jnp.zeros_like(kernel))
    start = jnp.stack([
        jnp.sum(weights[t:, :, None, :] * history[: hist - t], axis=0) for t in range(NSTEP)
    ])
    start = jnp.transpose(start, (0, 2, 1, 3)).reshape(NSTEP, 2 * RB, A)
    wts = weights[: NSTEP - 1].reshape(NSTEP - 1, RB, A)
    LW = min(128, cols)
    vm = pltpu.VMEM
    dma = pltpu.SemaphoreType.DMA
    scratch = [
        vm((planes, rows + 16, cols + 2 * LW), F32),
        vm((planes, rows + 16, cols), F32),
        vm((planes, rows, cols + 2 * LW), F32),
        vm((2 * NSTEP - 1, 2 * RB, A), F32),
        vm((NSTEP, 4 * nx, RB), F32),
        vm((NSTEP, 8 * nx, RB), F32),
        vm((RB, 4 * A), F32),
        vm((NSTEP, rows, cols), F32),
        vm((rows, cols), F32),
        vm((NSTEP, rows, cols), F32),
        vm((NSTEP, 2, rows, cols), F32),
        vm((RB, 4 * A), F32),
        vm((NSTEP, 4 * nx, RB), F32),
        vm((NSTEP, 4 * nx, RB), F32),
        vm((rows, cols), F32),
        vm((rows, cols), F32),
        vm((NSTEP, 2, planes, 8, cols), F32),
        vm((NSTEP, planes, rows, LW), F32),
        vm((NSTEP, rows, cols), F32),
        vm((NSTEP, 2, planes, 8, cols), F32),
        vm((NSTEP, planes, rows, LW), F32),
        dma((NSTEP,)), dma((NSTEP,)), dma((NSTEP,)), dma((NSTEP,)),
        dma((2, NSTEP)), dma((2, NSTEP)), dma((NSTEP,)), dma((NSTEP,)),
        dma((3,)), dma((3, NSTEP)), dma((3,)), dma((3, NSTEP)), dma, dma((NSTEP,)),
    ]
    whole = pl.BlockSpec(memory_space=pltpu.VMEM)
    args = [
        fields.reshape(4, planes, rows, cols), buoyancy[0], stiffness[0], stress_zero, direct_effect, log_state,
        start, wts, *[jnp.asarray(x) for x in mats], *[jnp.asarray(x) for x in vecs],
    ]
    out_f, out_l, out_s = pl.pallas_call(
        functools.partial(kernel_body, nx, both),
        out_shape=(
            jax.ShapeDtypeStruct((4, planes, rows, cols), F32),
            jax.ShapeDtypeStruct((rows, cols), F32),
            jax.ShapeDtypeStruct((NSTEP, 2 * RB, A), F32),
        ),
        in_specs=[whole] * len(args),
        out_specs=(whole, whole, whole),
        scratch_shapes=scratch,
        compiler_params=pltpu.CompilerParams(
            collective_id=0, has_side_effects=True, vmem_limit_bytes=60 * 1024 * 1024
        ),
    )(*args)
    spectra = out_s.reshape(NSTEP, 2, modes, strike).transpose(0, 2, 1, 3)
    return out_f.reshape(4, 1, planes, rows, cols), out_l, spectra


def solution(mesh, both=True):
    return jax.shard_map(
        functools.partial(per_device, mesh.shape["gx"], both),
        mesh=mesh,
        in_specs=(
            P(None, "grp", None, "gx", "gz"),
            P("grp", None, "gx", "gz"),
            P("grp", None, "gx", "gz"),
            P("gx", "gz"),
            P("gx", "gz"),
            P("gx", "gz"),
            P(None, ("grp", "gx", "gz"), None),
            P(None, ("grp", "gx", "gz"), None, None),
            P(("grp", "gx", "gz"), None),
        ),
        out_specs=(
            P(None, "grp", None, "gx", "gz"),
            P("gx", "gz"),
            P(None, ("grp", "gx", "gz"), None, None),
        ),
        check_vma=False,
    )
```

```python
import functools
import math

import jax
import jax.numpy as jnp
import numpy as np
from jax import lax
from jax.experimental import pallas as pl
from jax.experimental.pallas import tpu as pltpu
from jax.sharding import PartitionSpec as P

NSTEP = 4
NEWTON = 4
C1 = 9.0 / 8.0
C2 = 1.0 / 24.0
MESH = pl.DeviceIdType.MESH
BF = jnp.bfloat16
F32 = jnp.float32


def split_table(table):
    hi = np.asarray(table, np.float32).astype(jnp.bfloat16)
    lo = (table - hi.astype(np.float64)).astype(jnp.bfloat16)
    return np.stack([hi, lo])


def cis(turns):
    return np.cos(2 * np.pi * turns), np.sin(2 * np.pi * turns)


def make_tables(nx, rows, modes, scale):
    A = 2 * nx
    B = rows // 2
    R = modes
    depth = 4 * nx * R
    strike = nx * rows
    eye_r = np.eye(R)
    eye_p = np.eye(2)
    m, b, k, a = np.arange(B), np.arange(B), np.arange(A), np.arange(A)
    c, s = cis(np.outer(m, b) / B)
    inv = np.array([[c, -s], [s, c]])
    fwd = np.array([[c, s], [-s, c]])
    L1 = np.einsum("xybm,rs->xrbsmy", inv, eye_r).reshape(2 * R * B, 2 * R * B)
    L3 = np.einsum("xymb,rs->rmxysb", fwd, eye_r).reshape(2 * R * B, 2 * R * B) * scale
    c, s = cis(np.outer(b, k) / strike)
    twiddle = np.stack([np.tile(c, (R, 1)), np.tile(s, (R, 1))])
    c, s = cis(np.outer(a, k) / A)
    inv = np.array([[c, -s], [s, c]]).reshape(2, 2, nx, 2, A)
    T2 = np.einsum("xyjpk->jxpyk", inv).reshape(4 * nx, 2 * A)
    fwd = np.array([[c, s], [-s, c]]).reshape(2, 2, nx, 2, A)
    TV = np.einsum("xyjpk->jpyxk", fwd).reshape(4 * nx, 2 * A)
    i, z = np.arange(nx), np.arange(A)
    c, s = cis(np.outer(i, z) / A)
    sign = np.where(np.arange(2)[:, None] * z[None, :] % 2 == 1, -1.0, 1.0)
    inv = np.array([[c, -s], [s, c]])
    TI = np.einsum("xyiz,gz,pn->giypnxz", inv, sign, eye_p).reshape(8 * nx, 4 * A)
    fwd = np.array([[c, s], [-s, c]])
    TF = np.einsum("xyiz,pn->ipxnyz", fwd, eye_p).reshape(4 * nx, 4 * A)
    zz = np.arange(depth).reshape(2 * R, 1, A)
    r = np.arange(R)[None, :, None]
    wi, wf = [], []
    for q in range(2):
        c, s = cis((R * q + r) * zz / depth)
        wi.append(np.stack([c, -s], axis=2).reshape(2 * R, 2 * R, A) * scale)
    for g in range(2):
        for q in range(2):
            c, s = cis((R * q + r) * zz / depth)
            wf.append(np.stack([c, -s], axis=2).reshape(2 * R, 2 * R, A) * sign[g])
    mats = [split_table(x) for x in (L1, T2, TI, TF, TV, L3)]
    return mats, [np.asarray(x, np.float32) for x in (twiddle, np.stack(wi), np.stack(wf))]


def split(x):
    hi = x.astype(BF)
    return hi, (x - hi.astype(F32)).astype(BF)


def dot(x, y, dims):
    return lax.dot_general(x, y, (dims, ((), ())), preferred_element_type=F32)


def table_left(tab, x, dims):
    hi, lo = split(x)
    return dot(tab[0], hi, dims) + (dot(tab[0], lo, dims) + dot(tab[1], hi, dims))


def table_right(x, tab, dims):
    hi, lo = split(x)
    return dot(hi, tab[0], dims) + (dot(lo, tab[0], dims) + dot(hi, tab[1], dims))


def roll(x, shift, axis):
    return pltpu.roll(x, shift % x.shape[axis], axis)


def kernel_body(
    nx, fields_h, buoy_h, stiff_h, szero_h, direct_h, logs_h, kern_h, hist_h, trunc_h,
    L1_h, T2_h, TI_h, TF_h, TV_h, L3_h, TW_h, WI_h, WF_h,
    out_f, out_l, out_s,
    buoy, stiff, szero, direct, LS, KW, H, TRN, L1, T2, TI, TF, TV, L3, TW, WI, WF, WD, NS, FR,
    VP, SP, DP, ACC, GS, RI, OS, PS, RL, PR, SL, US, SF, RF, TR, SG, HV, DV, NP, HS, DS,
    insem, outsem, isend, irecv, fsend, frecv, psend, precv, lsend, lrecv, vsend, vrecv, ssend, srecv, gsend, grecv,
):
    g, j, q = lax.axis_index("grp"), lax.axis_index("gx"), lax.axis_index("gz")
    A = 2 * nx
    RB = TW.shape[1]
    RW, CW = szero.shape
    B = RW // 2
    R = RB // B
    LW = DV.shape[3]
    HC = CW // A
    HIST = H.shape[0]
    side = (2 * g - 1).astype(F32)
    rows_in = pl.ds(8, RW)
    cols_in = pl.ds(LW, CW)

    if nx == 64:
        turn = (2, 3, 1, 0)
        xs = [lax.rem(lax.div(j, 16) + k, 4) * 16 for k in turn]
        ys = [lax.rem(j, 4) + k for k in turn]
        peers_xy = [x + lax.rem(y, 4) for x in xs for y in ys]
        zs = lax.rem(lax.div(j, 4), 4)
        outer = 4

        def layer(i):
            return lax.rem(zs + i + 2, 4) * 4

        own_layer, own_xy = 2, 15
    else:
        peers_xy = [j * 0]
        outer = nx

        def layer(i):
            return lax.rem(j + i + 1, nx)

        own_layer, own_xy = nx - 1, 0

    def each_peer(act):
        def one_layer(i, carry):
            z = layer(i)
            for n, xy in enumerate(peers_xy):
                if n == own_xy:

                    @pl.when(i != own_layer)
                    def _():
                        act(z + xy)
                else:
                    act(z + xy)
            return carry

        lax.fori_loop(0, outer, one_layer, 0)

    barrier = pltpu.get_barrier_semaphore()

    def greet(peer):
        pl.semaphore_signal(barrier, inc=1, device_id=(g, peer, q), device_id_type=MESH)
        pl.semaphore_signal(barrier, inc=1, device_id=(1 - g, peer, q), device_id_type=MESH)

    each_peer(greet)
    pl.semaphore_signal(barrier, inc=1, device_id=(1 - g, j, q), device_id_type=MESH)
    pl.semaphore_signal(barrier, inc=1, device_id=(g, j, 1 - q), device_id_type=MESH)

    pairs = [
        (kern_h, KW), (trunc_h, TRN), (hist_h, H), (L1_h, L1), (TW_h, TW), (T2_h, T2),
        (fields_h.at[0], VP.at[:, rows_in, cols_in]), (stiff_h, stiff), (fields_h.at[2], SP.at[:, rows_in, :]),
        (fields_h.at[3], DP.at[:, :, cols_in]), (fields_h.at[1], NS), (TI_h, TI), (WI_h, WI), (szero_h, szero),
        (direct_h, direct), (logs_h, LS), (WF_h, WF), (TF_h, TF), (buoy_h, buoy), (TV_h, TV), (L3_h, L3),
    ]
    loads = [pltpu.make_async_copy(src, dst, insem.at[n]) for n, (src, dst) in enumerate(pairs)]
    for copy in loads:
        copy.start()
    for t in range(ACC.shape[0]):
        ACC[t] = jnp.zeros((2 * RB, A), F32)
    VP[:, pl.ds(0, 8), :] = jnp.zeros((4, 8, CW + 2 * LW), F32)
    VP[:, pl.ds(8 + RW, 8), :] = jnp.zeros((4, 8, CW + 2 * LW), F32)
    VP[:, rows_in, pl.ds(0, LW)] = jnp.zeros((4, RW, LW), F32)
    VP[:, rows_in, pl.ds(LW + CW, LW)] = jnp.zeros((4, RW, LW), F32)
    SP[:, pl.ds(0, 8), :] = jnp.zeros((4, 8, CW), F32)
    SP[:, pl.ds(8 + RW, 8), :] = jnp.zeros((4, 8, CW), F32)
    DP[:, :, pl.ds(0, LW)] = jnp.zeros((4, RW, LW), F32)
    DP[:, :, pl.ds(LW + CW, LW)] = jnp.zeros((4, RW, LW), F32)

    loads[0].wait()
    loads[1].wait()

    def mask_lag(lag, carry):
        for r in range(R):
            pick = pl.ds(r, B, stride=R)
            kept = jnp.where(lag < TRN[pick, :], KW[lag, pick, :], 0.0)
            for c in range(2):
                WD[lag, pl.ds(r * 2 * B + c, B, stride=2), :] = kept
        return carry

    lax.fori_loop(0, HIST, mask_lag, 0)

    def lag_sums(ahead):
        for r in range(R):
            part = pl.ds(r * 2 * B, 2 * B)

            def one_lag(lag, total):
                return total + WD[lag + ahead, part, :] * H[lag, part, :]

            ACC[ahead, part, :] = lax.fori_loop(0, HIST - ahead, one_lag, ACC[ahead, part, :])

    for copy in loads[2:6]:
        copy.wait()
    lag_sums(0)
    loads[6].wait()
    pl.semaphore_wait(barrier, 2 * (nx - 1) + 2)

    def remote(src, dst, send, recv, device):
        return pltpu.make_async_remote_copy(
            src_ref=src, dst_ref=dst, send_sem=send, recv_sem=recv, device_id=device, device_id_type=MESH
        )

    def row_copies(src_of, land, t, send, recv):
        up = remote(src_of(pl.ds(RW, 8)), land.at[t, 0], send.at[0], recv.at[0, t], (g, lax.rem(j + 1, nx), q))
        down = remote(src_of(pl.ds(8, 8)), land.at[t, 1], send.at[1], recv.at[1, t], (g, lax.rem(j + nx - 1, nx), q))
        return up, down

    def v_copies(t):
        up, down = row_copies(lambda d: VP.at[:, d, cols_in], HV, t, vsend, vrecv)
        right = remote(VP.at[:, rows_in, pl.ds(CW, LW)], DV.at[t], vsend.at[2], vrecv.at[2, t], (g, j, 1 - q))
        left = remote(VP.at[:, rows_in, pl.ds(LW, LW)], DV.at[t], vsend.at[2], vrecv.at[2, t], (g, j, 1 - q))
        across = remote(VP.at[0, rows_in, cols_in], NP.at[t], gsend, grecv.at[t], (1 - g, j, q))
        return up, down, right, left, across

    def s_copies(t):
        up, down = row_copies(lambda d: SP.at[:, d, :], HS, t, ssend, srecv)
        right = remote(DP.at[:, :, pl.ds(CW, LW)], DS.at[t], ssend.at[2], srecv.at[2, t], (g, j, 1 - q))
        left = remote(DP.at[:, :, pl.ds(LW, LW)], DS.at[t], ssend.at[2], srecv.at[2, t], (g, j, 1 - q))
        return up, down, right, left

    def start_halo(up, down, right, left):
        @pl.when(j < nx - 1)
        def _():
            up.start()

        @pl.when(j > 0)
        def _():
            down.start()

        @pl.when(q == 0)
        def _():
            right.start()

        @pl.when(q == 1)
        def _():
            left.start()

    def sent_halo(up, down, right, left):
        @pl.when(j < nx - 1)
        def _():
            up.wait_send()

        @pl.when(j > 0)
        def _():
            down.wait_send()

        right.wait_send()

    def recv_halo(up, down, right, t, land, depth_land, put_rows, put_cols):
        @pl.when(j > 0)
        def _():
            up.wait_recv()
            put_rows(0, land[t, 0])

        @pl.when(j < nx - 1)
        def _():
            down.wait_recv()
            put_rows(8 + RW, land[t, 1])

        right.wait_recv()

        @pl.when(q == 0)
        def _():
            put_cols(LW + CW, depth_land[t])

        @pl.when(q == 1)
        def _():
            put_cols(0, depth_land[t])

    def v_rows(at, x):
        VP[:, pl.ds(at, 8), cols_in] = x

    def v_cols(at, x):
        VP[:, rows_in, pl.ds(at, LW)] = x

    def s_rows(at, x):
        SP[:, pl.ds(at, 8), :] = x

    def d_cols(at, x):
        DP[:, :, pl.ds(at, LW)] = x

    first = v_copies(0)
    start_halo(*first[:4])
    first[4].start()

    def out_copies():
        return [
            pltpu.make_async_copy(SP.at[:, rows_in, :], out_f.at[2], outsem.at[0]),
            pltpu.make_async_copy(DP.at[:, :, cols_in], out_f.at[3], outsem.at[1]),
            pltpu.make_async_copy(VP.at[:, rows_in, cols_in], out_f.at[0], outsem.at[2]),
            pltpu.make_async_copy(NS, out_f.at[1], outsem.at[3]),
            pltpu.make_async_copy(LS, out_l, outsem.at[4]),
        ]

    def step_body(t, carry):
        x = table_left(L1, ACC[t], ((1,), (0,)))
        xr, xi = x[:RB], x[RB:]
        wide = jnp.concatenate([xr * TW[0] - xi * TW[1], xr * TW[1] + xi * TW[0]], axis=1)
        GS[t] = table_left(T2, wide, ((1,), (1,)))
        mine = pl.ds((g * nx + j) * 4, 4)

        def send_modes(peer):
            block = GS.at[t, pl.ds(peer * 4, 4)]
            remote(block, RI.at[t, mine], isend.at[t], irecv.at[t], (1 - g, peer, q)).start()
            remote(block, RI.at[t, mine], isend.at[t], irecv.at[t], (g, peer, q)).start()

        each_peer(send_modes)
        own = GS.at[t, pl.ds(j * 4, 4)]
        remote(own, RI.at[t, mine], isend.at[t], irecv.at[t], (1 - g, j, q)).start()
        pltpu.make_async_copy(own, RI.at[t, mine], irecv.at[t]).start()

        @pl.when(t == 0)
        def _():
            for copy in loads[7:11]:
                copy.wait()

        up, down, right, left, across = v_copies(t)
        recv_halo(up, down, right, t, HV, DV, v_rows, v_cols)
        sent_halo(up, down, right, left)

        def stress_chunk(i, c):
            r0 = pl.multiple_of(i * 8, 8)
            chunk = pl.ds(r0, 8)
            inner = pl.ds(r0 + 8, 8)
            vs = []
            for p in range(4):
                tall = VP[p, pl.ds(r0, 24), cols_in]
                wide = VP[p, inner, :]
                v = tall[8:16]
                vs.append(v)
                st = stiff[p, chunk, :]
                up1, up2, dn1 = (roll(tall, s, 0)[8:16] for s in (-1, -2, 1))
                SP[p, inner, :] = SP[p, inner, :] + st * (C1 * (up1 - v) - C2 * (up2 - dn1))
                up1, up2, dn1 = (roll(wide, s, 1)[:, LW : LW + CW] for s in (-1, -2, 1))
                DP[p, chunk, cols_in] = DP[p, chunk, cols_in] + st * (C1 * (up1 - v) - C2 * (up2 - dn1))
            for p in range(1, 4):
                far = 0.0 - (vs[p - 2] if p >= 2 else 0.0)
                if p < 3:
                    far = vs[p + 1] + far
                NS[p, chunk, :] = NS[p, chunk, :] + stiff[p, chunk, :] * (C1 * (vs[p] - vs[p - 1]) - C2 * far)
            return c

        lax.fori_loop(0, RW // 8, stress_chunk, 0)
        up, down, right, left = s_copies(t)
        start_halo(up, down, right, left)

        @pl.when(t == NSTEP - 1)
        def _():
            for copy in out_copies()[:2]:
                copy.start()

        across.wait()
        SG[...] = side * (VP[0, rows_in, cols_in] - NP[t])

        @pl.when(t < NSTEP - 1)
        def _():
            lag_sums(t + 1)

        @pl.when(t == 0)
        def _():
            for copy in loads[11:]:
                copy.wait()

        pltpu.make_async_copy(RI.at[t], RI.at[t], irecv.at[t]).wait()
        OS[...] = table_right(RI[t].T, TI, ((1,), (0,)))

        def depth_half(half, p, put):
            for hl in range(HC):
                tw = WI[q, half * HC + hl]
                total = None
                for k in range(2 * R):
                    r, c = k // 2, k % 2
                    term = tw[k : k + 1] * OS[r * B : (r + 1) * B, (2 * p + c) * A : (2 * p + c + 1) * A]
                    total = term if total is None else total + term
                put[p * B : (p + 1) * B, hl * A : (hl + 1) * A] = total

        parts = []
        for p in range(2):
            depth_half(1 - q, p, PS.at[t])
            here = pl.ds(p * B, B)
            part = remote(PS.at[t, here], PR.at[t, here], psend.at[p, t], precv.at[p, t], (g, j, 1 - q))
            part.start()
            parts.append(part)
        for p in range(2):
            depth_half(q, p, RL)

        CH = 16

        def friction_chunk(i, c):
            chunk = pl.ds(pl.multiple_of(i * CH, CH), CH)
            guess = SG[chunk, :]
            loading = szero[chunk, :] + (RL[chunk, :] + PR[t, chunk, :]) + guess
            a = direct[chunk, :]
            ls = LS[chunk, :]
            factor = jnp.exp(ls)
            af = a * factor
            v = guess
            for _ in range(NEWTON):
                s = v * factor
                root = jnp.sqrt(1.0 + s * s)
                size = jnp.log(jnp.abs(s) + root)
                misfit = a * jnp.where(s < 0.0, -size, size) + v - loading
                v = v - misfit / (af / root + 1.0)
            SL[t, q, chunk, :] = v
            TR[chunk, :] = side * (loading - v)
            LS[chunk, :] = 0.75 * ls - 0.2 * jnp.log(1.0 + v * v) + 0.1
            return c

        slips = []
        for p in range(2):
            parts[p].wait_recv()
            lax.fori_loop(p * B // CH, (p + 1) * B // CH, friction_chunk, 0)
            here = pl.ds(p * B, B)
            slip = remote(SL.at[t, q, here], SL.at[t, q, here], lsend.at[p, t], lrecv.at[p, t], (g, j, 1 - q))
            slip.start()
            slips.append(slip)

        def depth_terms(half, p, add):
            acc = None
            for hl in range(HC):
                tw = WF[2 * g + q, half * HC + hl]
                cells = SL[t, half, p * B : (p + 1) * B, hl * A : (hl + 1) * A]
                terms = [tw[k : k + 1] * cells for k in range(2 * R)]
                acc = terms if acc is None else [x + y for x, y in zip(acc, terms)]
            for k in range(2 * R):
                r, c = k // 2, k % 2
                at = (slice(r * B, (r + 1) * B), slice((2 * p + c) * A, (2 * p + c + 1) * A))
                US[at] = US[at] + acc[k] if add else acc[k]

        for p in range(2):
            depth_terms(q, p, False)
        for p in range(2):
            here = pl.ds(p * B, B)
            land = SL.at[t, 1 - q, here]
            pltpu.make_async_copy(land, land, lrecv.at[p, t]).wait()
            depth_terms(1 - q, p, True)
        SF[t] = table_left(TF, US[...], ((1,), (1,)))
        spot = pl.ds(j * 4, 4)

        def send_slip(peer):
            remote(SF.at[t, pl.ds(peer * 4, 4)], RF.at[t, spot], fsend.at[t], frecv.at[t], (g, peer, q)).start()

        each_peer(send_slip)
        pltpu.make_async_copy(SF.at[t, spot], RF.at[t, spot], frecv.at[t]).start()

        recv_halo(up, down, right, t, HS, DS, s_rows, d_cols)
        sent_halo(up, down, right, left)
        NS[0] = TR[...]

        def velocity_chunk(i, c):
            r0 = pl.multiple_of(i * 8, 8)
            chunk = pl.ds(r0, 8)
            inner = pl.ds(r0 + 8, 8)
            n0, n1, n2, n3 = (NS[p, chunk, :] for p in range(4))
            plane_terms = [
                C1 * (n1 - n0) - C2 * n2,
                C1 * (n2 - n1) - C2 * (n3 - n0),
                C1 * (n3 - n2) + C2 * n1,
                C2 * n2 - C1 * n3,
            ]
            for p in range(4):
                tall = SP[p, pl.ds(r0, 24), :]
                wide = DP[p, chunk, :]
                dn1, dn2, up1 = (roll(tall, s, 0)[8:16] for s in (1, 2, -1))
                total = plane_terms[p] + (C1 * (tall[8:16] - dn1) - C2 * (up1 - dn2))
                dn1, dn2, up1 = (roll(wide, s, 1)[:, LW : LW + CW] for s in (1, 2, -1))
                total = total + (C1 * (wide[:, LW : LW + CW] - dn1) - C2 * (up1 - dn2))
                VP[p, inner, cols_in] = VP[p, inner, cols_in] + buoy[p, chunk, :] * total
            return c

        lax.fori_loop(0, RW // 8, velocity_chunk, 0)

        @pl.when(t < NSTEP - 1)
        def _():
            later = v_copies(t + 1)
            start_halo(*later[:4])
            later[4].start()

        @pl.when(t == NSTEP - 1)
        def _():
            for copy in out_copies()[2:]:
                copy.start()

        for p in range(2):
            parts[p].wait_send()
            slips[p].wait_send()
        pltpu.make_async_copy(RF.at[t], RF.at[t], frecv.at[t]).wait()
        x = table_right(RF[t].T, TV, ((1,), (0,)))
        xr, xi = x[:, :A], x[:, A:]
        tall = jnp.concatenate([xr * TW[0] + xi * TW[1], xi * TW[0] - xr * TW[1]], axis=0)
        fresh = table_left(L3, tall, ((1,), (0,)))
        FR[t] = fresh
        for d in range(NSTEP - 1):
            ACC[t + 1 + d] = ACC[t + 1 + d] + WD[d] * fresh
        pltpu.make_async_copy(FR.at[t], out_s.at[t], outsem.at[5 + t]).start()
        return carry

    lax.fori_loop(0, NSTEP, step_body, 0)

    for copy in out_copies():
        copy.wait()
    for t in range(NSTEP):
        pltpu.make_async_copy(FR.at[t], out_s.at[t], outsem.at[5 + t]).wait()
        left = RI.at[t, pl.ds(0, (2 * nx - 1) * 4)]
        pltpu.make_async_copy(left, left, isend.at[t]).wait()
        left = RF.at[t, pl.ds(0, (nx - 1) * 4)]
        pltpu.make_async_copy(left, left, fsend.at[t]).wait()


def per_device(nx, fields, buoyancy, stiffness, stress_zero, direct_effect, log_state, kernel, history, truncation):
    planes, rows, cols = fields.shape[2:]
    hist, modes, _, strike = history.shape
    A = 2 * nx
    B = rows // 2
    RB = modes * B
    depth = 2 * cols
    scale = 1.0 / math.sqrt(strike * depth)
    mats, vecs = make_tables(nx, rows, modes, scale)
    kernel = kernel.reshape(hist, modes, B, A).transpose(0, 2, 1, 3).reshape(hist, RB, A)
    history = history.reshape(hist, modes, 2, B, A).transpose(0, 1, 3, 2, 4).reshape(hist, 2 * RB, A)
    truncation = truncation.reshape(modes, B, A).transpose(1, 0, 2).reshape(RB, A)
    LW = min(128, cols)
    vm = pltpu.VMEM
    dma = pltpu.SemaphoreType.DMA
    args = [
        fields.reshape(4, planes, rows, cols), buoyancy[0], stiffness[0], stress_zero, direct_effect, log_state,
        kernel, history, truncation, *[jnp.asarray(x) for x in mats], *[jnp.asarray(x) for x in vecs],
    ]
    scratch = [vm(x.shape, x.dtype) for x in args[1:]] + [
        vm((hist, 2 * RB, A), F32),
        vm((planes, rows, cols), F32),
        vm((NSTEP, 2 * RB, A), F32),
        vm((planes, rows + 16, cols + 2 * LW), F32),
        vm((planes, rows + 16, cols), F32),
        vm((planes, rows, cols + 2 * LW), F32),
        vm((2 * NSTEP - 1, 2 * RB, A), F32),
        vm((NSTEP, 4 * nx, RB), F32),
        vm((NSTEP, 8 * nx, RB), F32),
        vm((RB, 4 * A), F32),
        vm((NSTEP, rows, cols), F32),
        vm((rows, cols), F32),
        vm((NSTEP, rows, cols), F32),
        vm((NSTEP, 2, rows, cols), F32),
        vm((RB, 4 * A), F32),
        vm((NSTEP, 4 * nx, RB), F32),
        vm((NSTEP, 4 * nx, RB), F32),
        vm((rows, cols), F32),
        vm((rows, cols), F32),
        vm((NSTEP, 2, planes, 8, cols), F32),
        vm((NSTEP, planes, rows, LW), F32),
        vm((NSTEP, rows, cols), F32),
        vm((NSTEP, 2, planes, 8, cols), F32),
        vm((NSTEP, planes, rows, LW), F32),
        dma((21,)), dma((5 + NSTEP,)),
        dma((NSTEP,)), dma((NSTEP,)), dma((NSTEP,)), dma((NSTEP,)),
        dma((2, NSTEP)), dma((2, NSTEP)), dma((2, NSTEP)), dma((2, NSTEP)),
        dma((3,)), dma((3, NSTEP)), dma((3,)), dma((3, NSTEP)), dma, dma((NSTEP,)),
    ]
    hbm = pl.BlockSpec(memory_space=pl.ANY)
    out_f, out_l, out_s = pl.pallas_call(
        functools.partial(kernel_body, nx),
        out_shape=(
            jax.ShapeDtypeStruct((4, planes, rows, cols), F32),
            jax.ShapeDtypeStruct((rows, cols), F32),
            jax.ShapeDtypeStruct((NSTEP, 2 * RB, A), F32),
        ),
        in_specs=[hbm] * len(args),
        out_specs=(hbm, hbm, hbm),
        scratch_shapes=scratch,
        compiler_params=pltpu.CompilerParams(
            collective_id=0, has_side_effects=True, vmem_limit_bytes=60 * 1024 * 1024
        ),
    )(*args)
    spectra = out_s.reshape(NSTEP, modes, B, 2, A).transpose(0, 1, 3, 2, 4).reshape(NSTEP, modes, 2, strike)
    return out_f.reshape(4, 1, planes, rows, cols), out_l, spectra


def solution(mesh):
    return jax.shard_map(
        functools.partial(per_device, mesh.shape["gx"]),
        mesh=mesh,
        in_specs=(
            P(None, "grp", None, "gx", "gz"),
            P("grp", None, "gx", "gz"),
            P("grp", None, "gx", "gz"),
            P("gx", "gz"),
            P("gx", "gz"),
            P("gx", "gz"),
            P(None, ("grp", "gx", "gz"), None),
            P(None, ("grp", "gx", "gz"), None, None),
            P(("grp", "gx", "gz"), None),
        ),
        out_specs=(
            P(None, "grp", None, "gx", "gz"),
            P("gx", "gz"),
            P(None, ("grp", "gx", "gz"), None, None),
        ),
        check_vma=False,
    )
```

```python
import functools
import math

import jax
import jax.numpy as jnp
import numpy as np
from jax import lax
from jax.experimental import pallas as pl
from jax.experimental.pallas import tpu as pltpu
from jax.sharding import PartitionSpec as P

NSTEP = 4
NEWTON = 4
C1 = 9.0 / 8.0
C2 = 1.0 / 24.0
MESH = pl.DeviceIdType.MESH
BF = jnp.bfloat16
F32 = jnp.float32


def split_table(table):
    hi = np.asarray(table, np.float32).astype(jnp.bfloat16)
    lo = (table - hi.astype(np.float64)).astype(jnp.bfloat16)
    return np.stack([hi, lo])


def cis(turns):
    return np.cos(2 * np.pi * turns), np.sin(2 * np.pi * turns)


def make_tables(nx, rows, modes, scale):
    A = 2 * nx
    B = rows // 2
    R = modes
    depth = 4 * nx * R
    strike = nx * rows
    eye_r = np.eye(R)
    eye_p = np.eye(2)
    m, b, k, a = np.arange(B), np.arange(B), np.arange(A), np.arange(A)
    c, s = cis(np.outer(m, b) / B)
    inv = np.array([[c, -s], [s, c]])
    fwd = np.array([[c, s], [-s, c]])
    L1 = np.einsum("xybm,rs->xrbsmy", inv, eye_r).reshape(2 * R * B, 2 * R * B)
    L3 = np.einsum("xymb,rs->rmxysb", fwd, eye_r).reshape(2 * R * B, 2 * R * B) * scale
    c, s = cis(np.outer(b, k) / strike)
    twiddle = np.stack([np.tile(c, (R, 1)), np.tile(s, (R, 1))])
    c, s = cis(np.outer(a, k) / A)
    inv = np.array([[c, -s], [s, c]]).reshape(2, 2, nx, 2, A)
    T2 = np.einsum("xyjpk->jxpyk", inv).reshape(4 * nx, 2 * A)
    fwd = np.array([[c, s], [-s, c]]).reshape(2, 2, nx, 2, A)
    TV = np.einsum("xyjpk->jpyxk", fwd).reshape(4 * nx, 2 * A)
    i, z = np.arange(nx), np.arange(A)
    c, s = cis(np.outer(i, z) / A)
    sign = np.where(np.arange(2)[:, None] * z[None, :] % 2 == 1, -1.0, 1.0)
    inv = np.array([[c, -s], [s, c]])
    TI = np.einsum("xyiz,gz,pn->giypnxz", inv, sign, eye_p).reshape(8 * nx, 4 * A)
    fwd = np.array([[c, s], [-s, c]])
    TF = np.einsum("xyiz,pn->ipxnyz", fwd, eye_p).reshape(4 * nx, 4 * A)
    zz = np.arange(depth).reshape(2 * R, 1, A)
    r = np.arange(R)[None, :, None]
    wi, wf = [], []
    for q in range(2):
        c, s = cis((R * q + r) * zz / depth)
        wi.append(np.stack([c, -s], axis=2).reshape(2 * R, 2 * R, A) * scale)
    for g in range(2):
        for q in range(2):
            c, s = cis((R * q + r) * zz / depth)
            wf.append(np.stack([c, -s], axis=2).reshape(2 * R, 2 * R, A) * sign[g])
    mats = [split_table(x) for x in (L1, T2, TI, TF, TV, L3)]
    return mats, [np.asarray(x, np.float32) for x in (twiddle, np.stack(wi), np.stack(wf))]


def split(x):
    hi = x.astype(BF)
    return hi, (x - hi.astype(F32)).astype(BF)


def dot(x, y, dims):
    return lax.dot_general(x, y, (dims, ((), ())), preferred_element_type=F32)


def table_left(tab, x, dims):
    hi, lo = split(x)
    return dot(tab[0], hi, dims) + (dot(tab[0], lo, dims) + dot(tab[1], hi, dims))


def table_right(x, tab, dims):
    hi, lo = split(x)
    return dot(hi, tab[0], dims) + (dot(lo, tab[0], dims) + dot(hi, tab[1], dims))


def roll(x, shift, axis):
    return pltpu.roll(x, shift % x.shape[axis], axis)


def kernel_body(
    nx, fields_h, buoy_h, stiff_h, szero_h, direct_h, logs_h, kern_h, hist_h, trunc_h,
    L1_h, T2_h, TI_h, TF_h, TV_h, L3_h, TW_h, WI_h, WF_h,
    out_f, out_l, out_s,
    buoy, stiff, szero, direct, LS, KW, H, TRN, L1, T2, TI, TF, TV, L3, TW, WI, WF, WD, NS, FR,
    VP, SP, DP, ACC, GS, RI, OS, PS, RL, PR, SL, US, SF, RF, TR, SG, HV, DV, NP, HS, DS, HO,
    insem, outsem, isend, irecv, fsend, frecv, psend, precv, lsend, lrecv, vsend, vrecv, ssend, srecv, gsend, grecv,
):
    g, j, q = lax.axis_index("grp"), lax.axis_index("gx"), lax.axis_index("gz")
    A = 2 * nx
    RB = TW.shape[1]
    RW, CW = szero.shape
    B = RW // 2
    R = RB // B
    LW = DV.shape[3]
    HC = CW // A
    HIST = H.shape[0]
    side = (2 * g - 1).astype(F32)
    rows_in = pl.ds(8, RW)
    cols_in = pl.ds(LW, CW)

    if nx == 64:
        turn = (2, 3, 1, 0)
        xs = [lax.rem(lax.div(j, 16) + k, 4) * 16 for k in turn]
        ys = [lax.rem(j, 4) + k for k in turn]
        peers_xy = [x + lax.rem(y, 4) for x in xs for y in ys]
        zs = lax.rem(lax.div(j, 4), 4)
        outer = 4

        def layer(i):
            return lax.rem(zs + i + 2, 4) * 4

        own_layer, own_xy = 2, 15
    else:
        peers_xy = [j * 0]
        outer = nx

        def layer(i):
            return lax.rem(j + i + 1, nx)

        own_layer, own_xy = nx - 1, 0

    def each_peer(act):
        def one_layer(i, carry):
            z = layer(i)
            for n, xy in enumerate(peers_xy):
                if n == own_xy:

                    @pl.when(i != own_layer)
                    def _():
                        act(z + xy)
                else:
                    act(z + xy)
            return carry

        lax.fori_loop(0, outer, one_layer, 0)

    barrier = pltpu.get_barrier_semaphore()

    def greet(peer):
        pl.semaphore_signal(barrier, inc=1, device_id=(g, peer, q), device_id_type=MESH)
        pl.semaphore_signal(barrier, inc=1, device_id=(1 - g, peer, q), device_id_type=MESH)

    each_peer(greet)
    pl.semaphore_signal(barrier, inc=1, device_id=(1 - g, j, q), device_id_type=MESH)
    pl.semaphore_signal(barrier, inc=1, device_id=(g, j, 1 - q), device_id_type=MESH)

    pairs = [
        (kern_h, KW), (trunc_h, TRN), (hist_h, H), (L1_h, L1), (TW_h, TW), (T2_h, T2),
        (fields_h.at[0], VP.at[:, rows_in, cols_in]), (stiff_h, stiff), (fields_h.at[2], SP.at[:, rows_in, :]),
        (fields_h.at[3], DP.at[:, :, cols_in]), (fields_h.at[1], NS), (TI_h, TI), (WI_h, WI), (szero_h, szero),
        (direct_h, direct), (logs_h, LS), (WF_h, WF), (TF_h, TF), (buoy_h, buoy), (TV_h, TV), (L3_h, L3),
    ]
    loads = [pltpu.make_async_copy(src, dst, insem.at[n]) for n, (src, dst) in enumerate(pairs)]
    for copy in loads:
        copy.start()
    for t in range(ACC.shape[0]):
        ACC[t] = jnp.zeros((2 * RB, A), F32)
    VP[:, pl.ds(0, 8), :] = jnp.zeros((4, 8, CW + 2 * LW), F32)
    VP[:, pl.ds(8 + RW, 8), :] = jnp.zeros((4, 8, CW + 2 * LW), F32)
    VP[:, rows_in, pl.ds(0, LW)] = jnp.zeros((4, RW, LW), F32)
    VP[:, rows_in, pl.ds(LW + CW, LW)] = jnp.zeros((4, RW, LW), F32)
    SP[:, pl.ds(0, 8), :] = jnp.zeros((4, 8, CW), F32)
    SP[:, pl.ds(8 + RW, 8), :] = jnp.zeros((4, 8, CW), F32)
    DP[:, :, pl.ds(0, LW)] = jnp.zeros((4, RW, LW), F32)
    DP[:, :, pl.ds(LW + CW, LW)] = jnp.zeros((4, RW, LW), F32)

    loads[0].wait()
    loads[1].wait()

    def mask_lag(lag, carry):
        for r in range(R):
            pick = pl.ds(r, B, stride=R)
            kept = jnp.where(lag < TRN[pick, :], KW[lag, pick, :], 0.0)
            for c in range(2):
                WD[lag, pl.ds(r * 2 * B + c, B, stride=2), :] = kept
        return carry

    lax.fori_loop(0, HIST, mask_lag, 0)

    def lag_sums(ahead):
        for r in range(R):
            part = pl.ds(r * 2 * B, 2 * B)

            def one_lag(lag, total):
                return total + WD[lag + ahead, part, :] * H[lag, part, :]

            ACC[ahead, part, :] = lax.fori_loop(0, HIST - ahead, one_lag, ACC[ahead, part, :])

    for copy in loads[2:6]:
        copy.wait()
    lag_sums(0)
    loads[6].wait()
    pl.semaphore_wait(barrier, 2 * (nx - 1) + 2)

    def remote(src, dst, send, recv, device):
        return pltpu.make_async_remote_copy(
            src_ref=src, dst_ref=dst, send_sem=send, recv_sem=recv, device_id=device, device_id_type=MESH
        )

    def row_copies(kind, land, t, send, recv):
        up = remote(HO.at[kind, 0], land.at[t, 0], send.at[0], recv.at[0, t], (g, lax.rem(j + 1, nx), q))
        down = remote(HO.at[kind, 1], land.at[t, 1], send.at[1], recv.at[1, t], (g, lax.rem(j + nx - 1, nx), q))
        return up, down

    def pack_rows(kind, ref, cols):
        for p in range(4):
            HO[kind, 0, 2 * p : 2 * p + 2, :] = ref[p, pl.ds(RW + 6, 2), cols]
            HO[kind, 1, 2 * p : 2 * p + 2, :] = ref[p, pl.ds(8, 2), cols]

    def v_copies(t):
        up, down = row_copies(0, HV, t, vsend, vrecv)
        right = remote(VP.at[:, rows_in, pl.ds(CW, LW)], DV.at[t], vsend.at[2], vrecv.at[2, t], (g, j, 1 - q))
        left = remote(VP.at[:, rows_in, pl.ds(LW, LW)], DV.at[t], vsend.at[2], vrecv.at[2, t], (g, j, 1 - q))
        across = remote(VP.at[0, rows_in, cols_in], NP.at[t], gsend, grecv.at[t], (1 - g, j, q))
        return up, down, right, left, across

    def s_copies(t):
        up, down = row_copies(1, HS, t, ssend, srecv)
        right = remote(DP.at[:, :, pl.ds(CW, LW)], DS.at[t], ssend.at[2], srecv.at[2, t], (g, j, 1 - q))
        left = remote(DP.at[:, :, pl.ds(LW, LW)], DS.at[t], ssend.at[2], srecv.at[2, t], (g, j, 1 - q))
        return up, down, right, left

    def start_halo(up, down, right, left):
        @pl.when(j < nx - 1)
        def _():
            up.start()

        @pl.when(j > 0)
        def _():
            down.start()

        @pl.when(q == 0)
        def _():
            right.start()

        @pl.when(q == 1)
        def _():
            left.start()

    def sent_halo(up, down, right, left):
        @pl.when(j < nx - 1)
        def _():
            up.wait_send()

        @pl.when(j > 0)
        def _():
            down.wait_send()

        right.wait_send()

    def recv_halo(up, down, right, t, land, depth_land, put_rows, put_cols):
        @pl.when(j > 0)
        def _():
            up.wait_recv()
            put_rows(6, land[t, 0])

        @pl.when(j < nx - 1)
        def _():
            down.wait_recv()
            put_rows(8 + RW, land[t, 1])

        right.wait_recv()

        @pl.when(q == 0)
        def _():
            put_cols(LW + CW, depth_land[t])

        @pl.when(q == 1)
        def _():
            put_cols(0, depth_land[t])

    def v_rows(at, x):
        for p in range(4):
            VP[p, pl.ds(at, 2), cols_in] = x[2 * p : 2 * p + 2]

    def v_cols(at, x):
        VP[:, rows_in, pl.ds(at, LW)] = x

    def s_rows(at, x):
        for p in range(4):
            SP[p, pl.ds(at, 2), :] = x[2 * p : 2 * p + 2]

    def d_cols(at, x):
        DP[:, :, pl.ds(at, LW)] = x

    pack_rows(0, VP, cols_in)
    first = v_copies(0)
    start_halo(*first[:4])
    first[4].start()

    def out_copies():
        return [
            pltpu.make_async_copy(SP.at[:, rows_in, :], out_f.at[2], outsem.at[0]),
            pltpu.make_async_copy(DP.at[:, :, cols_in], out_f.at[3], outsem.at[1]),
            pltpu.make_async_copy(VP.at[:, rows_in, cols_in], out_f.at[0], outsem.at[2]),
            pltpu.make_async_copy(NS, out_f.at[1], outsem.at[3]),
            pltpu.make_async_copy(LS, out_l, outsem.at[4]),
        ]

    def step_body(t, carry):
        x = table_left(L1, ACC[t], ((1,), (0,)))
        xr, xi = x[:RB], x[RB:]
        wide = jnp.concatenate([xr * TW[0] - xi * TW[1], xr * TW[1] + xi * TW[0]], axis=1)
        GS[t] = table_left(T2, wide, ((1,), (1,)))
        mine = pl.ds((g * nx + j) * 4, 4)

        def send_modes(peer):
            block = GS.at[t, pl.ds(peer * 4, 4)]
            remote(block, RI.at[t, mine], isend.at[t], irecv.at[t], (1 - g, peer, q)).start()
            remote(block, RI.at[t, mine], isend.at[t], irecv.at[t], (g, peer, q)).start()

        each_peer(send_modes)
        own = GS.at[t, pl.ds(j * 4, 4)]
        remote(own, RI.at[t, mine], isend.at[t], irecv.at[t], (1 - g, j, q)).start()
        pltpu.make_async_copy(own, RI.at[t, mine], irecv.at[t]).start()

        @pl.when(t == 0)
        def _():
            for copy in loads[7:11]:
                copy.wait()

        up, down, right, left, across = v_copies(t)
        recv_halo(up, down, right, t, HV, DV, v_rows, v_cols)
        sent_halo(up, down, right, left)

        def stress_chunk(i, c):
            r0 = pl.multiple_of(i * 8, 8)
            chunk = pl.ds(r0, 8)
            inner = pl.ds(r0 + 8, 8)
            vs = []
            for p in range(4):
                tall = VP[p, pl.ds(r0, 24), cols_in]
                wide = VP[p, inner, :]
                v = tall[8:16]
                vs.append(v)
                st = stiff[p, chunk, :]
                up1, up2, dn1 = (roll(tall, s, 0)[8:16] for s in (-1, -2, 1))
                SP[p, inner, :] = SP[p, inner, :] + st * (C1 * (up1 - v) - C2 * (up2 - dn1))
                up1, up2, dn1 = (roll(wide, s, 1)[:, LW : LW + CW] for s in (-1, -2, 1))
                DP[p, chunk, cols_in] = DP[p, chunk, cols_in] + st * (C1 * (up1 - v) - C2 * (up2 - dn1))
            for p in range(1, 4):
                far = 0.0 - (vs[p - 2] if p >= 2 else 0.0)
                if p < 3:
                    far = vs[p + 1] + far
                NS[p, chunk, :] = NS[p, chunk, :] + stiff[p, chunk, :] * (C1 * (vs[p] - vs[p - 1]) - C2 * far)
            return c

        lax.fori_loop(0, RW // 8, stress_chunk, 0)
        pack_rows(1, SP, slice(None))
        up, down, right, left = s_copies(t)
        start_halo(up, down, right, left)

        @pl.when(t == NSTEP - 1)
        def _():
            for copy in out_copies()[:2]:
                copy.start()

        across.wait()
        SG[...] = side * (VP[0, rows_in, cols_in] - NP[t])

        @pl.when(t < NSTEP - 1)
        def _():
            lag_sums(t + 1)

        @pl.when(t == 0)
        def _():
            for copy in loads[11:]:
                copy.wait()

        pltpu.make_async_copy(RI.at[t], RI.at[t], irecv.at[t]).wait()
        OS[...] = table_right(RI[t].T, TI, ((1,), (0,)))

        def depth_half(half, p, put):
            for hl in range(HC):
                tw = WI[q, half * HC + hl]
                total = None
                for k in range(2 * R):
                    r, c = k // 2, k % 2
                    term = tw[k : k + 1] * OS[r * B : (r + 1) * B, (2 * p + c) * A : (2 * p + c + 1) * A]
                    total = term if total is None else total + term
                put[p * B : (p + 1) * B, hl * A : (hl + 1) * A] = total

        parts = []
        for p in range(2):
            depth_half(1 - q, p, PS.at[t])
            here = pl.ds(p * B, B)
            part = remote(PS.at[t, here], PR.at[t, here], psend.at[p, t], precv.at[p, t], (g, j, 1 - q))
            part.start()
            parts.append(part)
        for p in range(2):
            depth_half(q, p, RL)

        CH = 16

        def friction_chunk(i, c):
            chunk = pl.ds(pl.multiple_of(i * CH, CH), CH)
            guess = SG[chunk, :]
            loading = szero[chunk, :] + (RL[chunk, :] + PR[t, chunk, :]) + guess
            a = direct[chunk, :]
            ls = LS[chunk, :]
            factor = jnp.exp(ls)
            af = a * factor
            v = guess
            for _ in range(NEWTON):
                s = v * factor
                root = jnp.sqrt(1.0 + s * s)
                size = jnp.log(jnp.abs(s) + root)
                misfit = a * jnp.where(s < 0.0, -size, size) + v - loading
                v = v - misfit / (af / root + 1.0)
            SL[t, q, chunk, :] = v
            TR[chunk, :] = side * (loading - v)
            LS[chunk, :] = 0.75 * ls - 0.2 * jnp.log(1.0 + v * v) + 0.1
            return c

        slips = []
        for p in range(2):
            parts[p].wait_recv()
            lax.fori_loop(p * B // CH, (p + 1) * B // CH, friction_chunk, 0)
            here = pl.ds(p * B, B)
            slip = remote(SL.at[t, q, here], SL.at[t, q, here], lsend.at[p, t], lrecv.at[p, t], (g, j, 1 - q))
            slip.start()
            slips.append(slip)

        def depth_terms(half, p, add):
            acc = None
            for hl in range(HC):
                tw = WF[2 * g + q, half * HC + hl]
                cells = SL[t, half, p * B : (p + 1) * B, hl * A : (hl + 1) * A]
                terms = [tw[k : k + 1] * cells for k in range(2 * R)]
                acc = terms if acc is None else [x + y for x, y in zip(acc, terms)]
            for k in range(2 * R):
                r, c = k // 2, k % 2
                at = (slice(r * B, (r + 1) * B), slice((2 * p + c) * A, (2 * p + c + 1) * A))
                US[at] = US[at] + acc[k] if add else acc[k]

        for p in range(2):
            depth_terms(q, p, False)
        for p in range(2):
            here = pl.ds(p * B, B)
            land = SL.at[t, 1 - q, here]
            pltpu.make_async_copy(land, land, lrecv.at[p, t]).wait()
            depth_terms(1 - q, p, True)
        SF[t] = table_left(TF, US[...], ((1,), (1,)))
        spot = pl.ds(j * 4, 4)

        def send_slip(peer):
            remote(SF.at[t, pl.ds(peer * 4, 4)], RF.at[t, spot], fsend.at[t], frecv.at[t], (g, peer, q)).start()

        each_peer(send_slip)
        pltpu.make_async_copy(SF.at[t, spot], RF.at[t, spot], frecv.at[t]).start()

        recv_halo(up, down, right, t, HS, DS, s_rows, d_cols)
        sent_halo(up, down, right, left)
        NS[0] = TR[...]

        def velocity_chunk(i, c):
            r0 = pl.multiple_of(i * 8, 8)
            chunk = pl.ds(r0, 8)
            inner = pl.ds(r0 + 8, 8)
            n0, n1, n2, n3 = (NS[p, chunk, :] for p in range(4))
            plane_terms = [
                C1 * (n1 - n0) - C2 * n2,
                C1 * (n2 - n1) - C2 * (n3 - n0),
                C1 * (n3 - n2) + C2 * n1,
                C2 * n2 - C1 * n3,
            ]
            for p in range(4):
                tall = SP[p, pl.ds(r0, 24), :]
                wide = DP[p, chunk, :]
                dn1, dn2, up1 = (roll(tall, s, 0)[8:16] for s in (1, 2, -1))
                total = plane_terms[p] + (C1 * (tall[8:16] - dn1) - C2 * (up1 - dn2))
                dn1, dn2, up1 = (roll(wide, s, 1)[:, LW : LW + CW] for s in (1, 2, -1))
                total = total + (C1 * (wide[:, LW : LW + CW] - dn1) - C2 * (up1 - dn2))
                VP[p, inner, cols_in] = VP[p, inner, cols_in] + buoy[p, chunk, :] * total
            return c

        lax.fori_loop(0, RW // 8, velocity_chunk, 0)

        @pl.when(t < NSTEP - 1)
        def _():
            pack_rows(0, VP, cols_in)
            later = v_copies(t + 1)
            start_halo(*later[:4])
            later[4].start()

        @pl.when(t == NSTEP - 1)
        def _():
            for copy in out_copies()[2:]:
                copy.start()

        for p in range(2):
            parts[p].wait_send()
            slips[p].wait_send()
        pltpu.make_async_copy(RF.at[t], RF.at[t], frecv.at[t]).wait()
        x = table_right(RF[t].T, TV, ((1,), (0,)))
        xr, xi = x[:, :A], x[:, A:]
        tall = jnp.concatenate([xr * TW[0] + xi * TW[1], xi * TW[0] - xr * TW[1]], axis=0)
        fresh = table_left(L3, tall, ((1,), (0,)))
        FR[t] = fresh
        for d in range(NSTEP - 1):
            ACC[t + 1 + d] = ACC[t + 1 + d] + WD[d] * fresh
        pltpu.make_async_copy(FR.at[t], out_s.at[t], outsem.at[5 + t]).start()
        return carry

    lax.fori_loop(0, NSTEP, step_body, 0)

    for copy in out_copies():
        copy.wait()
    for t in range(NSTEP):
        pltpu.make_async_copy(FR.at[t], out_s.at[t], outsem.at[5 + t]).wait()
        left = RI.at[t, pl.ds(0, (2 * nx - 1) * 4)]
        pltpu.make_async_copy(left, left, isend.at[t]).wait()
        left = RF.at[t, pl.ds(0, (nx - 1) * 4)]
        pltpu.make_async_copy(left, left, fsend.at[t]).wait()


def hand_over(f_in, l_in, s_in, f_out, l_out, s_out, f, l, s, sem):
    pieces = [(f_in.at[n], f.at[n], f_out.at[n]) for n in range(f.shape[0])]
    pieces += [(s_in, s, s_out), (l_in, l, l_out)]
    for n, (src, mid, _) in enumerate(pieces):
        pltpu.make_async_copy(src, mid, sem.at[0, n]).start()
    for n, (src, mid, dst) in enumerate(pieces):
        pltpu.make_async_copy(src, mid, sem.at[0, n]).wait()
        pltpu.make_async_copy(mid, dst, sem.at[1, n]).start()
    for n, (_, mid, dst) in enumerate(pieces):
        pltpu.make_async_copy(mid, dst, sem.at[1, n]).wait()


def per_device(nx, fields, buoyancy, stiffness, stress_zero, direct_effect, log_state, kernel, history, truncation):
    planes, rows, cols = fields.shape[2:]
    hist, modes, _, strike = history.shape
    A = 2 * nx
    B = rows // 2
    RB = modes * B
    depth = 2 * cols
    scale = 1.0 / math.sqrt(strike * depth)
    mats, vecs = make_tables(nx, rows, modes, scale)
    kernel = kernel.reshape(hist, modes, B, A).transpose(0, 2, 1, 3).reshape(hist, RB, A)
    history = history.reshape(hist, modes, 2, B, A).transpose(0, 1, 3, 2, 4).reshape(hist, 2 * RB, A)
    truncation = truncation.reshape(modes, B, A).transpose(1, 0, 2).reshape(RB, A)
    LW = min(128, cols)
    vm = pltpu.VMEM
    dma = pltpu.SemaphoreType.DMA
    args = [
        fields.reshape(4, planes, rows, cols), buoyancy[0], stiffness[0], stress_zero, direct_effect, log_state,
        kernel, history, truncation, *[jnp.asarray(x) for x in mats], *[jnp.asarray(x) for x in vecs],
    ]
    scratch = [vm(x.shape, x.dtype) for x in args[1:]] + [
        vm((hist, 2 * RB, A), F32),
        vm((planes, rows, cols), F32),
        vm((NSTEP, 2 * RB, A), F32),
        vm((planes, rows + 16, cols + 2 * LW), F32),
        vm((planes, rows + 16, cols), F32),
        vm((planes, rows, cols + 2 * LW), F32),
        vm((2 * NSTEP - 1, 2 * RB, A), F32),
        vm((NSTEP, 4 * nx, RB), F32),
        vm((NSTEP, 8 * nx, RB), F32),
        vm((RB, 4 * A), F32),
        vm((NSTEP, rows, cols), F32),
        vm((rows, cols), F32),
        vm((NSTEP, rows, cols), F32),
        vm((NSTEP, 2, rows, cols), F32),
        vm((RB, 4 * A), F32),
        vm((NSTEP, 4 * nx, RB), F32),
        vm((NSTEP, 4 * nx, RB), F32),
        vm((rows, cols), F32),
        vm((rows, cols), F32),
        vm((NSTEP, 2, 8, cols), F32),
        vm((NSTEP, planes, rows, LW), F32),
        vm((NSTEP, rows, cols), F32),
        vm((NSTEP, 2, 8, cols), F32),
        vm((NSTEP, planes, rows, LW), F32),
        vm((2, 2, 8, cols), F32),
        dma((21,)), dma((5 + NSTEP,)),
        dma((NSTEP,)), dma((NSTEP,)), dma((NSTEP,)), dma((NSTEP,)),
        dma((2, NSTEP)), dma((2, NSTEP)), dma((2, NSTEP)), dma((2, NSTEP)),
        dma((3,)), dma((3, NSTEP)), dma((3,)), dma((3, NSTEP)), dma, dma((NSTEP,)),
    ]
    hbm = pl.BlockSpec(memory_space=pl.ANY)
    out_shape = (
        jax.ShapeDtypeStruct((4, planes, rows, cols), F32),
        jax.ShapeDtypeStruct((rows, cols), F32),
        jax.ShapeDtypeStruct((NSTEP, 2 * RB, A), F32),
    )
    results = pl.pallas_call(
        functools.partial(kernel_body, nx),
        out_shape=out_shape,
        in_specs=[hbm] * len(args),
        out_specs=(hbm, hbm, hbm),
        scratch_shapes=scratch,
        compiler_params=pltpu.CompilerParams(
            collective_id=0, has_side_effects=True, vmem_limit_bytes=60 * 1024 * 1024
        ),
    )(*args)
    out_f, out_l, out_s = pl.pallas_call(
        hand_over,
        out_shape=out_shape,
        in_specs=[hbm] * 3,
        out_specs=(hbm, hbm, hbm),
        scratch_shapes=[vm(x.shape, F32) for x in out_shape] + [dma((2, 6))],
        compiler_params=pltpu.CompilerParams(vmem_limit_bytes=60 * 1024 * 1024),
    )(*results)
    spectra = out_s.reshape(NSTEP, modes, B, 2, A).transpose(0, 1, 3, 2, 4).reshape(NSTEP, modes, 2, strike)
    return out_f.reshape(4, 1, planes, rows, cols), out_l, spectra


def solution(mesh):
    return jax.shard_map(
        functools.partial(per_device, mesh.shape["gx"]),
        mesh=mesh,
        in_specs=(
            P(None, "grp", None, "gx", "gz"),
            P("grp", None, "gx", "gz"),
            P("grp", None, "gx", "gz"),
            P("gx", "gz"),
            P("gx", "gz"),
            P("gx", "gz"),
            P(None, ("grp", "gx", "gz"), None),
            P(None, ("grp", "gx", "gz"), None, None),
            P(("grp", "gx", "gz"), None),
        ),
        out_specs=(
            P(None, "grp", None, "gx", "gz"),
            P("gx", "gz"),
            P(None, ("grp", "gx", "gz"), None, None),
        ),
        check_vma=False,
    )
```

```python
import functools
import math

import jax
import jax.numpy as jnp
import numpy as np
from jax import lax
from jax.experimental import pallas as pl
from jax.experimental.pallas import tpu as pltpu
from jax.sharding import PartitionSpec as P

NSTEP = 4
NEWTON = 4
C1 = 9.0 / 8.0
C2 = 1.0 / 24.0
MESH = pl.DeviceIdType.MESH
BF = jnp.bfloat16
F32 = jnp.float32


def split_table(table):
    hi = np.asarray(table, np.float32).astype(jnp.bfloat16)
    lo = (table - hi.astype(np.float64)).astype(jnp.bfloat16)
    return np.stack([hi, lo])


def cis(turns):
    return np.cos(2 * np.pi * turns), np.sin(2 * np.pi * turns)


def x_layers(nx):
    return 4 if nx == 64 else nx


def make_tables(nx, rows, modes, scale):
    A = 2 * nx
    B = rows // 2
    R = modes
    depth = 4 * nx * R
    strike = nx * rows
    eye_r = np.eye(R)
    eye_p = np.eye(2)
    m, b, k, a = np.arange(B), np.arange(B), np.arange(A), np.arange(A)
    c, s = cis(np.outer(m, b) / B)
    inv = np.array([[c, -s], [s, c]])
    fwd = np.array([[c, s], [-s, c]])
    L1 = np.einsum("xybm,rs->xrbsmy", inv, eye_r).reshape(2 * R * B, 2 * R * B)
    L3 = np.einsum("xymb,rs->rmxysb", fwd, eye_r).reshape(2 * R * B, 2 * R * B) * scale
    c, s = cis(np.outer(b, k) / strike)
    twiddle = np.stack([np.tile(c, (R, 1)), np.tile(s, (R, 1))])
    c, s = cis(np.outer(a, k) / A)
    inv = np.array([[c, -s], [s, c]]).reshape(2, 2, nx, 2, A)
    T2 = np.einsum("xyjpk->jxpyk", inv).reshape(4 * nx, 2 * A)
    fwd = np.array([[c, s], [-s, c]]).reshape(2, 2, nx, 2, A)
    TV = np.einsum("xyjpk->jpyxk", fwd).reshape(4 * nx, 2 * A)
    i, z = np.arange(nx), np.arange(A)
    c, s = cis(np.outer(i, z) / A)
    sign = np.where(np.arange(2)[:, None] * z[None, :] % 2 == 1, -1.0, 1.0)
    inv = np.array([[c, -s], [s, c]])
    layers = x_layers(nx)
    TI = np.einsum("xyiz,gz,pn->giypnxz", inv, sign, eye_p).reshape(2, layers, 4 * nx // layers, 4 * A)
    TI = TI.transpose(1, 0, 2, 3).reshape(8 * nx, 4 * A)
    fwd = np.array([[c, s], [-s, c]])
    TF = np.einsum("xyiz,pn->ipxnyz", fwd, eye_p).reshape(4 * nx, 4 * A)
    zz = np.arange(depth).reshape(2 * R, 1, A)
    r = np.arange(R)[None, :, None]
    wi, wf = [], []
    for q in range(2):
        c, s = cis((R * q + r) * zz / depth)
        wi.append(np.stack([c, -s], axis=2).reshape(2 * R, 2 * R, A) * scale)
    for g in range(2):
        for q in range(2):
            c, s = cis((R * q + r) * zz / depth)
            wf.append(np.stack([c, -s], axis=2).reshape(2 * R, 2 * R, A) * sign[g])
    mats = [split_table(x) for x in (L1, T2, TI, TF, TV, L3)]
    return mats, [np.asarray(x, np.float32) for x in (twiddle, np.stack(wi), np.stack(wf))]


def split(x):
    hi = x.astype(BF)
    return hi, (x - hi.astype(F32)).astype(BF)


def dot(x, y, dims):
    return lax.dot_general(x, y, (dims, ((), ())), preferred_element_type=F32)


def table_left(tab, x, dims):
    hi, lo = split(x)
    return dot(tab[0], hi, dims) + (dot(tab[0], lo, dims) + dot(tab[1], hi, dims))


def table_right(x, tab, dims):
    hi, lo = split(x)
    return dot(hi, tab[0], dims) + (dot(lo, tab[0], dims) + dot(hi, tab[1], dims))


def roll(x, shift, axis):
    return pltpu.roll(x, shift % x.shape[axis], axis)


def kernel_body(
    nx, fields_h, buoy_h, stiff_h, szero_h, direct_h, logs_h, kern_h, hist_h, trunc_h,
    L1_h, T2_h, TI_h, TF_h, TV_h, L3_h, TW_h, WI_h, WF_h,
    out_f, out_l, out_s,
    buoy, stiff, szero, direct, LS, KW, H, TRN, L1, T2, TI, TF, TV, L3, TW, WI, WF, WD, NS, FR,
    VP, SP, DP, ACC, GS, RI, OS, PS, RL, PR, SL, US, SF, RF, TR, SG, HV, DV, NP, HS, DS, HO,
    insem, outsem, isend, irecv, fsend, frecv, psend, precv, lsend, lrecv, vsend, vrecv, ssend, srecv, gsend, grecv,
):
    g, j, q = lax.axis_index("grp"), lax.axis_index("gx"), lax.axis_index("gz")
    A = 2 * nx
    RB = TW.shape[1]
    RW, CW = szero.shape
    B = RW // 2
    R = RB // B
    LW = DV.shape[3]
    HC = CW // A
    HIST = H.shape[0]
    side = (2 * g - 1).astype(F32)
    rows_in = pl.ds(8, RW)
    cols_in = pl.ds(LW, CW)

    LX = x_layers(nx)
    ZY = nx // LX
    jx = lax.div(j, ZY)
    if nx == 64:
        turn = (2, 3, 1, 0)
        zs = [lax.rem(lax.div(j, 4) + k, 4) * 4 for k in turn]
        ys = [lax.rem(j + k, 4) for k in turn]
        inner = [z + y for y in ys for z in zs]
    else:
        inner = [j * 0]

    def each_peer(act):
        def one_layer(i, carry):
            x = lax.rem(jx + i + LX // 2, LX) * ZY
            for zy in inner[:-1]:
                act(x + zy)

            @pl.when(i != LX - LX // 2)
            def _():
                act(x + inner[-1])

            return carry

        lax.fori_loop(0, LX, one_layer, 0)

    def layer_of(k):
        return lax.rem(jx + LX - (LX // 2 + k) % LX, LX)

    barrier = pltpu.get_barrier_semaphore()

    def greet(peer):
        pl.semaphore_signal(barrier, inc=1, device_id=(g, peer, q), device_id_type=MESH)
        pl.semaphore_signal(barrier, inc=1, device_id=(1 - g, peer, q), device_id_type=MESH)

    each_peer(greet)
    pl.semaphore_signal(barrier, inc=1, device_id=(1 - g, j, q), device_id_type=MESH)
    pl.semaphore_signal(barrier, inc=1, device_id=(g, j, 1 - q), device_id_type=MESH)

    pairs = [
        (kern_h, KW), (trunc_h, TRN), (hist_h, H), (L1_h, L1), (TW_h, TW), (T2_h, T2),
        (fields_h.at[0], VP.at[:, rows_in, cols_in]), (stiff_h, stiff), (fields_h.at[2], SP.at[:, rows_in, :]),
        (fields_h.at[3], DP.at[:, :, cols_in]), (fields_h.at[1], NS), (TI_h, TI), (WI_h, WI), (szero_h, szero),
        (direct_h, direct), (logs_h, LS), (WF_h, WF), (TF_h, TF), (buoy_h, buoy), (TV_h, TV), (L3_h, L3),
    ]
    loads = [pltpu.make_async_copy(src, dst, insem.at[n]) for n, (src, dst) in enumerate(pairs)]
    for copy in loads:
        copy.start()
    for t in range(ACC.shape[0]):
        ACC[t] = jnp.zeros((2 * RB, A), F32)
    VP[:, pl.ds(0, 8), :] = jnp.zeros((4, 8, CW + 2 * LW), F32)
    VP[:, pl.ds(8 + RW, 8), :] = jnp.zeros((4, 8, CW + 2 * LW), F32)
    VP[:, rows_in, pl.ds(0, LW)] = jnp.zeros((4, RW, LW), F32)
    VP[:, rows_in, pl.ds(LW + CW, LW)] = jnp.zeros((4, RW, LW), F32)
    SP[:, pl.ds(0, 8), :] = jnp.zeros((4, 8, CW), F32)
    SP[:, pl.ds(8 + RW, 8), :] = jnp.zeros((4, 8, CW), F32)
    DP[:, :, pl.ds(0, LW)] = jnp.zeros((4, RW, LW), F32)
    DP[:, :, pl.ds(LW + CW, LW)] = jnp.zeros((4, RW, LW), F32)

    loads[0].wait()
    loads[1].wait()

    def mask_lag(lag, carry):
        for r in range(R):
            pick = pl.ds(r, B, stride=R)
            kept = jnp.where(lag < TRN[pick, :], KW[lag, pick, :], 0.0)
            for c in range(2):
                WD[lag, pl.ds(r * 2 * B + c, B, stride=2), :] = kept
        return carry

    lax.fori_loop(0, HIST, mask_lag, 0)

    def lag_sums(ahead):
        for r in range(R):
            part = pl.ds(r * 2 * B, 2 * B)

            def one_lag(lag, total):
                return total + WD[lag + ahead, part, :] * H[lag, part, :]

            ACC[ahead, part, :] = lax.fori_loop(0, HIST - ahead, one_lag, ACC[ahead, part, :])

    for copy in loads[2:6]:
        copy.wait()
    lag_sums(0)

    def strike_inverse(t):
        x = table_left(L1, ACC[t], ((1,), (0,)))
        xr, xi = x[:RB], x[RB:]
        wide = jnp.concatenate([xr * TW[0] - xi * TW[1], xr * TW[1] + xi * TW[0]], axis=1)
        GS[t] = table_left(T2, wide, ((1,), (1,)))

    strike_inverse(0)
    loads[6].wait()
    pl.semaphore_wait(barrier, 2 * (nx - 1) + 2)

    def remote(src, dst, send, recv, device):
        return pltpu.make_async_remote_copy(
            src_ref=src, dst_ref=dst, send_sem=send, recv_sem=recv, device_id=device, device_id_type=MESH
        )

    def row_copies(kind, land, t, send, recv):
        up = remote(HO.at[kind, 0], land.at[t, 0], send.at[0], recv.at[0, t], (g, lax.rem(j + 1, nx), q))
        down = remote(HO.at[kind, 1], land.at[t, 1], send.at[1], recv.at[1, t], (g, lax.rem(j + nx - 1, nx), q))
        return up, down

    def pack_rows(kind, ref, cols):
        for p in range(4):
            HO[kind, 0, 2 * p : 2 * p + 2, :] = ref[p, pl.ds(RW + 6, 2), cols]
            HO[kind, 1, 2 * p : 2 * p + 2, :] = ref[p, pl.ds(8, 2), cols]

    def v_copies(t):
        up, down = row_copies(0, HV, t, vsend, vrecv)
        right = remote(VP.at[:, rows_in, pl.ds(CW, LW)], DV.at[t], vsend.at[2], vrecv.at[2, t], (g, j, 1 - q))
        left = remote(VP.at[:, rows_in, pl.ds(LW, LW)], DV.at[t], vsend.at[2], vrecv.at[2, t], (g, j, 1 - q))
        across = remote(VP.at[0, rows_in, cols_in], NP.at[t], gsend, grecv.at[t], (1 - g, j, q))
        return up, down, right, left, across

    def s_copies(t):
        up, down = row_copies(1, HS, t, ssend, srecv)
        right = remote(DP.at[:, :, pl.ds(CW, LW)], DS.at[t], ssend.at[2], srecv.at[2, t], (g, j, 1 - q))
        left = remote(DP.at[:, :, pl.ds(LW, LW)], DS.at[t], ssend.at[2], srecv.at[2, t], (g, j, 1 - q))
        return up, down, right, left

    def start_halo(up, down, right, left):
        @pl.when(j < nx - 1)
        def _():
            up.start()

        @pl.when(j > 0)
        def _():
            down.start()

        @pl.when(q == 0)
        def _():
            right.start()

        @pl.when(q == 1)
        def _():
            left.start()

    def sent_halo(up, down, right, left):
        @pl.when(j < nx - 1)
        def _():
            up.wait_send()

        @pl.when(j > 0)
        def _():
            down.wait_send()

        right.wait_send()

    def recv_halo(up, down, right, t, land, depth_land, put_rows, put_cols):
        @pl.when(j > 0)
        def _():
            up.wait_recv()
            put_rows(6, land[t, 0])

        @pl.when(j < nx - 1)
        def _():
            down.wait_recv()
            put_rows(8 + RW, land[t, 1])

        right.wait_recv()

        @pl.when(q == 0)
        def _():
            put_cols(LW + CW, depth_land[t])

        @pl.when(q == 1)
        def _():
            put_cols(0, depth_land[t])

    def v_rows(at, x):
        for p in range(4):
            VP[p, pl.ds(at, 2), cols_in] = x[2 * p : 2 * p + 2]

    def v_cols(at, x):
        VP[:, rows_in, pl.ds(at, LW)] = x

    def s_rows(at, x):
        for p in range(4):
            SP[p, pl.ds(at, 2), :] = x[2 * p : 2 * p + 2]

    def d_cols(at, x):
        DP[:, :, pl.ds(at, LW)] = x

    pack_rows(0, VP, cols_in)
    first = v_copies(0)
    start_halo(*first[:4])

    def out_copies():
        return [
            pltpu.make_async_copy(SP.at[:, rows_in, :], out_f.at[2], outsem.at[0]),
            pltpu.make_async_copy(DP.at[:, :, cols_in], out_f.at[3], outsem.at[1]),
            pltpu.make_async_copy(VP.at[:, rows_in, cols_in], out_f.at[0], outsem.at[2]),
            pltpu.make_async_copy(NS, out_f.at[1], outsem.at[3]),
            pltpu.make_async_copy(LS, out_l, outsem.at[4]),
        ]

    def step_body(t, carry):
        mine = pl.ds((jx * 2 * ZY + g * ZY + lax.rem(j, ZY)) * 4, 4)
        landed = irecv.at[jx, t]

        def send_modes(peer):
            block = GS.at[t, pl.ds(peer * 4, 4)]
            remote(block, RI.at[t, mine], isend.at[t], landed, (1 - g, peer, q)).start()
            remote(block, RI.at[t, mine], isend.at[t], landed, (g, peer, q)).start()

        each_peer(send_modes)
        own = GS.at[t, pl.ds(j * 4, 4)]
        remote(own, RI.at[t, mine], isend.at[t], landed, (1 - g, j, q)).start()
        pltpu.make_async_copy(own, RI.at[t, mine], landed).start()

        @pl.when(t == 0)
        def _():
            first[4].start()

        @pl.when(t == 0)
        def _():
            for copy in loads[7:11]:
                copy.wait()

        up, down, right, left, across = v_copies(t)
        recv_halo(up, down, right, t, HV, DV, v_rows, v_cols)
        sent_halo(up, down, right, left)

        def stress_chunk(i, c):
            r0 = pl.multiple_of(i * 8, 8)
            chunk = pl.ds(r0, 8)
            inner = pl.ds(r0 + 8, 8)
            vs = []
            for p in range(4):
                tall = VP[p, pl.ds(r0, 24), cols_in]
                wide = VP[p, inner, :]
                v = tall[8:16]
                vs.append(v)
                st = stiff[p, chunk, :]
                up1, up2, dn1 = (roll(tall, s, 0)[8:16] for s in (-1, -2, 1))
                SP[p, inner, :] = SP[p, inner, :] + st * (C1 * (up1 - v) - C2 * (up2 - dn1))
                up1, up2, dn1 = (roll(wide, s, 1)[:, LW : LW + CW] for s in (-1, -2, 1))
                DP[p, chunk, cols_in] = DP[p, chunk, cols_in] + st * (C1 * (up1 - v) - C2 * (up2 - dn1))
            for p in range(1, 4):
                far = 0.0 - (vs[p - 2] if p >= 2 else 0.0)
                if p < 3:
                    far = vs[p + 1] + far
                NS[p, chunk, :] = NS[p, chunk, :] + stiff[p, chunk, :] * (C1 * (vs[p] - vs[p - 1]) - C2 * far)
            return c

        lax.fori_loop(0, RW // 8, stress_chunk, 0)
        pack_rows(1, SP, slice(None))
        up, down, right, left = s_copies(t)
        start_halo(up, down, right, left)

        @pl.when(t == NSTEP - 1)
        def _():
            for copy in out_copies()[:2]:
                copy.start()

        across.wait()
        SG[...] = side * (VP[0, rows_in, cols_in] - NP[t])

        @pl.when(t < NSTEP - 1)
        def _():
            lag_sums(t + 1)

        @pl.when(t == 0)
        def _():
            for copy in loads[11:]:
                copy.wait()

        count = 8 * ZY
        for k in range(0, LX, 2):
            xs, spots = [], []
            for n in (k, k + 1):
                layer = layer_of(n)
                spot = pl.ds(pl.multiple_of(layer * count, count), count)
                pltpu.make_async_copy(RI.at[t, spot], RI.at[t, spot], irecv.at[layer, t]).wait()
                xs.append(RI[t, spot, :].T)
                spots.append(spot)
            tab = [jnp.concatenate([TI[n, spot, :] for spot in spots], axis=0) for n in range(2)]
            term = table_right(jnp.concatenate(xs, axis=1), tab, ((1,), (0,)))
            OS[...] = term if k == 0 else OS[...] + term

        def depth_half(half, p, put):
            for hl in range(HC):
                tw = WI[q, half * HC + hl]
                total = None
                for k in range(2 * R):
                    r, c = k // 2, k % 2
                    term = tw[k : k + 1] * OS[r * B : (r + 1) * B, (2 * p + c) * A : (2 * p + c + 1) * A]
                    total = term if total is None else total + term
                put[p * B : (p + 1) * B, hl * A : (hl + 1) * A] = total

        parts = []
        for p in range(2):
            depth_half(1 - q, p, PS.at[t])
            here = pl.ds(p * B, B)
            part = remote(PS.at[t, here], PR.at[t, here], psend.at[p, t], precv.at[p, t], (g, j, 1 - q))
            part.start()
            parts.append(part)
        for p in range(2):
            depth_half(q, p, RL)

        CH = 16

        def friction_chunk(i, c):
            chunk = pl.ds(pl.multiple_of(i * CH, CH), CH)
            guess = SG[chunk, :]
            loading = szero[chunk, :] + (RL[chunk, :] + PR[t, chunk, :]) + guess
            a = direct[chunk, :]
            ls = LS[chunk, :]
            factor = jnp.exp(ls)
            af = a * factor
            v = guess
            for _ in range(NEWTON):
                s = v * factor
                root = jnp.sqrt(1.0 + s * s)
                size = jnp.log(jnp.abs(s) + root)
                misfit = a * jnp.where(s < 0.0, -size, size) + v - loading
                v = v - misfit / (af / root + 1.0)
            SL[t, q, chunk, :] = v
            TR[chunk, :] = side * (loading - v)
            LS[chunk, :] = 0.75 * ls - 0.2 * jnp.log(1.0 + v * v) + 0.1
            return c

        slips = []
        for p in range(2):
            parts[p].wait_recv()
            lax.fori_loop(p * B // CH, (p + 1) * B // CH, friction_chunk, 0)
            here = pl.ds(p * B, B)
            slip = remote(SL.at[t, q, here], SL.at[t, q, here], lsend.at[p, t], lrecv.at[p, t], (g, j, 1 - q))
            slip.start()
            slips.append(slip)

        def depth_terms(half, p, add):
            acc = None
            for hl in range(HC):
                tw = WF[2 * g + q, half * HC + hl]
                cells = SL[t, half, p * B : (p + 1) * B, hl * A : (hl + 1) * A]
                terms = [tw[k : k + 1] * cells for k in range(2 * R)]
                acc = terms if acc is None else [x + y for x, y in zip(acc, terms)]
            for k in range(2 * R):
                r, c = k // 2, k % 2
                at = (slice(r * B, (r + 1) * B), slice((2 * p + c) * A, (2 * p + c + 1) * A))
                US[at] = US[at] + acc[k] if add else acc[k]

        for p in range(2):
            depth_terms(q, p, False)
        for p in range(2):
            here = pl.ds(p * B, B)
            land = SL.at[t, 1 - q, here]
            pltpu.make_async_copy(land, land, lrecv.at[p, t]).wait()
            depth_terms(1 - q, p, True)
        SF[t] = table_left(TF, US[...], ((1,), (1,)))
        spot = pl.ds(j * 4, 4)
        arrived = frecv.at[jx, t]

        def send_slip(peer):
            remote(SF.at[t, pl.ds(peer * 4, 4)], RF.at[t, spot], fsend.at[t], arrived, (g, peer, q)).start()

        each_peer(send_slip)
        pltpu.make_async_copy(SF.at[t, spot], RF.at[t, spot], arrived).start()

        recv_halo(up, down, right, t, HS, DS, s_rows, d_cols)
        sent_halo(up, down, right, left)
        NS[0] = TR[...]

        def velocity_chunk(i, c):
            r0 = pl.multiple_of(i * 8, 8)
            chunk = pl.ds(r0, 8)
            inner = pl.ds(r0 + 8, 8)
            n0, n1, n2, n3 = (NS[p, chunk, :] for p in range(4))
            plane_terms = [
                C1 * (n1 - n0) - C2 * n2,
                C1 * (n2 - n1) - C2 * (n3 - n0),
                C1 * (n3 - n2) + C2 * n1,
                C2 * n2 - C1 * n3,
            ]
            for p in range(4):
                tall = SP[p, pl.ds(r0, 24), :]
                wide = DP[p, chunk, :]
                dn1, dn2, up1 = (roll(tall, s, 0)[8:16] for s in (1, 2, -1))
                total = plane_terms[p] + (C1 * (tall[8:16] - dn1) - C2 * (up1 - dn2))
                dn1, dn2, up1 = (roll(wide, s, 1)[:, LW : LW + CW] for s in (1, 2, -1))
                total = total + (C1 * (wide[:, LW : LW + CW] - dn1) - C2 * (up1 - dn2))
                VP[p, inner, cols_in] = VP[p, inner, cols_in] + buoy[p, chunk, :] * total
            return c

        lax.fori_loop(0, RW // 8, velocity_chunk, 0)

        @pl.when(t < NSTEP - 1)
        def _():
            pack_rows(0, VP, cols_in)
            later = v_copies(t + 1)
            start_halo(*later[:4])
            later[4].start()

        @pl.when(t == NSTEP - 1)
        def _():
            for copy in out_copies()[2:]:
                copy.start()

        for p in range(2):
            parts[p].wait_send()
            slips[p].wait_send()
        count = 4 * ZY
        xs, spots = [], []
        for k in range(0, LX, 2):
            pair = []
            for n in (k, k + 1):
                layer = layer_of(n)
                spot = pl.ds(pl.multiple_of(layer * count, count), count)
                pltpu.make_async_copy(RF.at[t, spot], RF.at[t, spot], frecv.at[layer, t]).wait()
                pair.append(RF[t, spot, :])
                spots.append(spot)
            xs.append(jnp.concatenate(pair, axis=0).T)
        tab = [jnp.concatenate([TV[n, spot, :] for spot in spots], axis=0) for n in range(2)]
        x = table_right(jnp.concatenate(xs, axis=1), tab, ((1,), (0,)))
        xr, xi = x[:, :A], x[:, A:]
        tall = jnp.concatenate([xr * TW[0] + xi * TW[1], xi * TW[0] - xr * TW[1]], axis=0)
        fresh = table_left(L3, tall, ((1,), (0,)))
        FR[t] = fresh
        pltpu.make_async_copy(FR.at[t], out_s.at[t], outsem.at[5 + t]).start()

        @pl.when(t < NSTEP - 1)
        def _():
            for d in range(NSTEP - 1):
                ACC[t + 1 + d] = ACC[t + 1 + d] + WD[d] * fresh
            strike_inverse(t + 1)

        return carry

    lax.fori_loop(0, NSTEP, step_body, 0)

    for copy in out_copies():
        copy.wait()
    for t in range(NSTEP):
        pltpu.make_async_copy(FR.at[t], out_s.at[t], outsem.at[5 + t]).wait()
        left = RI.at[t, pl.ds(0, (2 * nx - 1) * 4)]
        pltpu.make_async_copy(left, left, isend.at[t]).wait()
        left = RF.at[t, pl.ds(0, (nx - 1) * 4)]
        pltpu.make_async_copy(left, left, fsend.at[t]).wait()


def hand_over(f_in, l_in, s_in, f_out, l_out, s_out, f, l, s, sem):
    pieces = [(f_in.at[n], f.at[n], f_out.at[n]) for n in range(f.shape[0])]
    pieces += [(s_in, s, s_out), (l_in, l, l_out)]
    for n, (src, mid, _) in enumerate(pieces):
        pltpu.make_async_copy(src, mid, sem.at[0, n]).start()
    for n, (src, mid, dst) in enumerate(pieces):
        pltpu.make_async_copy(src, mid, sem.at[0, n]).wait()
        pltpu.make_async_copy(mid, dst, sem.at[1, n]).start()
    for n, (_, mid, dst) in enumerate(pieces):
        pltpu.make_async_copy(mid, dst, sem.at[1, n]).wait()


def per_device(nx, fields, buoyancy, stiffness, stress_zero, direct_effect, log_state, kernel, history, truncation):
    planes, rows, cols = fields.shape[2:]
    hist, modes, _, strike = history.shape
    A = 2 * nx
    B = rows // 2
    RB = modes * B
    depth = 2 * cols
    scale = 1.0 / math.sqrt(strike * depth)
    mats, vecs = make_tables(nx, rows, modes, scale)
    kernel = kernel.reshape(hist, modes, B, A).transpose(0, 2, 1, 3).reshape(hist, RB, A)
    history = history.reshape(hist, modes, 2, B, A).transpose(0, 1, 3, 2, 4).reshape(hist, 2 * RB, A)
    truncation = truncation.reshape(modes, B, A).transpose(1, 0, 2).reshape(RB, A)
    LW = min(128, cols)
    vm = pltpu.VMEM
    dma = pltpu.SemaphoreType.DMA
    args = [
        fields.reshape(4, planes, rows, cols), buoyancy[0], stiffness[0], stress_zero, direct_effect, log_state,
        kernel, history, truncation, *[jnp.asarray(x) for x in mats], *[jnp.asarray(x) for x in vecs],
    ]
    scratch = [vm(x.shape, x.dtype) for x in args[1:]] + [
        vm((hist, 2 * RB, A), F32),
        vm((planes, rows, cols), F32),
        vm((NSTEP, 2 * RB, A), F32),
        vm((planes, rows + 16, cols + 2 * LW), F32),
        vm((planes, rows + 16, cols), F32),
        vm((planes, rows, cols + 2 * LW), F32),
        vm((2 * NSTEP - 1, 2 * RB, A), F32),
        vm((NSTEP, 4 * nx, RB), F32),
        vm((NSTEP, 8 * nx, RB), F32),
        vm((RB, 4 * A), F32),
        vm((NSTEP, rows, cols), F32),
        vm((rows, cols), F32),
        vm((NSTEP, rows, cols), F32),
        vm((NSTEP, 2, rows, cols), F32),
        vm((RB, 4 * A), F32),
        vm((NSTEP, 4 * nx, RB), F32),
        vm((NSTEP, 4 * nx, RB), F32),
        vm((rows, cols), F32),
        vm((rows, cols), F32),
        vm((NSTEP, 2, 8, cols), F32),
        vm((NSTEP, planes, rows, LW), F32),
        vm((NSTEP, rows, cols), F32),
        vm((NSTEP, 2, 8, cols), F32),
        vm((NSTEP, planes, rows, LW), F32),
        vm((2, 2, 8, cols), F32),
        dma((21,)), dma((5 + NSTEP,)),
        dma((NSTEP,)), dma((x_layers(nx), NSTEP)), dma((NSTEP,)), dma((x_layers(nx), NSTEP)),
        dma((2, NSTEP)), dma((2, NSTEP)), dma((2, NSTEP)), dma((2, NSTEP)),
        dma((3,)), dma((3, NSTEP)), dma((3,)), dma((3, NSTEP)), dma, dma((NSTEP,)),
    ]
    hbm = pl.BlockSpec(memory_space=pl.ANY)
    out_shape = (
        jax.ShapeDtypeStruct((4, planes, rows, cols), F32),
        jax.ShapeDtypeStruct((rows, cols), F32),
        jax.ShapeDtypeStruct((NSTEP, 2 * RB, A), F32),
    )
    results = pl.pallas_call(
        functools.partial(kernel_body, nx),
        out_shape=out_shape,
        in_specs=[hbm] * len(args),
        out_specs=(hbm, hbm, hbm),
        scratch_shapes=scratch,
        compiler_params=pltpu.CompilerParams(
            collective_id=0, has_side_effects=True, vmem_limit_bytes=60 * 1024 * 1024
        ),
    )(*args)
    out_f, out_l, out_s = pl.pallas_call(
        hand_over,
        out_shape=out_shape,
        in_specs=[hbm] * 3,
        out_specs=(hbm, hbm, hbm),
        scratch_shapes=[vm(x.shape, F32) for x in out_shape] + [dma((2, 6))],
        compiler_params=pltpu.CompilerParams(vmem_limit_bytes=60 * 1024 * 1024),
    )(*results)
    spectra = out_s.reshape(NSTEP, modes, B, 2, A).transpose(0, 1, 3, 2, 4).reshape(NSTEP, modes, 2, strike)
    return out_f.reshape(4, 1, planes, rows, cols), out_l, spectra


def solution(mesh):
    return jax.shard_map(
        functools.partial(per_device, mesh.shape["gx"]),
        mesh=mesh,
        in_specs=(
            P(None, "grp", None, "gx", "gz"),
            P("grp", None, "gx", "gz"),
            P("grp", None, "gx", "gz"),
            P("gx", "gz"),
            P("gx", "gz"),
            P("gx", "gz"),
            P(None, ("grp", "gx", "gz"), None),
            P(None, ("grp", "gx", "gz"), None, None),
            P(("grp", "gx", "gz"), None),
        ),
        out_specs=(
            P(None, "grp", None, "gx", "gz"),
            P("gx", "gz"),
            P(None, ("grp", "gx", "gz"), None, None),
        ),
        check_vma=False,
    )
```

```python
import functools
import math

import jax
import jax.numpy as jnp
import numpy as np
from jax import lax
from jax.experimental import pallas as pl
from jax.experimental.pallas import tpu as pltpu
from jax.sharding import PartitionSpec as P

NSTEP = 4
NEWTON = 4
C1 = 9.0 / 8.0
C2 = 1.0 / 24.0
MESH = pl.DeviceIdType.MESH
BF = jnp.bfloat16
F32 = jnp.float32


def split_table(table):
    hi = np.asarray(table, np.float32).astype(jnp.bfloat16)
    lo = (table - hi.astype(np.float64)).astype(jnp.bfloat16)
    return np.stack([hi, lo])


def cis(turns):
    return np.cos(2 * np.pi * turns), np.sin(2 * np.pi * turns)


def x_layers(nx):
    return 4 if nx == 64 else nx


def layer_order(nx):
    places = np.arange(nx)
    return places.reshape(4, 4, 4).transpose(1, 0, 2).reshape(nx) if nx == 64 else places


def make_tables(nx, rows, modes, scale):
    A = 2 * nx
    B = rows // 2
    R = modes
    depth = 4 * nx * R
    strike = nx * rows
    eye_r = np.eye(R)
    eye_p = np.eye(2)
    m, b, k, a = np.arange(B), np.arange(B), np.arange(A), np.arange(A)
    c, s = cis(np.outer(m, b) / B)
    inv = np.array([[c, -s], [s, c]])
    fwd = np.array([[c, s], [-s, c]])
    L1 = np.einsum("xybm,rs->xrbsmy", inv, eye_r).reshape(2 * R * B, 2 * R * B)
    L3 = np.einsum("xymb,rs->rmxysb", fwd, eye_r).reshape(2 * R * B, 2 * R * B) * scale
    c, s = cis(np.outer(b, k) / strike)
    twiddle = np.stack([np.tile(c, (R, 1)), np.tile(s, (R, 1))])
    c, s = cis(np.outer(a, k) / A)
    inv = np.array([[c, -s], [s, c]]).reshape(2, 2, nx, 2, A)
    T2 = np.einsum("xyjpk->jxpyk", inv).reshape(4 * nx, 2 * A)
    fwd = np.array([[c, s], [-s, c]]).reshape(2, 2, nx, 2, A)
    TV = np.einsum("xyjpk->jpyxk", fwd).reshape(4 * nx, 2 * A)
    i, z = np.arange(nx), np.arange(A)
    c, s = cis(np.outer(i, z) / A)
    sign = np.where(np.arange(2)[:, None] * z[None, :] % 2 == 1, -1.0, 1.0)
    inv = np.array([[c, -s], [s, c]])
    layers = x_layers(nx)
    TI = np.einsum("xyiz,gz,pn->giypnxz", inv, sign, eye_p).reshape(2, nx, 4, 4 * A)
    by_layer = layer_order(nx)
    TI = TI[:, by_layer].reshape(2, layers, 4 * nx // layers, 4 * A).transpose(1, 0, 2, 3).reshape(8 * nx, 4 * A)
    TV = TV.reshape(nx, 4, 2 * A)[by_layer].reshape(4 * nx, 2 * A)
    fwd = np.array([[c, s], [-s, c]])
    TF = np.einsum("xyiz,pn->ipxnyz", fwd, eye_p).reshape(4 * nx, 4 * A)
    zz = np.arange(depth).reshape(2 * R, 1, A)
    r = np.arange(R)[None, :, None]
    wi, wf = [], []
    for q in range(2):
        c, s = cis((R * q + r) * zz / depth)
        wi.append(np.stack([c, -s], axis=2).reshape(2 * R, 2 * R, A) * scale)
    for g in range(2):
        for q in range(2):
            c, s = cis((R * q + r) * zz / depth)
            wf.append(np.stack([c, -s], axis=2).reshape(2 * R, 2 * R, A) * sign[g])
    mats = [split_table(x) for x in (L1, T2, TI, TF, TV, L3)]
    return mats, [np.asarray(x, np.float32) for x in (twiddle, np.stack(wi), np.stack(wf))]


def split(x):
    hi = x.astype(BF)
    return hi, (x - hi.astype(F32)).astype(BF)


def dot(x, y, dims):
    return lax.dot_general(x, y, (dims, ((), ())), preferred_element_type=F32)


def table_left(tab, x, dims):
    hi, lo = split(x)
    return dot(tab[0], hi, dims) + (dot(tab[0], lo, dims) + dot(tab[1], hi, dims))


def table_right(x, tab, dims):
    hi, lo = split(x)
    return dot(hi, tab[0], dims) + (dot(lo, tab[0], dims) + dot(hi, tab[1], dims))


def roll(x, shift, axis):
    return pltpu.roll(x, shift % x.shape[axis], axis)


def kernel_body(
    nx, fields_h, buoy_h, stiff_h, szero_h, direct_h, logs_h, kern_h, hist_h, trunc_h,
    L1_h, T2_h, TI_h, TF_h, TV_h, L3_h, TW_h, WI_h, WF_h,
    out_f, out_l, out_s,
    buoy, stiff, szero, direct, LS, KW, H, TRN, L1, T2, TI, TF, TV, L3, TW, WI, WF, WD, NS, FR,
    VP, SP, DP, ACC, GS, RI, OS, PS, RL, PR, SL, US, SF, RF, TR, SG, HV, DV, NP, HS, DS, HO,
    insem, outsem, isend, irecv, fsend, frecv, psend, precv, lsend, lrecv, vsend, vrecv, ssend, srecv, gsend, grecv,
):
    g, j, q = lax.axis_index("grp"), lax.axis_index("gx"), lax.axis_index("gz")
    A = 2 * nx
    RB = TW.shape[1]
    RW, CW = szero.shape
    B = RW // 2
    R = RB // B
    LW = DV.shape[3]
    HC = CW // A
    HIST = H.shape[0]
    side = (2 * g - 1).astype(F32)
    rows_in = pl.ds(8, RW)
    cols_in = pl.ds(LW, CW)

    LX = x_layers(nx)
    ZY = nx // LX
    if nx == 64:
        turn = (2, 3, 1, 0)
        jz, step = lax.rem(lax.div(j, 4), 4), 4
        jxy = lax.div(j, 16) * 4 + lax.rem(j, 4)
        xs = [lax.rem(lax.div(j, 16) + k, 4) * 16 for k in turn]
        ys = [lax.rem(j + k, 4) for k in turn]
        inner = [x + y for x in xs for y in ys]
    else:
        jz, step, jxy, inner = j, 1, j * 0, [j * 0]

    def each_peer(act):
        def one_layer(i, carry):
            z = lax.rem(jz + i + LX // 2, LX) * step
            for xy in inner[:-1]:
                act(z + xy)

            @pl.when(i != LX - LX // 2)
            def _():
                act(z + inner[-1])

            return carry

        lax.fori_loop(0, LX, one_layer, 0)

    def layer_of(k):
        return lax.rem(jz + LX - (LX // 2 + k) % LX, LX)

    barrier = pltpu.get_barrier_semaphore()

    def greet(peer):
        pl.semaphore_signal(barrier, inc=1, device_id=(g, peer, q), device_id_type=MESH)
        pl.semaphore_signal(barrier, inc=1, device_id=(1 - g, peer, q), device_id_type=MESH)

    each_peer(greet)
    pl.semaphore_signal(barrier, inc=1, device_id=(1 - g, j, q), device_id_type=MESH)
    pl.semaphore_signal(barrier, inc=1, device_id=(g, j, 1 - q), device_id_type=MESH)

    pairs = [
        (kern_h, KW), (trunc_h, TRN), (hist_h, H), (L1_h, L1), (TW_h, TW), (T2_h, T2),
        (fields_h.at[0], VP.at[:, rows_in, cols_in]), (stiff_h, stiff), (fields_h.at[2], SP.at[:, rows_in, :]),
        (fields_h.at[3], DP.at[:, :, cols_in]), (fields_h.at[1], NS), (TI_h, TI), (WI_h, WI), (szero_h, szero),
        (direct_h, direct), (logs_h, LS), (WF_h, WF), (TF_h, TF), (buoy_h, buoy), (TV_h, TV), (L3_h, L3),
    ]
    loads = [pltpu.make_async_copy(src, dst, insem.at[n]) for n, (src, dst) in enumerate(pairs)]
    for copy in loads:
        copy.start()
    for t in range(ACC.shape[0]):
        ACC[t] = jnp.zeros((2 * RB, A), F32)
    VP[:, pl.ds(0, 8), :] = jnp.zeros((4, 8, CW + 2 * LW), F32)
    VP[:, pl.ds(8 + RW, 8), :] = jnp.zeros((4, 8, CW + 2 * LW), F32)
    VP[:, rows_in, pl.ds(0, LW)] = jnp.zeros((4, RW, LW), F32)
    VP[:, rows_in, pl.ds(LW + CW, LW)] = jnp.zeros((4, RW, LW), F32)
    SP[:, pl.ds(0, 8), :] = jnp.zeros((4, 8, CW), F32)
    SP[:, pl.ds(8 + RW, 8), :] = jnp.zeros((4, 8, CW), F32)
    DP[:, :, pl.ds(0, LW)] = jnp.zeros((4, RW, LW), F32)
    DP[:, :, pl.ds(LW + CW, LW)] = jnp.zeros((4, RW, LW), F32)

    loads[0].wait()
    loads[1].wait()

    def mask_lag(lag, carry):
        for r in range(R):
            pick = pl.ds(r, B, stride=R)
            kept = jnp.where(lag < TRN[pick, :], KW[lag, pick, :], 0.0)
            for c in range(2):
                WD[lag, pl.ds(r * 2 * B + c, B, stride=2), :] = kept
        return carry

    lax.fori_loop(0, HIST, mask_lag, 0)

    def lag_sums(ahead):
        for r in range(R):
            part = pl.ds(r * 2 * B, 2 * B)

            def one_lag(lag, total):
                return total + WD[lag + ahead, part, :] * H[lag, part, :]

            ACC[ahead, part, :] = lax.fori_loop(0, HIST - ahead, one_lag, ACC[ahead, part, :])

    for copy in loads[2:6]:
        copy.wait()
    lag_sums(0)

    def strike_inverse(t):
        x = table_left(L1, ACC[t], ((1,), (0,)))
        xr, xi = x[:RB], x[RB:]
        wide = jnp.concatenate([xr * TW[0] - xi * TW[1], xr * TW[1] + xi * TW[0]], axis=1)
        GS[t] = table_left(T2, wide, ((1,), (1,)))

    strike_inverse(0)
    loads[6].wait()
    pl.semaphore_wait(barrier, 2 * (nx - 1) + 2)

    def remote(src, dst, send, recv, device):
        return pltpu.make_async_remote_copy(
            src_ref=src, dst_ref=dst, send_sem=send, recv_sem=recv, device_id=device, device_id_type=MESH
        )

    def row_copies(kind, land, t, send, recv):
        up = remote(HO.at[kind, 0], land.at[t, 0], send.at[0], recv.at[0, t], (g, lax.rem(j + 1, nx), q))
        down = remote(HO.at[kind, 1], land.at[t, 1], send.at[1], recv.at[1, t], (g, lax.rem(j + nx - 1, nx), q))
        return up, down

    def pack_rows(kind, ref, cols):
        for p in range(4):
            HO[kind, 0, 2 * p : 2 * p + 2, :] = ref[p, pl.ds(RW + 6, 2), cols]
            HO[kind, 1, 2 * p : 2 * p + 2, :] = ref[p, pl.ds(8, 2), cols]

    def v_copies(t):
        up, down = row_copies(0, HV, t, vsend, vrecv)
        right = remote(VP.at[:, rows_in, pl.ds(CW, LW)], DV.at[t], vsend.at[2], vrecv.at[2, t], (g, j, 1 - q))
        left = remote(VP.at[:, rows_in, pl.ds(LW, LW)], DV.at[t], vsend.at[2], vrecv.at[2, t], (g, j, 1 - q))
        across = remote(VP.at[0, rows_in, cols_in], NP.at[t], gsend, grecv.at[t], (1 - g, j, q))
        return up, down, right, left, across

    def s_copies(t):
        up, down = row_copies(1, HS, t, ssend, srecv)
        right = remote(DP.at[:, :, pl.ds(CW, LW)], DS.at[t], ssend.at[2], srecv.at[2, t], (g, j, 1 - q))
        left = remote(DP.at[:, :, pl.ds(LW, LW)], DS.at[t], ssend.at[2], srecv.at[2, t], (g, j, 1 - q))
        return up, down, right, left

    def start_halo(up, down, right, left):
        @pl.when(j < nx - 1)
        def _():
            up.start()

        @pl.when(j > 0)
        def _():
            down.start()

        @pl.when(q == 0)
        def _():
            right.start()

        @pl.when(q == 1)
        def _():
            left.start()

    def sent_halo(up, down, right, left):
        @pl.when(j < nx - 1)
        def _():
            up.wait_send()

        @pl.when(j > 0)
        def _():
            down.wait_send()

        right.wait_send()

    def recv_halo(up, down, right, t, land, depth_land, put_rows, put_cols):
        @pl.when(j > 0)
        def _():
            up.wait_recv()
            put_rows(6, land[t, 0])

        @pl.when(j < nx - 1)
        def _():
            down.wait_recv()
            put_rows(8 + RW, land[t, 1])

        right.wait_recv()

        @pl.when(q == 0)
        def _():
            put_cols(LW + CW, depth_land[t])

        @pl.when(q == 1)
        def _():
            put_cols(0, depth_land[t])

    def v_rows(at, x):
        for p in range(4):
            VP[p, pl.ds(at, 2), cols_in] = x[2 * p : 2 * p + 2]

    def v_cols(at, x):
        VP[:, rows_in, pl.ds(at, LW)] = x

    def s_rows(at, x):
        for p in range(4):
            SP[p, pl.ds(at, 2), :] = x[2 * p : 2 * p + 2]

    def d_cols(at, x):
        DP[:, :, pl.ds(at, LW)] = x

    pack_rows(0, VP, cols_in)
    first = v_copies(0)
    start_halo(*first[:4])

    def out_copies():
        return [
            pltpu.make_async_copy(SP.at[:, rows_in, :], out_f.at[2], outsem.at[0]),
            pltpu.make_async_copy(DP.at[:, :, cols_in], out_f.at[3], outsem.at[1]),
            pltpu.make_async_copy(VP.at[:, rows_in, cols_in], out_f.at[0], outsem.at[2]),
            pltpu.make_async_copy(NS, out_f.at[1], outsem.at[3]),
            pltpu.make_async_copy(LS, out_l, outsem.at[4]),
        ]

    def step_body(t, carry):
        mine = pl.ds((jz * 2 * ZY + g * ZY + jxy) * 4, 4)
        landed = irecv.at[jz, t]

        def send_modes(peer):
            block = GS.at[t, pl.ds(peer * 4, 4)]
            remote(block, RI.at[t, mine], isend.at[t], landed, (1 - g, peer, q)).start()
            remote(block, RI.at[t, mine], isend.at[t], landed, (g, peer, q)).start()

        each_peer(send_modes)
        own = GS.at[t, pl.ds(j * 4, 4)]
        remote(own, RI.at[t, mine], isend.at[t], landed, (1 - g, j, q)).start()
        pltpu.make_async_copy(own, RI.at[t, mine], landed).start()

        @pl.when(t == 0)
        def _():
            first[4].start()

        @pl.when(t == 0)
        def _():
            for copy in loads[7:11]:
                copy.wait()

        up, down, right, left, across = v_copies(t)
        recv_halo(up, down, right, t, HV, DV, v_rows, v_cols)
        sent_halo(up, down, right, left)

        def stress_chunk(i, c):
            r0 = pl.multiple_of(i * 8, 8)
            chunk = pl.ds(r0, 8)
            inner = pl.ds(r0 + 8, 8)
            vs = []
            for p in range(4):
                tall = VP[p, pl.ds(r0, 24), cols_in]
                wide = VP[p, inner, :]
                v = tall[8:16]
                vs.append(v)
                st = stiff[p, chunk, :]
                up1, up2, dn1 = (roll(tall, s, 0)[8:16] for s in (-1, -2, 1))
                SP[p, inner, :] = SP[p, inner, :] + st * (C1 * (up1 - v) - C2 * (up2 - dn1))
                up1, up2, dn1 = (roll(wide, s, 1)[:, LW : LW + CW] for s in (-1, -2, 1))
                DP[p, chunk, cols_in] = DP[p, chunk, cols_in] + st * (C1 * (up1 - v) - C2 * (up2 - dn1))
            for p in range(1, 4):
                far = 0.0 - (vs[p - 2] if p >= 2 else 0.0)
                if p < 3:
                    far = vs[p + 1] + far
                NS[p, chunk, :] = NS[p, chunk, :] + stiff[p, chunk, :] * (C1 * (vs[p] - vs[p - 1]) - C2 * far)
            return c

        lax.fori_loop(0, RW // 8, stress_chunk, 0)
        pack_rows(1, SP, slice(None))
        up, down, right, left = s_copies(t)
        start_halo(up, down, right, left)

        @pl.when(t == NSTEP - 1)
        def _():
            for copy in out_copies()[:2]:
                copy.start()

        across.wait()
        SG[...] = side * (VP[0, rows_in, cols_in] - NP[t])

        @pl.when(t < NSTEP - 1)
        def _():
            lag_sums(t + 1)

        @pl.when(t == 0)
        def _():
            for copy in loads[11:]:
                copy.wait()

        count = 8 * ZY
        for k in range(0, LX, 2):
            xs, spots = [], []
            for n in (k, k + 1):
                layer = layer_of(n)
                spot = pl.ds(pl.multiple_of(layer * count, count), count)
                pltpu.make_async_copy(RI.at[t, spot], RI.at[t, spot], irecv.at[layer, t]).wait()
                xs.append(RI[t, spot, :].T)
                spots.append(spot)
            tab = [jnp.concatenate([TI[n, spot, :] for spot in spots], axis=0) for n in range(2)]
            term = table_right(jnp.concatenate(xs, axis=1), tab, ((1,), (0,)))
            OS[...] = term if k == 0 else OS[...] + term

        def depth_half(half, p, put):
            for hl in range(HC):
                tw = WI[q, half * HC + hl]
                total = None
                for k in range(2 * R):
                    r, c = k // 2, k % 2
                    term = tw[k : k + 1] * OS[r * B : (r + 1) * B, (2 * p + c) * A : (2 * p + c + 1) * A]
                    total = term if total is None else total + term
                put[p * B : (p + 1) * B, hl * A : (hl + 1) * A] = total

        parts = []
        for p in range(2):
            depth_half(1 - q, p, PS.at[t])
            here = pl.ds(p * B, B)
            part = remote(PS.at[t, here], PR.at[t, here], psend.at[p, t], precv.at[p, t], (g, j, 1 - q))
            part.start()
            parts.append(part)
        for p in range(2):
            depth_half(q, p, RL)

        CH = 16

        def friction_chunk(i, c):
            chunk = pl.ds(pl.multiple_of(i * CH, CH), CH)
            guess = SG[chunk, :]
            loading = szero[chunk, :] + (RL[chunk, :] + PR[t, chunk, :]) + guess
            a = direct[chunk, :]
            ls = LS[chunk, :]
            factor = jnp.exp(ls)
            af = a * factor
            v = guess
            for _ in range(NEWTON):
                s = v * factor
                root = jnp.sqrt(1.0 + s * s)
                size = jnp.log(jnp.abs(s) + root)
                misfit = a * jnp.where(s < 0.0, -size, size) + v - loading
                v = v - misfit / (af / root + 1.0)
            SL[t, q, chunk, :] = v
            TR[chunk, :] = side * (loading - v)
            LS[chunk, :] = 0.75 * ls - 0.2 * jnp.log(1.0 + v * v) + 0.1
            return c

        slips = []
        for p in range(2):
            parts[p].wait_recv()
            lax.fori_loop(p * B // CH, (p + 1) * B // CH, friction_chunk, 0)
            here = pl.ds(p * B, B)
            slip = remote(SL.at[t, q, here], SL.at[t, q, here], lsend.at[p, t], lrecv.at[p, t], (g, j, 1 - q))
            slip.start()
            slips.append(slip)

        def depth_terms(half, p, add):
            acc = None
            for hl in range(HC):
                tw = WF[2 * g + q, half * HC + hl]
                cells = SL[t, half, p * B : (p + 1) * B, hl * A : (hl + 1) * A]
                terms = [tw[k : k + 1] * cells for k in range(2 * R)]
                acc = terms if acc is None else [x + y for x, y in zip(acc, terms)]
            for k in range(2 * R):
                r, c = k // 2, k % 2
                at = (slice(r * B, (r + 1) * B), slice((2 * p + c) * A, (2 * p + c + 1) * A))
                US[at] = US[at] + acc[k] if add else acc[k]

        for p in range(2):
            depth_terms(q, p, False)
        for p in range(2):
            here = pl.ds(p * B, B)
            land = SL.at[t, 1 - q, here]
            pltpu.make_async_copy(land, land, lrecv.at[p, t]).wait()
            depth_terms(1 - q, p, True)
        SF[t] = table_left(TF, US[...], ((1,), (1,)))
        spot = pl.ds((jz * ZY + jxy) * 4, 4)
        block_here = pl.ds(j * 4, 4)
        arrived = frecv.at[jz, t]

        def send_slip(peer):
            remote(SF.at[t, pl.ds(peer * 4, 4)], RF.at[t, spot], fsend.at[t], arrived, (g, peer, q)).start()

        each_peer(send_slip)
        pltpu.make_async_copy(SF.at[t, block_here], RF.at[t, spot], arrived).start()

        recv_halo(up, down, right, t, HS, DS, s_rows, d_cols)
        sent_halo(up, down, right, left)
        NS[0] = TR[...]

        def velocity_chunk(i, c):
            r0 = pl.multiple_of(i * 8, 8)
            chunk = pl.ds(r0, 8)
            inner = pl.ds(r0 + 8, 8)
            n0, n1, n2, n3 = (NS[p, chunk, :] for p in range(4))
            plane_terms = [
                C1 * (n1 - n0) - C2 * n2,
                C1 * (n2 - n1) - C2 * (n3 - n0),
                C1 * (n3 - n2) + C2 * n1,
                C2 * n2 - C1 * n3,
            ]
            for p in range(4):
                tall = SP[p, pl.ds(r0, 24), :]
                wide = DP[p, chunk, :]
                dn1, dn2, up1 = (roll(tall, s, 0)[8:16] for s in (1, 2, -1))
                total = plane_terms[p] + (C1 * (tall[8:16] - dn1) - C2 * (up1 - dn2))
                dn1, dn2, up1 = (roll(wide, s, 1)[:, LW : LW + CW] for s in (1, 2, -1))
                total = total + (C1 * (wide[:, LW : LW + CW] - dn1) - C2 * (up1 - dn2))
                VP[p, inner, cols_in] = VP[p, inner, cols_in] + buoy[p, chunk, :] * total
            return c

        lax.fori_loop(0, RW // 8, velocity_chunk, 0)

        @pl.when(t < NSTEP - 1)
        def _():
            pack_rows(0, VP, cols_in)
            later = v_copies(t + 1)
            start_halo(*later[:4])
            later[4].start()

        @pl.when(t == NSTEP - 1)
        def _():
            for copy in out_copies()[2:]:
                copy.start()

        for p in range(2):
            parts[p].wait_send()
            slips[p].wait_send()
        count = 4 * ZY
        xs, spots = [], []
        for k in range(0, LX, 2):
            pair = []
            for n in (k, k + 1):
                layer = layer_of(n)
                spot = pl.ds(pl.multiple_of(layer * count, count), count)
                pltpu.make_async_copy(RF.at[t, spot], RF.at[t, spot], frecv.at[layer, t]).wait()
                pair.append(RF[t, spot, :])
                spots.append(spot)
            xs.append(jnp.concatenate(pair, axis=0).T)
        tab = [jnp.concatenate([TV[n, spot, :] for spot in spots], axis=0) for n in range(2)]
        x = table_right(jnp.concatenate(xs, axis=1), tab, ((1,), (0,)))
        xr, xi = x[:, :A], x[:, A:]
        tall = jnp.concatenate([xr * TW[0] + xi * TW[1], xi * TW[0] - xr * TW[1]], axis=0)
        fresh = table_left(L3, tall, ((1,), (0,)))
        FR[t] = fresh
        pltpu.make_async_copy(FR.at[t], out_s.at[t], outsem.at[5 + t]).start()

        @pl.when(t < NSTEP - 1)
        def _():
            for d in range(NSTEP - 1):
                ACC[t + 1 + d] = ACC[t + 1 + d] + WD[d] * fresh
            strike_inverse(t + 1)

        return carry

    lax.fori_loop(0, NSTEP, step_body, 0)

    for copy in out_copies():
        copy.wait()
    for t in range(NSTEP):
        pltpu.make_async_copy(FR.at[t], out_s.at[t], outsem.at[5 + t]).wait()
        left = RI.at[t, pl.ds(0, (2 * nx - 1) * 4)]
        pltpu.make_async_copy(left, left, isend.at[t]).wait()
        left = RF.at[t, pl.ds(0, (nx - 1) * 4)]
        pltpu.make_async_copy(left, left, fsend.at[t]).wait()


def hand_over(f_in, l_in, s_in, f_out, l_out, s_out, f, l, s, sem):
    pieces = [(f_in.at[n], f.at[n], f_out.at[n]) for n in range(f.shape[0])]
    pieces += [(s_in, s, s_out), (l_in, l, l_out)]
    for n, (src, mid, _) in enumerate(pieces):
        pltpu.make_async_copy(src, mid, sem.at[0, n]).start()
    for n, (src, mid, dst) in enumerate(pieces):
        pltpu.make_async_copy(src, mid, sem.at[0, n]).wait()
        pltpu.make_async_copy(mid, dst, sem.at[1, n]).start()
    for n, (_, mid, dst) in enumerate(pieces):
        pltpu.make_async_copy(mid, dst, sem.at[1, n]).wait()


def per_device(nx, fields, buoyancy, stiffness, stress_zero, direct_effect, log_state, kernel, history, truncation):
    planes, rows, cols = fields.shape[2:]
    hist, modes, _, strike = history.shape
    A = 2 * nx
    B = rows // 2
    RB = modes * B
    depth = 2 * cols
    scale = 1.0 / math.sqrt(strike * depth)
    mats, vecs = make_tables(nx, rows, modes, scale)
    kernel = kernel.reshape(hist, modes, B, A).transpose(0, 2, 1, 3).reshape(hist, RB, A)
    history = history.reshape(hist, modes, 2, B, A).transpose(0, 1, 3, 2, 4).reshape(hist, 2 * RB, A)
    truncation = truncation.reshape(modes, B, A).transpose(1, 0, 2).reshape(RB, A)
    LW = min(128, cols)
    vm = pltpu.VMEM
    dma = pltpu.SemaphoreType.DMA
    args = [
        fields.reshape(4, planes, rows, cols), buoyancy[0], stiffness[0], stress_zero, direct_effect, log_state,
        kernel, history, truncation, *[jnp.asarray(x) for x in mats], *[jnp.asarray(x) for x in vecs],
    ]
    scratch = [vm(x.shape, x.dtype) for x in args[1:]] + [
        vm((hist, 2 * RB, A), F32),
        vm((planes, rows, cols), F32),
        vm((NSTEP, 2 * RB, A), F32),
        vm((planes, rows + 16, cols + 2 * LW), F32),
        vm((planes, rows + 16, cols), F32),
        vm((planes, rows, cols + 2 * LW), F32),
        vm((2 * NSTEP - 1, 2 * RB, A), F32),
        vm((NSTEP, 4 * nx, RB), F32),
        vm((NSTEP, 8 * nx, RB), F32),
        vm((RB, 4 * A), F32),
        vm((NSTEP, rows, cols), F32),
        vm((rows, cols), F32),
        vm((NSTEP, rows, cols), F32),
        vm((NSTEP, 2, rows, cols), F32),
        vm((RB, 4 * A), F32),
        vm((NSTEP, 4 * nx, RB), F32),
        vm((NSTEP, 4 * nx, RB), F32),
        vm((rows, cols), F32),
        vm((rows, cols), F32),
        vm((NSTEP, 2, 8, cols), F32),
        vm((NSTEP, planes, rows, LW), F32),
        vm((NSTEP, rows, cols), F32),
        vm((NSTEP, 2, 8, cols), F32),
        vm((NSTEP, planes, rows, LW), F32),
        vm((2, 2, 8, cols), F32),
        dma((21,)), dma((5 + NSTEP,)),
        dma((NSTEP,)), dma((x_layers(nx), NSTEP)), dma((NSTEP,)), dma((x_layers(nx), NSTEP)),
        dma((2, NSTEP)), dma((2, NSTEP)), dma((2, NSTEP)), dma((2, NSTEP)),
        dma((3,)), dma((3, NSTEP)), dma((3,)), dma((3, NSTEP)), dma, dma((NSTEP,)),
    ]
    hbm = pl.BlockSpec(memory_space=pl.ANY)
    out_shape = (
        jax.ShapeDtypeStruct((4, planes, rows, cols), F32),
        jax.ShapeDtypeStruct((rows, cols), F32),
        jax.ShapeDtypeStruct((NSTEP, 2 * RB, A), F32),
    )
    results = pl.pallas_call(
        functools.partial(kernel_body, nx),
        out_shape=out_shape,
        in_specs=[hbm] * len(args),
        out_specs=(hbm, hbm, hbm),
        scratch_shapes=scratch,
        compiler_params=pltpu.CompilerParams(
            collective_id=0, has_side_effects=True, vmem_limit_bytes=60 * 1024 * 1024
        ),
    )(*args)
    out_f, out_l, out_s = pl.pallas_call(
        hand_over,
        out_shape=out_shape,
        in_specs=[hbm] * 3,
        out_specs=(hbm, hbm, hbm),
        scratch_shapes=[vm(x.shape, F32) for x in out_shape] + [dma((2, 6))],
        compiler_params=pltpu.CompilerParams(vmem_limit_bytes=60 * 1024 * 1024),
    )(*results)
    spectra = out_s.reshape(NSTEP, modes, B, 2, A).transpose(0, 1, 3, 2, 4).reshape(NSTEP, modes, 2, strike)
    return out_f.reshape(4, 1, planes, rows, cols), out_l, spectra


def solution(mesh):
    return jax.shard_map(
        functools.partial(per_device, mesh.shape["gx"]),
        mesh=mesh,
        in_specs=(
            P(None, "grp", None, "gx", "gz"),
            P("grp", None, "gx", "gz"),
            P("grp", None, "gx", "gz"),
            P("gx", "gz"),
            P("gx", "gz"),
            P("gx", "gz"),
            P(None, ("grp", "gx", "gz"), None),
            P(None, ("grp", "gx", "gz"), None, None),
            P(("grp", "gx", "gz"), None),
        ),
        out_specs=(
            P(None, "grp", None, "gx", "gz"),
            P("gx", "gz"),
            P(None, ("grp", "gx", "gz"), None, None),
        ),
        check_vma=False,
    )
```

```python
import functools
import math

import jax
import jax.numpy as jnp
import numpy as np
from jax import lax
from jax.experimental import pallas as pl
from jax.experimental.pallas import tpu as pltpu
from jax.sharding import PartitionSpec as P

NSTEP = 4
NEWTON = 4
C1 = 9.0 / 8.0
C2 = 1.0 / 24.0
MESH = pl.DeviceIdType.MESH
BF = jnp.bfloat16
F32 = jnp.float32


def split_table(table):
    hi = np.asarray(table, np.float32).astype(jnp.bfloat16)
    lo = (table - hi.astype(np.float64)).astype(jnp.bfloat16)
    return np.stack([hi, lo])


def cis(turns):
    return np.cos(2 * np.pi * turns), np.sin(2 * np.pi * turns)


def x_layers(nx):
    return 4 if nx == 64 else nx


def layer_order(nx):
    places = np.arange(nx)
    return places.reshape(4, 4, 4).transpose(1, 0, 2).reshape(nx) if nx == 64 else places


def make_tables(nx, rows, modes, scale):
    A = 2 * nx
    B = rows // 2
    R = modes
    depth = 4 * nx * R
    strike = nx * rows
    eye_r = np.eye(R)
    eye_p = np.eye(2)
    m, b, k, a = np.arange(B), np.arange(B), np.arange(A), np.arange(A)
    c, s = cis(np.outer(m, b) / B)
    inv = np.array([[c, -s], [s, c]])
    fwd = np.array([[c, s], [-s, c]])
    L1 = np.einsum("xybm,rs->xrbsmy", inv, eye_r).reshape(2 * R * B, 2 * R * B)
    L3 = np.einsum("xymb,rs->rmxysb", fwd, eye_r).reshape(2 * R * B, 2 * R * B) * scale
    c, s = cis(np.outer(b, k) / strike)
    twiddle = np.stack([np.tile(c, (R, 1)), np.tile(s, (R, 1))])
    c, s = cis(np.outer(a, k) / A)
    inv = np.array([[c, -s], [s, c]]).reshape(2, 2, nx, 2, A)
    T2 = np.einsum("xyjpk->jxpyk", inv).reshape(4 * nx, 2 * A)
    fwd = np.array([[c, s], [-s, c]]).reshape(2, 2, nx, 2, A)
    TV = np.einsum("xyjpk->jpyxk", fwd).reshape(4 * nx, 2 * A)
    i, z = np.arange(nx), np.arange(A)
    c, s = cis(np.outer(i, z) / A)
    sign = np.where(np.arange(2)[:, None] * z[None, :] % 2 == 1, -1.0, 1.0)
    inv = np.array([[c, -s], [s, c]])
    layers = x_layers(nx)
    TI = np.einsum("xyiz,gz,pn->giypnxz", inv, sign, eye_p).reshape(2, nx, 4, 4 * A)
    by_layer = layer_order(nx)
    TI = TI[:, by_layer].reshape(2, layers, 4 * nx // layers, 4 * A).transpose(1, 0, 2, 3).reshape(8 * nx, 4 * A)
    TV = TV.reshape(nx, 4, 2 * A)[by_layer].reshape(4 * nx, 2 * A)
    fwd = np.array([[c, s], [-s, c]])
    TF = np.einsum("xyiz,pn->ipxnyz", fwd, eye_p).reshape(4 * nx, 4 * A)
    zz = np.arange(depth).reshape(2 * R, 1, A)
    r = np.arange(R)[None, :, None]
    wi, wf = [], []
    for q in range(2):
        c, s = cis((R * q + r) * zz / depth)
        wi.append(np.stack([c, -s], axis=2).reshape(2 * R, 2 * R, A) * scale)
    for g in range(2):
        for q in range(2):
            c, s = cis((R * q + r) * zz / depth)
            wf.append(np.stack([c, -s], axis=2).reshape(2 * R, 2 * R, A) * sign[g])
    mats = [split_table(x) for x in (L1, T2, TI, TF, TV, L3)]
    return mats, [np.asarray(x, np.float32) for x in (twiddle, np.stack(wi), np.stack(wf))]


def split(x):
    hi = x.astype(BF)
    return hi, (x - hi.astype(F32)).astype(BF)


def dot(x, y, dims):
    return lax.dot_general(x, y, (dims, ((), ())), preferred_element_type=F32)


def table_left(tab, x, dims):
    hi, lo = split(x)
    return dot(tab[0], hi, dims) + (dot(tab[0], lo, dims) + dot(tab[1], hi, dims))


def table_right(x, tab, dims):
    hi, lo = split(x)
    return dot(hi, tab[0], dims) + (dot(lo, tab[0], dims) + dot(hi, tab[1], dims))


def roll(x, shift, axis):
    return pltpu.roll(x, shift % x.shape[axis], axis)


def kernel_body(
    nx, fields_h, buoy_h, stiff_h, szero_h, direct_h, logs_h, kern_h, hist_h, trunc_h,
    L1_h, T2_h, TI_h, TF_h, TV_h, L3_h, TW_h, WI_h, WF_h,
    out_f, out_l, out_s,
    buoy, stiff, szero, direct, LS, KW, H, TRN, L1, T2, TI, TF, TV, L3, TW, WI, WF, WD, NS, FR,
    VP, SP, DP, ACC, GS, RI, OS, PS, RL, PR, SL, US, SF, RF, TR, SG, HV, DV, NP, HS, DS, HO,
    insem, outsem, isend, irecv, fsend, frecv, psend, precv, lsend, lrecv, vsend, vrecv, ssend, srecv, gsend, grecv,
):
    g, j, q = lax.axis_index("grp"), lax.axis_index("gx"), lax.axis_index("gz")
    A = 2 * nx
    RB = TW.shape[1]
    RW, CW = szero.shape
    B = RW // 2
    R = RB // B
    LW = DV.shape[3]
    HC = CW // A
    HIST = H.shape[0]
    side = (2 * g - 1).astype(F32)
    rows_in = pl.ds(8, RW)
    cols_in = pl.ds(LW, CW)

    LX = x_layers(nx)
    ZY = nx // LX
    if nx == 64:
        turn = (2, 3, 1, 0)
        jz, step = lax.rem(lax.div(j, 4), 4), 4
        jxy = lax.div(j, 16) * 4 + lax.rem(j, 4)
        xs = [lax.rem(lax.div(j, 16) + k, 4) * 16 for k in turn]
        ys = [lax.rem(j + k, 4) for k in turn]
        inner = [x + y for x in xs for y in ys]
    else:
        jz, step, jxy, inner = j, 1, j * 0, [j * 0]

    def each_peer(act):
        def one_layer(i, carry):
            z = lax.rem(jz + i + LX // 2, LX) * step
            for xy in inner[:-1]:
                act(z + xy)

            @pl.when(i != LX - LX // 2)
            def _():
                act(z + inner[-1])

            return carry

        lax.fori_loop(0, LX, one_layer, 0)

    def layer_of(k):
        return lax.rem(jz + LX - (LX // 2 + k) % LX, LX)

    barrier = pltpu.get_barrier_semaphore()

    def greet(peer):
        pl.semaphore_signal(barrier, inc=1, device_id=(g, peer, q), device_id_type=MESH)
        pl.semaphore_signal(barrier, inc=1, device_id=(1 - g, peer, q), device_id_type=MESH)

    each_peer(greet)
    pl.semaphore_signal(barrier, inc=1, device_id=(1 - g, j, q), device_id_type=MESH)
    pl.semaphore_signal(barrier, inc=1, device_id=(g, j, 1 - q), device_id_type=MESH)

    pairs = [
        (kern_h, KW), (trunc_h, TRN), (hist_h, H), (L1_h, L1), (TW_h, TW), (T2_h, T2),
        (fields_h.at[0], VP.at[:, rows_in, cols_in]), (stiff_h, stiff), (fields_h.at[2], SP.at[:, rows_in, :]),
        (fields_h.at[3], DP.at[:, :, cols_in]), (fields_h.at[1], NS), (TI_h, TI), (WI_h, WI), (szero_h, szero),
        (direct_h, direct), (logs_h, LS), (WF_h, WF), (TF_h, TF), (buoy_h, buoy), (TV_h, TV), (L3_h, L3),
    ]
    loads = [pltpu.make_async_copy(src, dst, insem.at[n]) for n, (src, dst) in enumerate(pairs)]
    for copy in loads:
        copy.start()
    for t in range(ACC.shape[0]):
        ACC[t] = jnp.zeros((2 * RB, A), F32)
    VP[:, pl.ds(0, 8), :] = jnp.zeros((4, 8, CW + 2 * LW), F32)
    VP[:, pl.ds(8 + RW, 8), :] = jnp.zeros((4, 8, CW + 2 * LW), F32)
    VP[:, rows_in, pl.ds(0, LW)] = jnp.zeros((4, RW, LW), F32)
    VP[:, rows_in, pl.ds(LW + CW, LW)] = jnp.zeros((4, RW, LW), F32)
    SP[:, pl.ds(0, 8), :] = jnp.zeros((4, 8, CW), F32)
    SP[:, pl.ds(8 + RW, 8), :] = jnp.zeros((4, 8, CW), F32)
    DP[:, :, pl.ds(0, LW)] = jnp.zeros((4, RW, LW), F32)
    DP[:, :, pl.ds(LW + CW, LW)] = jnp.zeros((4, RW, LW), F32)

    loads[0].wait()
    loads[1].wait()

    def mask_lag(lag, carry):
        for r in range(R):
            pick = pl.ds(r, B, stride=R)
            kept = jnp.where(lag < TRN[pick, :], KW[lag, pick, :], 0.0)
            for c in range(2):
                WD[lag, pl.ds(r * 2 * B + c, B, stride=2), :] = kept
        return carry

    lax.fori_loop(0, HIST, mask_lag, 0)

    def lag_sums(ahead):
        for r in range(R):
            part = pl.ds(r * 2 * B, 2 * B)

            def one_lag(lag, total):
                return total + WD[lag + ahead, part, :] * H[lag, part, :]

            ACC[ahead, part, :] = lax.fori_loop(0, HIST - ahead, one_lag, ACC[ahead, part, :])

    for copy in loads[2:6]:
        copy.wait()
    lag_sums(0)

    def strike_inverse(t):
        x = table_left(L1, ACC[t], ((1,), (0,)))
        xr, xi = x[:RB], x[RB:]
        wide = jnp.concatenate([xr * TW[0] - xi * TW[1], xr * TW[1] + xi * TW[0]], axis=1)
        GS[t] = table_left(T2, wide, ((1,), (1,)))

    strike_inverse(0)
    loads[6].wait()
    pl.semaphore_wait(barrier, 2 * (nx - 1) + 2)

    def remote(src, dst, send, recv, device):
        return pltpu.make_async_remote_copy(
            src_ref=src, dst_ref=dst, send_sem=send, recv_sem=recv, device_id=device, device_id_type=MESH
        )

    def row_copies(kind, land, t, send, recv):
        up = remote(HO.at[kind, 0], land.at[t, 0], send.at[0], recv.at[0, t], (g, lax.rem(j + 1, nx), q))
        down = remote(HO.at[kind, 1], land.at[t, 1], send.at[1], recv.at[1, t], (g, lax.rem(j + nx - 1, nx), q))
        return up, down

    def pack_rows(kind, ref, cols):
        for p in range(4):
            HO[kind, 0, 2 * p : 2 * p + 2, :] = ref[p, pl.ds(RW + 6, 2), cols]
            HO[kind, 1, 2 * p : 2 * p + 2, :] = ref[p, pl.ds(8, 2), cols]

    def v_copies(t):
        up, down = row_copies(0, HV, t, vsend, vrecv)
        right = remote(VP.at[:, rows_in, pl.ds(CW, LW)], DV.at[t], vsend.at[2], vrecv.at[2, t], (g, j, 1 - q))
        left = remote(VP.at[:, rows_in, pl.ds(LW, LW)], DV.at[t], vsend.at[2], vrecv.at[2, t], (g, j, 1 - q))
        across = remote(VP.at[0, rows_in, cols_in], NP.at[t], gsend, grecv.at[t], (1 - g, j, q))
        return up, down, right, left, across

    def s_copies(t):
        up, down = row_copies(1, HS, t, ssend, srecv)
        right = remote(DP.at[:, :, pl.ds(CW, LW)], DS.at[t], ssend.at[2], srecv.at[2, t], (g, j, 1 - q))
        left = remote(DP.at[:, :, pl.ds(LW, LW)], DS.at[t], ssend.at[2], srecv.at[2, t], (g, j, 1 - q))
        return up, down, right, left

    def start_halo(up, down, right, left):
        @pl.when(j < nx - 1)
        def _():
            up.start()

        @pl.when(j > 0)
        def _():
            down.start()

        @pl.when(q == 0)
        def _():
            right.start()

        @pl.when(q == 1)
        def _():
            left.start()

    def sent_halo(up, down, right, left):
        @pl.when(j < nx - 1)
        def _():
            up.wait_send()

        @pl.when(j > 0)
        def _():
            down.wait_send()

        right.wait_send()

    def recv_halo(up, down, right, t, land, depth_land, put_rows, put_cols):
        @pl.when(j > 0)
        def _():
            up.wait_recv()
            put_rows(6, land[t, 0])

        @pl.when(j < nx - 1)
        def _():
            down.wait_recv()
            put_rows(8 + RW, land[t, 1])

        right.wait_recv()

        @pl.when(q == 0)
        def _():
            put_cols(LW + CW, depth_land[t])

        @pl.when(q == 1)
        def _():
            put_cols(0, depth_land[t])

    def v_rows(at, x):
        for p in range(4):
            VP[p, pl.ds(at, 2), cols_in] = x[2 * p : 2 * p + 2]

    def v_cols(at, x):
        VP[:, rows_in, pl.ds(at, LW)] = x

    def s_rows(at, x):
        for p in range(4):
            SP[p, pl.ds(at, 2), :] = x[2 * p : 2 * p + 2]

    def d_cols(at, x):
        DP[:, :, pl.ds(at, LW)] = x

    pack_rows(0, VP, cols_in)
    first = v_copies(0)
    start_halo(*first[:4])

    def out_copies():
        return [
            pltpu.make_async_copy(SP.at[:, rows_in, :], out_f.at[2], outsem.at[0]),
            pltpu.make_async_copy(DP.at[:, :, cols_in], out_f.at[3], outsem.at[1]),
            pltpu.make_async_copy(VP.at[:, rows_in, cols_in], out_f.at[0], outsem.at[2]),
            pltpu.make_async_copy(NS, out_f.at[1], outsem.at[3]),
            pltpu.make_async_copy(LS, out_l, outsem.at[4]),
        ]

    def step_body(t, carry):
        mine = pl.ds((jz * 2 * ZY + g * ZY + jxy) * 4, 4)
        landed = irecv.at[jz, t]

        def send_modes(peer):
            block = GS.at[t, pl.ds(peer * 4, 4)]
            remote(block, RI.at[t, mine], isend.at[t], landed, (1 - g, peer, q)).start()
            remote(block, RI.at[t, mine], isend.at[t], landed, (g, peer, q)).start()

        each_peer(send_modes)
        own = GS.at[t, pl.ds(j * 4, 4)]
        remote(own, RI.at[t, mine], isend.at[t], landed, (1 - g, j, q)).start()
        pltpu.make_async_copy(own, RI.at[t, mine], landed).start()

        @pl.when(t == 0)
        def _():
            first[4].start()

        @pl.when(t == 0)
        def _():
            for copy in loads[7:11]:
                copy.wait()

        up, down, right, left, across = v_copies(t)
        recv_halo(up, down, right, t, HV, DV, v_rows, v_cols)
        sent_halo(up, down, right, left)

        def stress_chunk(i, c):
            r0 = pl.multiple_of(i * 8, 8)
            chunk = pl.ds(r0, 8)
            inner = pl.ds(r0 + 8, 8)
            vs = []
            for p in range(4):
                tall = VP[p, pl.ds(r0, 24), cols_in]
                wide = VP[p, inner, :]
                v = tall[8:16]
                vs.append(v)
                st = stiff[p, chunk, :]
                up1, up2, dn1 = (roll(tall, s, 0)[8:16] for s in (-1, -2, 1))
                SP[p, inner, :] = SP[p, inner, :] + st * (C1 * (up1 - v) - C2 * (up2 - dn1))
                up1, up2, dn1 = (roll(wide, s, 1)[:, LW : LW + CW] for s in (-1, -2, 1))
                DP[p, chunk, cols_in] = DP[p, chunk, cols_in] + st * (C1 * (up1 - v) - C2 * (up2 - dn1))
            for p in range(1, 4):
                far = 0.0 - (vs[p - 2] if p >= 2 else 0.0)
                if p < 3:
                    far = vs[p + 1] + far
                NS[p, chunk, :] = NS[p, chunk, :] + stiff[p, chunk, :] * (C1 * (vs[p] - vs[p - 1]) - C2 * far)
            return c

        lax.fori_loop(0, RW // 8, stress_chunk, 0)
        pack_rows(1, SP, slice(None))
        up, down, right, left = s_copies(t)
        start_halo(up, down, right, left)

        @pl.when(t == NSTEP - 1)
        def _():
            for copy in out_copies()[:2]:
                copy.start()

        across.wait()
        SG[...] = side * (VP[0, rows_in, cols_in] - NP[t])

        @pl.when(t < NSTEP - 1)
        def _():
            lag_sums(t + 1)

        @pl.when(t == 0)
        def _():
            for copy in loads[11:]:
                copy.wait()

        count = 8 * ZY
        for k in range(0, LX, 2):
            xs, spots = [], []
            for n in (k, k + 1):
                layer = layer_of(n)
                spot = pl.ds(pl.multiple_of(layer * count, count), count)
                pltpu.make_async_copy(RI.at[t, spot], RI.at[t, spot], irecv.at[layer, t]).wait()
                xs.append(RI[t, spot, :].T)
                spots.append(spot)
            tab = [jnp.concatenate([TI[n, spot, :] for spot in spots], axis=0) for n in range(2)]
            term = table_right(jnp.concatenate(xs, axis=1), tab, ((1,), (0,)))
            OS[...] = term if k == 0 else OS[...] + term

        def depth_half(half, p, put):
            for hl in range(HC):
                tw = WI[q, half * HC + hl]
                total = None
                for k in range(2 * R):
                    r, c = k // 2, k % 2
                    term = tw[k : k + 1] * OS[r * B : (r + 1) * B, (2 * p + c) * A : (2 * p + c + 1) * A]
                    total = term if total is None else total + term
                put[p * B : (p + 1) * B, hl * A : (hl + 1) * A] = total

        parts = []
        for p in range(2):
            depth_half(1 - q, p, PS.at[t])
            here = pl.ds(p * B, B)
            part = remote(PS.at[t, here], PR.at[t, here], psend.at[p, t], precv.at[p, t], (g, j, 1 - q))
            part.start()
            parts.append(part)
        for p in range(2):
            depth_half(q, p, RL)

        CH = 16

        def friction_chunk(i, c):
            chunk = pl.ds(pl.multiple_of(i * CH, CH), CH)
            guess = SG[chunk, :]
            loading = szero[chunk, :] + (RL[chunk, :] + PR[t, chunk, :]) + guess
            a = direct[chunk, :]
            ls = LS[chunk, :]
            factor = jnp.exp(ls)
            af = a * factor
            v = guess
            for _ in range(NEWTON):
                s = v * factor
                root = jnp.sqrt(1.0 + s * s)
                size = jnp.log(jnp.abs(s) + root)
                misfit = a * jnp.where(s < 0.0, -size, size) + v - loading
                v = v - misfit / (af / root + 1.0)
            SL[t, q, chunk, :] = v
            TR[chunk, :] = side * (loading - v)
            LS[chunk, :] = 0.75 * ls - 0.2 * jnp.log(1.0 + v * v) + 0.1
            return c

        slips = []
        for p in range(2):
            parts[p].wait_recv()
            lax.fori_loop(p * B // CH, (p + 1) * B // CH, friction_chunk, 0)
            here = pl.ds(p * B, B)
            slip = remote(SL.at[t, q, here], SL.at[t, q, here], lsend.at[p, t], lrecv.at[p, t], (g, j, 1 - q))
            slip.start()
            slips.append(slip)

        def depth_terms(half, p, add):
            acc = None
            for hl in range(HC):
                tw = WF[2 * g + q, half * HC + hl]
                cells = SL[t, half, p * B : (p + 1) * B, hl * A : (hl + 1) * A]
                terms = [tw[k : k + 1] * cells for k in range(2 * R)]
                acc = terms if acc is None else [x + y for x, y in zip(acc, terms)]
            for k in range(2 * R):
                r, c = k // 2, k % 2
                at = (slice(r * B, (r + 1) * B), slice((2 * p + c) * A, (2 * p + c + 1) * A))
                US[at] = US[at] + acc[k] if add else acc[k]

        for p in range(2):
            depth_terms(q, p, False)
        for p in range(2):
            here = pl.ds(p * B, B)
            land = SL.at[t, 1 - q, here]
            pltpu.make_async_copy(land, land, lrecv.at[p, t]).wait()
            depth_terms(1 - q, p, True)
        SF[t] = table_left(TF, US[...], ((1,), (1,)))
        spot = pl.ds((jz * ZY + jxy) * 4, 4)
        block_here = pl.ds(j * 4, 4)
        arrived = frecv.at[jz, t]

        def send_slip(peer):
            remote(SF.at[t, pl.ds(peer * 4, 4)], RF.at[t, spot], fsend.at[t], arrived, (g, peer, q)).start()

        each_peer(send_slip)
        pltpu.make_async_copy(SF.at[t, block_here], RF.at[t, spot], arrived).start()

        recv_halo(up, down, right, t, HS, DS, s_rows, d_cols)
        sent_halo(up, down, right, left)
        NS[0] = TR[...]

        def fault_chunk(i, c):
            r0 = pl.multiple_of(i * 8, 8)
            chunk = pl.ds(r0, 8)
            inner = pl.ds(r0 + 8, 8)
            n0, n1, n2, n3 = (NS[p, chunk, :] for p in range(4))
            plane_terms = [
                C1 * (n1 - n0) - C2 * n2,
                C1 * (n2 - n1) - C2 * (n3 - n0),
                C1 * (n3 - n2) + C2 * n1,
                C2 * n2 - C1 * n3,
            ]
            for p in range(1):
                tall = SP[p, pl.ds(r0, 24), :]
                wide = DP[p, chunk, :]
                dn1, dn2, up1 = (roll(tall, s, 0)[8:16] for s in (1, 2, -1))
                total = plane_terms[p] + (C1 * (tall[8:16] - dn1) - C2 * (up1 - dn2))
                dn1, dn2, up1 = (roll(wide, s, 1)[:, LW : LW + CW] for s in (1, 2, -1))
                total = total + (C1 * (wide[:, LW : LW + CW] - dn1) - C2 * (up1 - dn2))
                VP[p, inner, cols_in] = VP[p, inner, cols_in] + buoy[p, chunk, :] * total
            return c

        lax.fori_loop(0, RW // 8, fault_chunk, 0)

        @pl.when(t < NSTEP - 1)
        def _():
            v_copies(t + 1)[4].start()

        def velocity_chunk(i, c):
            r0 = pl.multiple_of(i * 8, 8)
            chunk = pl.ds(r0, 8)
            inner = pl.ds(r0 + 8, 8)
            n0, n1, n2, n3 = (NS[p, chunk, :] for p in range(4))
            plane_terms = [
                C1 * (n1 - n0) - C2 * n2,
                C1 * (n2 - n1) - C2 * (n3 - n0),
                C1 * (n3 - n2) + C2 * n1,
                C2 * n2 - C1 * n3,
            ]
            for p in range(1, 4):
                tall = SP[p, pl.ds(r0, 24), :]
                wide = DP[p, chunk, :]
                dn1, dn2, up1 = (roll(tall, s, 0)[8:16] for s in (1, 2, -1))
                total = plane_terms[p] + (C1 * (tall[8:16] - dn1) - C2 * (up1 - dn2))
                dn1, dn2, up1 = (roll(wide, s, 1)[:, LW : LW + CW] for s in (1, 2, -1))
                total = total + (C1 * (wide[:, LW : LW + CW] - dn1) - C2 * (up1 - dn2))
                VP[p, inner, cols_in] = VP[p, inner, cols_in] + buoy[p, chunk, :] * total
            return c

        lax.fori_loop(0, RW // 8, velocity_chunk, 0)

        @pl.when(t < NSTEP - 1)
        def _():
            pack_rows(0, VP, cols_in)
            start_halo(*v_copies(t + 1)[:4])

        @pl.when(t == NSTEP - 1)
        def _():
            for copy in out_copies()[2:]:
                copy.start()

        for p in range(2):
            parts[p].wait_send()
            slips[p].wait_send()
        count = 4 * ZY
        xs, spots = [], []
        for k in range(0, LX, 2):
            pair = []
            for n in (k, k + 1):
                layer = layer_of(n)
                spot = pl.ds(pl.multiple_of(layer * count, count), count)
                pltpu.make_async_copy(RF.at[t, spot], RF.at[t, spot], frecv.at[layer, t]).wait()
                pair.append(RF[t, spot, :])
                spots.append(spot)
            xs.append(jnp.concatenate(pair, axis=0).T)
        tab = [jnp.concatenate([TV[n, spot, :] for spot in spots], axis=0) for n in range(2)]
        x = table_right(jnp.concatenate(xs, axis=1), tab, ((1,), (0,)))
        xr, xi = x[:, :A], x[:, A:]
        tall = jnp.concatenate([xr * TW[0] + xi * TW[1], xi * TW[0] - xr * TW[1]], axis=0)
        fresh = table_left(L3, tall, ((1,), (0,)))
        FR[t] = fresh
        pltpu.make_async_copy(FR.at[t], out_s.at[t], outsem.at[5 + t]).start()

        @pl.when(t < NSTEP - 1)
        def _():
            for d in range(NSTEP - 1):
                ACC[t + 1 + d] = ACC[t + 1 + d] + WD[d] * fresh
            strike_inverse(t + 1)

        return carry

    lax.fori_loop(0, NSTEP, step_body, 0)

    for copy in out_copies():
        copy.wait()
    for t in range(NSTEP):
        pltpu.make_async_copy(FR.at[t], out_s.at[t], outsem.at[5 + t]).wait()
        left = RI.at[t, pl.ds(0, (2 * nx - 1) * 4)]
        pltpu.make_async_copy(left, left, isend.at[t]).wait()
        left = RF.at[t, pl.ds(0, (nx - 1) * 4)]
        pltpu.make_async_copy(left, left, fsend.at[t]).wait()


def hand_over(f_in, l_in, s_in, f_out, l_out, s_out, f, l, s, sem):
    pieces = [(f_in.at[n], f.at[n], f_out.at[n]) for n in range(f.shape[0])]
    pieces += [(s_in, s, s_out), (l_in, l, l_out)]
    for n, (src, mid, _) in enumerate(pieces):
        pltpu.make_async_copy(src, mid, sem.at[0, n]).start()
    for n, (src, mid, dst) in enumerate(pieces):
        pltpu.make_async_copy(src, mid, sem.at[0, n]).wait()
        pltpu.make_async_copy(mid, dst, sem.at[1, n]).start()
    for n, (_, mid, dst) in enumerate(pieces):
        pltpu.make_async_copy(mid, dst, sem.at[1, n]).wait()


def per_device(nx, fields, buoyancy, stiffness, stress_zero, direct_effect, log_state, kernel, history, truncation):
    planes, rows, cols = fields.shape[2:]
    hist, modes, _, strike = history.shape
    A = 2 * nx
    B = rows // 2
    RB = modes * B
    depth = 2 * cols
    scale = 1.0 / math.sqrt(strike * depth)
    mats, vecs = make_tables(nx, rows, modes, scale)
    kernel = kernel.reshape(hist, modes, B, A).transpose(0, 2, 1, 3).reshape(hist, RB, A)
    history = history.reshape(hist, modes, 2, B, A).transpose(0, 1, 3, 2, 4).reshape(hist, 2 * RB, A)
    truncation = truncation.reshape(modes, B, A).transpose(1, 0, 2).reshape(RB, A)
    LW = min(128, cols)
    vm = pltpu.VMEM
    dma = pltpu.SemaphoreType.DMA
    args = [
        fields.reshape(4, planes, rows, cols), buoyancy[0], stiffness[0], stress_zero, direct_effect, log_state,
        kernel, history, truncation, *[jnp.asarray(x) for x in mats], *[jnp.asarray(x) for x in vecs],
    ]
    scratch = [vm(x.shape, x.dtype) for x in args[1:]] + [
        vm((hist, 2 * RB, A), F32),
        vm((planes, rows, cols), F32),
        vm((NSTEP, 2 * RB, A), F32),
        vm((planes, rows + 16, cols + 2 * LW), F32),
        vm((planes, rows + 16, cols), F32),
        vm((planes, rows, cols + 2 * LW), F32),
        vm((2 * NSTEP - 1, 2 * RB, A), F32),
        vm((NSTEP, 4 * nx, RB), F32),
        vm((NSTEP, 8 * nx, RB), F32),
        vm((RB, 4 * A), F32),
        vm((NSTEP, rows, cols), F32),
        vm((rows, cols), F32),
        vm((NSTEP, rows, cols), F32),
        vm((NSTEP, 2, rows, cols), F32),
        vm((RB, 4 * A), F32),
        vm((NSTEP, 4 * nx, RB), F32),
        vm((NSTEP, 4 * nx, RB), F32),
        vm((rows, cols), F32),
        vm((rows, cols), F32),
        vm((NSTEP, 2, 8, cols), F32),
        vm((NSTEP, planes, rows, LW), F32),
        vm((NSTEP, rows, cols), F32),
        vm((NSTEP, 2, 8, cols), F32),
        vm((NSTEP, planes, rows, LW), F32),
        vm((2, 2, 8, cols), F32),
        dma((21,)), dma((5 + NSTEP,)),
        dma((NSTEP,)), dma((x_layers(nx), NSTEP)), dma((NSTEP,)), dma((x_layers(nx), NSTEP)),
        dma((2, NSTEP)), dma((2, NSTEP)), dma((2, NSTEP)), dma((2, NSTEP)),
        dma((3,)), dma((3, NSTEP)), dma((3,)), dma((3, NSTEP)), dma, dma((NSTEP,)),
    ]
    hbm = pl.BlockSpec(memory_space=pl.ANY)
    out_shape = (
        jax.ShapeDtypeStruct((4, planes, rows, cols), F32),
        jax.ShapeDtypeStruct((rows, cols), F32),
        jax.ShapeDtypeStruct((NSTEP, 2 * RB, A), F32),
    )
    results = pl.pallas_call(
        functools.partial(kernel_body, nx),
        out_shape=out_shape,
        in_specs=[hbm] * len(args),
        out_specs=(hbm, hbm, hbm),
        scratch_shapes=scratch,
        compiler_params=pltpu.CompilerParams(
            collective_id=0, has_side_effects=True, vmem_limit_bytes=60 * 1024 * 1024
        ),
    )(*args)
    out_f, out_l, out_s = pl.pallas_call(
        hand_over,
        out_shape=out_shape,
        in_specs=[hbm] * 3,
        out_specs=(hbm, hbm, hbm),
        scratch_shapes=[vm(x.shape, F32) for x in out_shape] + [dma((2, 6))],
        compiler_params=pltpu.CompilerParams(vmem_limit_bytes=60 * 1024 * 1024),
    )(*results)
    spectra = out_s.reshape(NSTEP, modes, B, 2, A).transpose(0, 1, 3, 2, 4).reshape(NSTEP, modes, 2, strike)
    return out_f.reshape(4, 1, planes, rows, cols), out_l, spectra


def solution(mesh):
    return jax.shard_map(
        functools.partial(per_device, mesh.shape["gx"]),
        mesh=mesh,
        in_specs=(
            P(None, "grp", None, "gx", "gz"),
            P("grp", None, "gx", "gz"),
            P("grp", None, "gx", "gz"),
            P("gx", "gz"),
            P("gx", "gz"),
            P("gx", "gz"),
            P(None, ("grp", "gx", "gz"), None),
            P(None, ("grp", "gx", "gz"), None, None),
            P(("grp", "gx", "gz"), None),
        ),
        out_specs=(
            P(None, "grp", None, "gx", "gz"),
            P("gx", "gz"),
            P(None, ("grp", "gx", "gz"), None, None),
        ),
        check_vma=False,
    )
```

```python
import functools
import math

import jax
import jax.numpy as jnp
import numpy as np
from jax import lax
from jax.experimental import pallas as pl
from jax.experimental.pallas import tpu as pltpu
from jax.sharding import PartitionSpec as P

NSTEP = 4
NEWTON = 4
C1 = 9.0 / 8.0
C2 = 1.0 / 24.0
MESH = pl.DeviceIdType.MESH
BF = jnp.bfloat16
F32 = jnp.float32


def split_table(table):
    hi = np.asarray(table, np.float32).astype(jnp.bfloat16)
    lo = (table - hi.astype(np.float64)).astype(jnp.bfloat16)
    return np.stack([hi, lo])


def cis(turns):
    return np.cos(2 * np.pi * turns), np.sin(2 * np.pi * turns)


def x_layers(nx):
    return 4 if nx == 64 else nx


def layer_order(nx):
    places = np.arange(nx)
    return places.reshape(4, 4, 4).transpose(1, 0, 2).reshape(nx) if nx == 64 else places


def make_tables(nx, rows, modes, scale):
    A = 2 * nx
    B = rows // 2
    R = modes
    depth = 4 * nx * R
    strike = nx * rows
    eye_r = np.eye(R)
    eye_p = np.eye(2)
    m, b, k, a = np.arange(B), np.arange(B), np.arange(A), np.arange(A)
    c, s = cis(np.outer(m, b) / B)
    inv = np.array([[c, -s], [s, c]])
    fwd = np.array([[c, s], [-s, c]])
    L1 = np.einsum("xybm,rs->xrbsmy", inv, eye_r).reshape(2 * R * B, 2 * R * B)
    L3 = np.einsum("xymb,rs->rmxysb", fwd, eye_r).reshape(2 * R * B, 2 * R * B) * scale
    c, s = cis(np.outer(b, k) / strike)
    twiddle = np.stack([np.tile(c, (R, 1)), np.tile(s, (R, 1))])
    c, s = cis(np.outer(a, k) / A)
    inv = np.array([[c, -s], [s, c]]).reshape(2, 2, nx, 2, A)
    T2 = np.einsum("xyjpk->jxpyk", inv).reshape(4 * nx, 2 * A)
    fwd = np.array([[c, s], [-s, c]]).reshape(2, 2, nx, 2, A)
    TV = np.einsum("xyjpk->jpyxk", fwd).reshape(4 * nx, 2 * A)
    i, z = np.arange(nx), np.arange(A)
    c, s = cis(np.outer(i, z) / A)
    sign = np.where(np.arange(2)[:, None] * z[None, :] % 2 == 1, -1.0, 1.0)
    inv = np.array([[c, -s], [s, c]])
    layers = x_layers(nx)
    TI = np.einsum("xyiz,gz,pn->giypnxz", inv, sign, eye_p).reshape(2, nx, 4, 4 * A)
    by_layer = layer_order(nx)
    TI = TI[:, by_layer].reshape(2, layers, 4 * nx // layers, 4 * A).transpose(1, 0, 2, 3).reshape(8 * nx, 4 * A)
    TV = TV.reshape(nx, 4, 2 * A)[by_layer].reshape(4 * nx, 2 * A)
    fwd = np.array([[c, s], [-s, c]])
    TF = np.einsum("xyiz,pn->ipxnyz", fwd, eye_p).reshape(4 * nx, 4 * A)
    zz = np.arange(depth).reshape(2 * R, 1, A)
    r = np.arange(R)[None, :, None]
    wi, wf = [], []
    for q in range(2):
        c, s = cis((R * q + r) * zz / depth)
        wi.append(np.stack([c, -s], axis=2).reshape(2 * R, 2 * R, A) * scale)
    for g in range(2):
        for q in range(2):
            c, s = cis((R * q + r) * zz / depth)
            wf.append(np.stack([c, -s], axis=2).reshape(2 * R, 2 * R, A) * sign[g])
    mats = [split_table(x) for x in (L1, T2, TI, TF, TV, L3)]
    return mats, [np.asarray(x, np.float32) for x in (twiddle, np.stack(wi), np.stack(wf))]


def split(x):
    hi = x.astype(BF)
    return hi, (x - hi.astype(F32)).astype(BF)


def dot(x, y, dims):
    return lax.dot_general(x, y, (dims, ((), ())), preferred_element_type=F32)


def table_left(tab, x, dims):
    hi, lo = split(x)
    return dot(tab[0], hi, dims) + (dot(tab[0], lo, dims) + dot(tab[1], hi, dims))


def table_right(x, tab, dims):
    hi, lo = split(x)
    return dot(hi, tab[0], dims) + (dot(lo, tab[0], dims) + dot(hi, tab[1], dims))


def roll(x, shift, axis):
    return pltpu.roll(x, shift % x.shape[axis], axis)


def kernel_body(
    nx, fields_h, buoy_h, stiff_h, szero_h, direct_h, logs_h, kern_h, hist_h, trunc_h,
    L1_h, T2_h, TI_h, TF_h, TV_h, L3_h, TW_h, WI_h, WF_h,
    out_f, out_l, out_s,
    buoy, stiff, szero, direct, LS, KW, H, TRN, L1, T2, TI, TF, TV, L3, TW, WI, WF, WD, NS, FR,
    VP, SP, DP, ACC, GS, RI, OS, PS, RL, PR, SL, US, SF, RF, TR, SG, HV, DV, NP, HS, DS, HO,
    insem, outsem, isend, irecv, fsend, frecv, psend, precv, lsend, lrecv, vsend, vrecv, ssend, srecv, gsend, grecv,
):
    g, j, q = lax.axis_index("grp"), lax.axis_index("gx"), lax.axis_index("gz")
    A = 2 * nx
    RB = TW.shape[1]
    RW, CW = szero.shape
    B = RW // 2
    R = RB // B
    LW = DV.shape[3]
    HC = CW // A
    HIST = H.shape[0]
    side = (2 * g - 1).astype(F32)
    rows_in = pl.ds(8, RW)
    cols_in = pl.ds(LW, CW)

    LX = x_layers(nx)
    ZY = nx // LX
    if nx == 64:
        turn = (2, 3, 1, 0)
        jz, step = lax.rem(lax.div(j, 4), 4), 4
        jxy = lax.div(j, 16) * 4 + lax.rem(j, 4)
        xs = [lax.rem(lax.div(j, 16) + k, 4) * 16 for k in turn]
        ys = [lax.rem(j + k, 4) for k in turn]
        inner = [x + y for x in xs for y in ys]
    else:
        jz, step, jxy, inner = j, 1, j * 0, [j * 0]

    def each_peer(act):
        def one_layer(i, carry):
            z = lax.rem(jz + i + LX // 2, LX) * step
            for xy in inner[:-1]:
                act(z + xy)

            @pl.when(i != LX - LX // 2)
            def _():
                act(z + inner[-1])

            return carry

        lax.fori_loop(0, LX, one_layer, 0)

    def layer_of(k):
        return lax.rem(jz + LX - (LX // 2 + k) % LX, LX)

    barrier = pltpu.get_barrier_semaphore()

    def greet(peer):
        pl.semaphore_signal(barrier, inc=1, device_id=(g, peer, q), device_id_type=MESH)
        pl.semaphore_signal(barrier, inc=1, device_id=(1 - g, peer, q), device_id_type=MESH)

    each_peer(greet)
    pl.semaphore_signal(barrier, inc=1, device_id=(1 - g, j, q), device_id_type=MESH)
    pl.semaphore_signal(barrier, inc=1, device_id=(g, j, 1 - q), device_id_type=MESH)

    pairs = [
        (kern_h, KW), (trunc_h, TRN), (hist_h, H), (L1_h, L1), (TW_h, TW), (T2_h, T2),
        (fields_h.at[0], VP.at[:, rows_in, cols_in]), (stiff_h, stiff), (fields_h.at[2], SP.at[:, rows_in, :]),
        (fields_h.at[3], DP.at[:, :, cols_in]), (fields_h.at[1], NS), (TI_h, TI), (WI_h, WI), (szero_h, szero),
        (direct_h, direct), (logs_h, LS), (WF_h, WF), (TF_h, TF), (buoy_h, buoy), (TV_h, TV), (L3_h, L3),
    ]
    loads = [pltpu.make_async_copy(src, dst, insem.at[n]) for n, (src, dst) in enumerate(pairs)]
    for copy in loads:
        copy.start()
    for t in range(ACC.shape[0]):
        ACC[t] = jnp.zeros((2 * RB, A), F32)
    VP[:, pl.ds(0, 8), :] = jnp.zeros((4, 8, CW + 2 * LW), F32)
    VP[:, pl.ds(8 + RW, 8), :] = jnp.zeros((4, 8, CW + 2 * LW), F32)
    VP[:, rows_in, pl.ds(0, LW)] = jnp.zeros((4, RW, LW), F32)
    VP[:, rows_in, pl.ds(LW + CW, LW)] = jnp.zeros((4, RW, LW), F32)
    SP[:, pl.ds(0, 8), :] = jnp.zeros((4, 8, CW), F32)
    SP[:, pl.ds(8 + RW, 8), :] = jnp.zeros((4, 8, CW), F32)
    DP[:, :, pl.ds(0, LW)] = jnp.zeros((4, RW, LW), F32)
    DP[:, :, pl.ds(LW + CW, LW)] = jnp.zeros((4, RW, LW), F32)

    loads[0].wait()
    loads[1].wait()

    def mask_lag(lag, carry):
        for r in range(R):
            pick = pl.ds(r, B, stride=R)
            kept = jnp.where(lag < TRN[pick, :], KW[lag, pick, :], 0.0)
            for c in range(2):
                WD[lag, pl.ds(r * 2 * B + c, B, stride=2), :] = kept
        return carry

    lax.fori_loop(0, HIST, mask_lag, 0)

    def lag_sums(ahead):
        for r in range(R):
            part = pl.ds(r * 2 * B, 2 * B)

            def one_lag(lag, total):
                return total + WD[lag + ahead, part, :] * H[lag, part, :]

            ACC[ahead, part, :] = lax.fori_loop(0, HIST - ahead, one_lag, ACC[ahead, part, :])

    for copy in loads[2:6]:
        copy.wait()
    lag_sums(0)

    def strike_inverse(t):
        x = table_left(L1, ACC[t], ((1,), (0,)))
        xr, xi = x[:RB], x[RB:]
        wide = jnp.concatenate([xr * TW[0] - xi * TW[1], xr * TW[1] + xi * TW[0]], axis=1)
        GS[t] = table_left(T2, wide, ((1,), (1,)))

    strike_inverse(0)
    loads[6].wait()
    pl.semaphore_wait(barrier, 2 * (nx - 1) + 2)

    def remote(src, dst, send, recv, device):
        return pltpu.make_async_remote_copy(
            src_ref=src, dst_ref=dst, send_sem=send, recv_sem=recv, device_id=device, device_id_type=MESH
        )

    def row_copies(kind, land, t, send, recv):
        up = remote(HO.at[kind, 0], land.at[t, 0], send.at[0], recv.at[0, t], (g, lax.rem(j + 1, nx), q))
        down = remote(HO.at[kind, 1], land.at[t, 1], send.at[1], recv.at[1, t], (g, lax.rem(j + nx - 1, nx), q))
        return up, down

    def pack_rows(kind, ref, cols):
        for p in range(4):
            HO[kind, 0, 2 * p : 2 * p + 2, :] = ref[p, pl.ds(RW + 6, 2), cols]
            HO[kind, 1, 2 * p : 2 * p + 2, :] = ref[p, pl.ds(8, 2), cols]

    def v_copies(t):
        up, down = row_copies(0, HV, t, vsend, vrecv)
        right = remote(VP.at[:, rows_in, pl.ds(CW, LW)], DV.at[t], vsend.at[2], vrecv.at[2, t], (g, j, 1 - q))
        left = remote(VP.at[:, rows_in, pl.ds(LW, LW)], DV.at[t], vsend.at[2], vrecv.at[2, t], (g, j, 1 - q))
        across = remote(VP.at[0, rows_in, cols_in], NP.at[t], gsend, grecv.at[t], (1 - g, j, q))
        return up, down, right, left, across

    def s_copies(t):
        up, down = row_copies(1, HS, t, ssend, srecv)
        right = remote(DP.at[:, :, pl.ds(CW, LW)], DS.at[t], ssend.at[2], srecv.at[2, t], (g, j, 1 - q))
        left = remote(DP.at[:, :, pl.ds(LW, LW)], DS.at[t], ssend.at[2], srecv.at[2, t], (g, j, 1 - q))
        return up, down, right, left

    def start_halo(up, down, right, left):
        @pl.when(j < nx - 1)
        def _():
            up.start()

        @pl.when(j > 0)
        def _():
            down.start()

        @pl.when(q == 0)
        def _():
            right.start()

        @pl.when(q == 1)
        def _():
            left.start()

    def sent_halo(up, down, right, left):
        @pl.when(j < nx - 1)
        def _():
            up.wait_send()

        @pl.when(j > 0)
        def _():
            down.wait_send()

        right.wait_send()

    def recv_halo(up, down, right, t, land, depth_land, put_rows, put_cols):
        @pl.when(j > 0)
        def _():
            up.wait_recv()
            put_rows(6, land[t, 0])

        @pl.when(j < nx - 1)
        def _():
            down.wait_recv()
            put_rows(8 + RW, land[t, 1])

        right.wait_recv()

        @pl.when(q == 0)
        def _():
            put_cols(LW + CW, depth_land[t])

        @pl.when(q == 1)
        def _():
            put_cols(0, depth_land[t])

    def v_rows(at, x):
        for p in range(4):
            VP[p, pl.ds(at, 2), cols_in] = x[2 * p : 2 * p + 2]

    def v_cols(at, x):
        VP[:, rows_in, pl.ds(at, LW)] = x

    def s_rows(at, x):
        for p in range(4):
            SP[p, pl.ds(at, 2), :] = x[2 * p : 2 * p + 2]

    def d_cols(at, x):
        DP[:, :, pl.ds(at, LW)] = x

    pack_rows(0, VP, cols_in)
    first = v_copies(0)
    start_halo(*first[:4])

    def out_copies():
        return [
            pltpu.make_async_copy(SP.at[:, rows_in, :], out_f.at[2], outsem.at[0]),
            pltpu.make_async_copy(DP.at[:, :, cols_in], out_f.at[3], outsem.at[1]),
            pltpu.make_async_copy(VP.at[:, rows_in, cols_in], out_f.at[0], outsem.at[2]),
            pltpu.make_async_copy(NS, out_f.at[1], outsem.at[3]),
            pltpu.make_async_copy(LS, out_l, outsem.at[4]),
        ]

    def step_body(t, carry):
        mine = pl.ds((jz * 2 * ZY + g * ZY + jxy) * 4, 4)
        landed = irecv.at[jz, t]

        def send_modes(peer):
            block = GS.at[t, pl.ds(peer * 4, 4)]
            remote(block, RI.at[t, mine], isend.at[t], landed, (g, peer, q)).start()
            remote(block, RI.at[t, mine], isend.at[t], landed, (1 - g, peer, q)).start()

        each_peer(send_modes)
        own = GS.at[t, pl.ds(j * 4, 4)]
        remote(own, RI.at[t, mine], isend.at[t], landed, (1 - g, j, q)).start()
        pltpu.make_async_copy(own, RI.at[t, mine], landed).start()

        @pl.when(t == 0)
        def _():
            first[4].start()

        @pl.when(t == 0)
        def _():
            for copy in loads[7:11]:
                copy.wait()

        up, down, right, left, across = v_copies(t)
        recv_halo(up, down, right, t, HV, DV, v_rows, v_cols)
        sent_halo(up, down, right, left)

        def stress_chunk(i, c):
            r0 = pl.multiple_of(i * 8, 8)
            chunk = pl.ds(r0, 8)
            inner = pl.ds(r0 + 8, 8)
            vs = []
            for p in range(4):
                tall = VP[p, pl.ds(r0, 24), cols_in]
                wide = VP[p, inner, :]
                v = tall[8:16]
                vs.append(v)
                st = stiff[p, chunk, :]
                up1, up2, dn1 = (roll(tall, s, 0)[8:16] for s in (-1, -2, 1))
                SP[p, inner, :] = SP[p, inner, :] + st * (C1 * (up1 - v) - C2 * (up2 - dn1))
                up1, up2, dn1 = (roll(wide, s, 1)[:, LW : LW + CW] for s in (-1, -2, 1))
                DP[p, chunk, cols_in] = DP[p, chunk, cols_in] + st * (C1 * (up1 - v) - C2 * (up2 - dn1))
            for p in range(1, 4):
                far = 0.0 - (vs[p - 2] if p >= 2 else 0.0)
                if p < 3:
                    far = vs[p + 1] + far
                NS[p, chunk, :] = NS[p, chunk, :] + stiff[p, chunk, :] * (C1 * (vs[p] - vs[p - 1]) - C2 * far)
            return c

        lax.fori_loop(0, RW // 8, stress_chunk, 0)
        pack_rows(1, SP, slice(None))
        up, down, right, left = s_copies(t)
        start_halo(up, down, right, left)

        @pl.when(t == NSTEP - 1)
        def _():
            for copy in out_copies()[:2]:
                copy.start()

        across.wait()
        SG[...] = side * (VP[0, rows_in, cols_in] - NP[t])

        @pl.when(t < NSTEP - 1)
        def _():
            lag_sums(t + 1)

        @pl.when(t == 0)
        def _():
            for copy in loads[11:]:
                copy.wait()

        count = 8 * ZY
        for k in range(0, LX, 2):
            xs, spots = [], []
            for n in (k, k + 1):
                layer = layer_of(n)
                spot = pl.ds(pl.multiple_of(layer * count, count), count)
                pltpu.make_async_copy(RI.at[t, spot], RI.at[t, spot], irecv.at[layer, t]).wait()
                xs.append(RI[t, spot, :].T)
                spots.append(spot)
            tab = [jnp.concatenate([TI[n, spot, :] for spot in spots], axis=0) for n in range(2)]
            term = table_right(jnp.concatenate(xs, axis=1), tab, ((1,), (0,)))
            OS[...] = term if k == 0 else OS[...] + term

        def depth_half(half, p, put):
            for hl in range(HC):
                tw = WI[q, half * HC + hl]
                total = None
                for k in range(2 * R):
                    r, c = k // 2, k % 2
                    term = tw[k : k + 1] * OS[r * B : (r + 1) * B, (2 * p + c) * A : (2 * p + c + 1) * A]
                    total = term if total is None else total + term
                put[p * B : (p + 1) * B, hl * A : (hl + 1) * A] = total

        parts = []
        for p in range(2):
            depth_half(1 - q, p, PS.at[t])
            here = pl.ds(p * B, B)
            part = remote(PS.at[t, here], PR.at[t, here], psend.at[p, t], precv.at[p, t], (g, j, 1 - q))
            part.start()
            parts.append(part)
        for p in range(2):
            depth_half(q, p, RL)

        CH = 16

        def friction_chunk(i, c):
            chunk = pl.ds(pl.multiple_of(i * CH, CH), CH)
            guess = SG[chunk, :]
            loading = szero[chunk, :] + (RL[chunk, :] + PR[t, chunk, :]) + guess
            a = direct[chunk, :]
            ls = LS[chunk, :]
            factor = jnp.exp(ls)
            af = a * factor
            v = guess
            for _ in range(NEWTON):
                s = v * factor
                root = jnp.sqrt(1.0 + s * s)
                size = jnp.log(jnp.abs(s) + root)
                misfit = a * jnp.where(s < 0.0, -size, size) + v - loading
                v = v - misfit / (af / root + 1.0)
            SL[t, q, chunk, :] = v
            TR[chunk, :] = side * (loading - v)
            LS[chunk, :] = 0.75 * ls - 0.2 * jnp.log(1.0 + v * v) + 0.1
            return c

        slips = []
        for p in range(2):
            parts[p].wait_recv()
            lax.fori_loop(p * B // CH, (p + 1) * B // CH, friction_chunk, 0)
            here = pl.ds(p * B, B)
            slip = remote(SL.at[t, q, here], SL.at[t, q, here], lsend.at[p, t], lrecv.at[p, t], (g, j, 1 - q))
            slip.start()
            slips.append(slip)

        def depth_terms(half, p, add):
            acc = None
            for hl in range(HC):
                tw = WF[2 * g + q, half * HC + hl]
                cells = SL[t, half, p * B : (p + 1) * B, hl * A : (hl + 1) * A]
                terms = [tw[k : k + 1] * cells for k in range(2 * R)]
                acc = terms if acc is None else [x + y for x, y in zip(acc, terms)]
            for k in range(2 * R):
                r, c = k // 2, k % 2
                at = (slice(r * B, (r + 1) * B), slice((2 * p + c) * A, (2 * p + c + 1) * A))
                US[at] = US[at] + acc[k] if add else acc[k]

        for p in range(2):
            depth_terms(q, p, False)
        for p in range(2):
            here = pl.ds(p * B, B)
            land = SL.at[t, 1 - q, here]
            pltpu.make_async_copy(land, land, lrecv.at[p, t]).wait()
            depth_terms(1 - q, p, True)
        SF[t] = table_left(TF, US[...], ((1,), (1,)))
        spot = pl.ds((jz * ZY + jxy) * 4, 4)
        block_here = pl.ds(j * 4, 4)
        arrived = frecv.at[jz, t]

        def send_slip(peer):
            remote(SF.at[t, pl.ds(peer * 4, 4)], RF.at[t, spot], fsend.at[t], arrived, (g, peer, q)).start()

        each_peer(send_slip)
        pltpu.make_async_copy(SF.at[t, block_here], RF.at[t, spot], arrived).start()

        recv_halo(up, down, right, t, HS, DS, s_rows, d_cols)
        sent_halo(up, down, right, left)
        NS[0] = TR[...]

        def fault_chunk(i, c):
            r0 = pl.multiple_of(i * 8, 8)
            chunk = pl.ds(r0, 8)
            inner = pl.ds(r0 + 8, 8)
            n0, n1, n2, n3 = (NS[p, chunk, :] for p in range(4))
            plane_terms = [
                C1 * (n1 - n0) - C2 * n2,
                C1 * (n2 - n1) - C2 * (n3 - n0),
                C1 * (n3 - n2) + C2 * n1,
                C2 * n2 - C1 * n3,
            ]
            for p in range(1):
                tall = SP[p, pl.ds(r0, 24), :]
                wide = DP[p, chunk, :]
                dn1, dn2, up1 = (roll(tall, s, 0)[8:16] for s in (1, 2, -1))
                total = plane_terms[p] + (C1 * (tall[8:16] - dn1) - C2 * (up1 - dn2))
                dn1, dn2, up1 = (roll(wide, s, 1)[:, LW : LW + CW] for s in (1, 2, -1))
                total = total + (C1 * (wide[:, LW : LW + CW] - dn1) - C2 * (up1 - dn2))
                VP[p, inner, cols_in] = VP[p, inner, cols_in] + buoy[p, chunk, :] * total
            return c

        lax.fori_loop(0, RW // 8, fault_chunk, 0)

        @pl.when(t < NSTEP - 1)
        def _():
            v_copies(t + 1)[4].start()

        def velocity_chunk(i, c):
            r0 = pl.multiple_of(i * 8, 8)
            chunk = pl.ds(r0, 8)
            inner = pl.ds(r0 + 8, 8)
            n0, n1, n2, n3 = (NS[p, chunk, :] for p in range(4))
            plane_terms = [
                C1 * (n1 - n0) - C2 * n2,
                C1 * (n2 - n1) - C2 * (n3 - n0),
                C1 * (n3 - n2) + C2 * n1,
                C2 * n2 - C1 * n3,
            ]
            for p in range(1, 4):
                tall = SP[p, pl.ds(r0, 24), :]
                wide = DP[p, chunk, :]
                dn1, dn2, up1 = (roll(tall, s, 0)[8:16] for s in (1, 2, -1))
                total = plane_terms[p] + (C1 * (tall[8:16] - dn1) - C2 * (up1 - dn2))
                dn1, dn2, up1 = (roll(wide, s, 1)[:, LW : LW + CW] for s in (1, 2, -1))
                total = total + (C1 * (wide[:, LW : LW + CW] - dn1) - C2 * (up1 - dn2))
                VP[p, inner, cols_in] = VP[p, inner, cols_in] + buoy[p, chunk, :] * total
            return c

        lax.fori_loop(0, RW // 8, velocity_chunk, 0)

        @pl.when(t < NSTEP - 1)
        def _():
            pack_rows(0, VP, cols_in)
            start_halo(*v_copies(t + 1)[:4])

        @pl.when(t == NSTEP - 1)
        def _():
            for copy in out_copies()[2:]:
                copy.start()

        for p in range(2):
            parts[p].wait_send()
            slips[p].wait_send()
        count = 4 * ZY
        xs, spots = [], []
        for k in range(0, LX, 2):
            pair = []
            for n in (k, k + 1):
                layer = layer_of(n)
                spot = pl.ds(pl.multiple_of(layer * count, count), count)
                pltpu.make_async_copy(RF.at[t, spot], RF.at[t, spot], frecv.at[layer, t]).wait()
                pair.append(RF[t, spot, :])
                spots.append(spot)
            xs.append(jnp.concatenate(pair, axis=0).T)
        tab = [jnp.concatenate([TV[n, spot, :] for spot in spots], axis=0) for n in range(2)]
        x = table_right(jnp.concatenate(xs, axis=1), tab, ((1,), (0,)))
        xr, xi = x[:, :A], x[:, A:]
        tall = jnp.concatenate([xr * TW[0] + xi * TW[1], xi * TW[0] - xr * TW[1]], axis=0)
        fresh = table_left(L3, tall, ((1,), (0,)))
        FR[t] = fresh
        pltpu.make_async_copy(FR.at[t], out_s.at[t], outsem.at[5 + t]).start()

        @pl.when(t < NSTEP - 1)
        def _():
            for d in range(NSTEP - 1):
                ACC[t + 1 + d] = ACC[t + 1 + d] + WD[d] * fresh
            strike_inverse(t + 1)

        return carry

    lax.fori_loop(0, NSTEP, step_body, 0)

    for copy in out_copies():
        copy.wait()
    for t in range(NSTEP):
        pltpu.make_async_copy(FR.at[t], out_s.at[t], outsem.at[5 + t]).wait()
        left = RI.at[t, pl.ds(0, (2 * nx - 1) * 4)]
        pltpu.make_async_copy(left, left, isend.at[t]).wait()
        left = RF.at[t, pl.ds(0, (nx - 1) * 4)]
        pltpu.make_async_copy(left, left, fsend.at[t]).wait()


def hand_over(f_in, l_in, s_in, f_out, l_out, s_out, f, l, s, sem):
    pieces = [(f_in.at[n], f.at[n], f_out.at[n]) for n in range(f.shape[0])]
    pieces += [(s_in, s, s_out), (l_in, l, l_out)]
    for n, (src, mid, _) in enumerate(pieces):
        pltpu.make_async_copy(src, mid, sem.at[0, n]).start()
    for n, (src, mid, dst) in enumerate(pieces):
        pltpu.make_async_copy(src, mid, sem.at[0, n]).wait()
        pltpu.make_async_copy(mid, dst, sem.at[1, n]).start()
    for n, (_, mid, dst) in enumerate(pieces):
        pltpu.make_async_copy(mid, dst, sem.at[1, n]).wait()


def per_device(nx, fields, buoyancy, stiffness, stress_zero, direct_effect, log_state, kernel, history, truncation):
    planes, rows, cols = fields.shape[2:]
    hist, modes, _, strike = history.shape
    A = 2 * nx
    B = rows // 2
    RB = modes * B
    depth = 2 * cols
    scale = 1.0 / math.sqrt(strike * depth)
    mats, vecs = make_tables(nx, rows, modes, scale)
    kernel = kernel.reshape(hist, modes, B, A).transpose(0, 2, 1, 3).reshape(hist, RB, A)
    history = history.reshape(hist, modes, 2, B, A).transpose(0, 1, 3, 2, 4).reshape(hist, 2 * RB, A)
    truncation = truncation.reshape(modes, B, A).transpose(1, 0, 2).reshape(RB, A)
    LW = min(128, cols)
    vm = pltpu.VMEM
    dma = pltpu.SemaphoreType.DMA
    args = [
        fields.reshape(4, planes, rows, cols), buoyancy[0], stiffness[0], stress_zero, direct_effect, log_state,
        kernel, history, truncation, *[jnp.asarray(x) for x in mats], *[jnp.asarray(x) for x in vecs],
    ]
    scratch = [vm(x.shape, x.dtype) for x in args[1:]] + [
        vm((hist, 2 * RB, A), F32),
        vm((planes, rows, cols), F32),
        vm((NSTEP, 2 * RB, A), F32),
        vm((planes, rows + 16, cols + 2 * LW), F32),
        vm((planes, rows + 16, cols), F32),
        vm((planes, rows, cols + 2 * LW), F32),
        vm((2 * NSTEP - 1, 2 * RB, A), F32),
        vm((NSTEP, 4 * nx, RB), F32),
        vm((NSTEP, 8 * nx, RB), F32),
        vm((RB, 4 * A), F32),
        vm((NSTEP, rows, cols), F32),
        vm((rows, cols), F32),
        vm((NSTEP, rows, cols), F32),
        vm((NSTEP, 2, rows, cols), F32),
        vm((RB, 4 * A), F32),
        vm((NSTEP, 4 * nx, RB), F32),
        vm((NSTEP, 4 * nx, RB), F32),
        vm((rows, cols), F32),
        vm((rows, cols), F32),
        vm((NSTEP, 2, 8, cols), F32),
        vm((NSTEP, planes, rows, LW), F32),
        vm((NSTEP, rows, cols), F32),
        vm((NSTEP, 2, 8, cols), F32),
        vm((NSTEP, planes, rows, LW), F32),
        vm((2, 2, 8, cols), F32),
        dma((21,)), dma((5 + NSTEP,)),
        dma((NSTEP,)), dma((x_layers(nx), NSTEP)), dma((NSTEP,)), dma((x_layers(nx), NSTEP)),
        dma((2, NSTEP)), dma((2, NSTEP)), dma((2, NSTEP)), dma((2, NSTEP)),
        dma((3,)), dma((3, NSTEP)), dma((3,)), dma((3, NSTEP)), dma, dma((NSTEP,)),
    ]
    hbm = pl.BlockSpec(memory_space=pl.ANY)
    out_shape = (
        jax.ShapeDtypeStruct((4, planes, rows, cols), F32),
        jax.ShapeDtypeStruct((rows, cols), F32),
        jax.ShapeDtypeStruct((NSTEP, 2 * RB, A), F32),
    )
    results = pl.pallas_call(
        functools.partial(kernel_body, nx),
        out_shape=out_shape,
        in_specs=[hbm] * len(args),
        out_specs=(hbm, hbm, hbm),
        scratch_shapes=scratch,
        compiler_params=pltpu.CompilerParams(
            collective_id=0, has_side_effects=True, vmem_limit_bytes=60 * 1024 * 1024
        ),
    )(*args)
    out_f, out_l, out_s = pl.pallas_call(
        hand_over,
        out_shape=out_shape,
        in_specs=[hbm] * 3,
        out_specs=(hbm, hbm, hbm),
        scratch_shapes=[vm(x.shape, F32) for x in out_shape] + [dma((2, 6))],
        compiler_params=pltpu.CompilerParams(vmem_limit_bytes=60 * 1024 * 1024),
    )(*results)
    spectra = out_s.reshape(NSTEP, modes, B, 2, A).transpose(0, 1, 3, 2, 4).reshape(NSTEP, modes, 2, strike)
    return out_f.reshape(4, 1, planes, rows, cols), out_l, spectra


def solution(mesh):
    return jax.shard_map(
        functools.partial(per_device, mesh.shape["gx"]),
        mesh=mesh,
        in_specs=(
            P(None, "grp", None, "gx", "gz"),
            P("grp", None, "gx", "gz"),
            P("grp", None, "gx", "gz"),
            P("gx", "gz"),
            P("gx", "gz"),
            P("gx", "gz"),
            P(None, ("grp", "gx", "gz"), None),
            P(None, ("grp", "gx", "gz"), None, None),
            P(("grp", "gx", "gz"), None),
        ),
        out_specs=(
            P(None, "grp", None, "gx", "gz"),
            P("gx", "gz"),
            P(None, ("grp", "gx", "gz"), None, None),
        ),
        check_vma=False,
    )
```
